256 devices in a mesh: subcube: 2 (over y_hi), row: 8 (over z), col: 16 (over x, y_lo, core).
Axes of the slice: x: 4, y: 4 (y_hi: 2, y_lo: 2; y = y_hi * 2 + y_lo), z: 8, core: 2. Of those that a mesh axis runs over, the one named last changes fastest.
Arguments:
- front_entries: float32 [16, 8, 64, 24576], P('col', 'row', None, 'subcube'), may hold values from -6 to 6
- child_blocks: float32 [2, 16, 8, 64, 12288], P('subcube', 'col', 'row'), may hold values from -6 to 6
- row_maps: int32 [2, 12288], replicated, may hold values from 0 to 24575, as said below
- pivot_inverses: float32 [2, 512, 512], P(None, 'row')
- tile_mask: int32 [48, 16], P(('subcube', 'row'), 'col'), may hold values 0 or 1
Outputs:
- factored: float32 [24576, 8192], P(('subcube', 'row'), 'col')
The draws below stay inside these ranges and needn't reach their ends.
Inputs may be any that keep to these rules, and one draw needn't show every extreme that they name: Each row of row_maps lists 12288 distinct front rows in increasing order; its first is 0 and its last 24575.
All inputs are finite; a program needn't handle non-finite values. No bound on the sum of `tile_mask` on one device may be relied on, other than what follows from the above.
Results may differ from the reference program's by a relative error of at most 0.0001.
Values sent between devices are 32-bit elements; how exact they have to be, the bound alone decides.
No kernel may reach another device: no remote copies, remote signals or barrier semaphores. Data moves between devices by JAX's collectives and lax.ppermute only.
A program may use at most 128 MiB of HBM per device.

```python
import math
import jax
import jax.numpy as jnp
from jax import lax

FRONT = 24576
CHILD = 12288
PANEL = 512
PANELS = 2
COLS = 8192
COL_THIN = 64
N_ROW = 8
N_COL = 16


def draw_row_maps(key, part):
    listed = []
    for child_index in range(2):
        child_key = jax.random.fold_in(key, 11 + child_index)
        shuffled = jax.random.permutation(child_key, FRONT - 2) + 1
        chosen_rows = jnp.concatenate([jnp.zeros((1,), jnp.int32), shuffled[:CHILD - 2].astype(jnp.int32), jnp.full((1,), FRONT - 1, jnp.int32)])
        listed.append(jnp.sort(chosen_rows))
    return jnp.stack(listed).astype(jnp.int32)


def draw_pivot_inverses(key, part):
    first_key, second_key = jax.random.split(jax.random.fold_in(key, 29))
    diagonal_part = jax.random.uniform(first_key, (PANELS, PANEL), jnp.float32, 0.1, 0.3) / math.sqrt(PANEL)
    off_diagonal = jax.random.normal(second_key, (PANELS, PANEL, PANEL), jnp.float32) * (0.1 / PANEL)
    return (off_diagonal + diagonal_part[:, :, None] * jnp.eye(PANEL, dtype=jnp.float32)[None]).astype(jnp.float32)


def place_ends(array, key, smallest, largest):
    index_at = [jax.random.randint(jax.random.fold_in(key, axis), (), 0, length) for axis, length in enumerate(array.shape)]
    main_axis = array.shape.index(max(array.shape))
    neighbour = index_at[:main_axis] + [(index_at[main_axis] + 1) % array.shape[main_axis]] + index_at[main_axis + 1:]
    return array.at[tuple(index_at)].set(smallest).at[tuple(neighbour)].set(largest)


def block_scale(rng, dims, pieces, least, top_value):
    level, own = 1.0, jax.random.fold_in(rng, 6)
    for axis_at, blocks in pieces:
        steps = jnp.exp(jax.random.uniform(jax.random.fold_in(own, axis_at), (blocks,), jnp.float32, least / len(pieces), top_value / len(pieces)))
        level = level * jnp.repeat(steps, dims[axis_at] // blocks).reshape([-1 if axis == axis_at else 1 for axis in range(len(dims))])
    return level


def gaussian(own_key, shape, width, reach, cuts=(), kind=jnp.bfloat16):
    values = jax.random.normal(own_key, shape, jnp.float32) * width
    if len(cuts) > 0:
        values = block_scale(own_key, shape, cuts, -0.22, 0.18) * values
    return jnp.clip(values, min=-reach, max=reach).astype(kind)


def setup_inputs(seed: int = 0) -> dict:
    key_list = jax.random.split(jax.random.key(seed), 6)
    front_entries = gaussian(key_list[0], (N_COL, N_ROW, COL_THIN, FRONT), 1.0, 6.0, ((0, 16), (1, 8), (3, 2)), jnp.float32)
    child_blocks = gaussian(key_list[1], (2, N_COL, N_ROW, COL_THIN, CHILD), 1.0, 6.0, ((0, 2), (1, 16), (2, 8)), jnp.float32)
    row_maps = draw_row_maps(jax.random.fold_in(key_list[5], 71), 0)
    pivot_inverses = draw_pivot_inverses(jax.random.fold_in(key_list[5], 71), 0)
    tile_mask = place_ends((jax.random.randint(key_list[4], (FRONT // PANEL, COLS // PANEL), 0, 4) < 3).astype(jnp.int32), jax.random.fold_in(key_list[4], 1), 0, 1)
    return dict(front_entries=front_entries, child_blocks=child_blocks, row_maps=row_maps, pivot_inverses=pivot_inverses, tile_mask=tile_mask)


def reference(front_entries, child_blocks, row_maps, pivot_inverses, tile_mask):
    front_matrix = front_entries.reshape(COLS, FRONT).T
    child_matrix = jnp.transpose(child_blocks.reshape(2, COLS, CHILD), (0, 2, 1))
    for child_index in range(2):
        front_matrix = front_matrix.at[row_maps[child_index]].add(child_matrix[child_index])
    kept_tiles = jnp.repeat(jnp.repeat(tile_mask.astype(jnp.float32), PANEL, axis=0), PANEL, axis=1)
    row_ids = jnp.arange(FRONT, dtype=jnp.int32)
    for panel_index in range(PANELS):
        first_col = panel_index * PANEL
        after_col = first_col + PANEL
        current = front_matrix[:, first_col:after_col]
        scaled = jnp.dot(current, pivot_inverses[panel_index],
                         precision=lax.Precision.HIGHEST, preferred_element_type=jnp.float32)
        update = jnp.dot(scaled, front_matrix[first_col:after_col, after_col:],
                         precision=lax.Precision.HIGHEST, preferred_element_type=jnp.float32)
        below = (row_ids >= after_col).astype(jnp.float32)[:, None]
        front_matrix = front_matrix.at[:, after_col:].add(-update * kept_tiles[:, after_col:] * below)
        front_matrix = front_matrix.at[:, first_col:after_col].set(
            jnp.where((row_ids >= first_col)[:, None], scaled, current))
    return front_matrix
```

```python
import functools

import jax
import jax.numpy as jnp
from jax import lax
from jax.experimental import pallas as pl
from jax.experimental.pallas import tpu as pltpu
from jax.sharding import PartitionSpec as P

PANEL = 512
PANELS = 2
LANES = 128
BIG = 2**30
VMEM_BYTES = 56 * 2**20


def extend_kernel(bases, scalars, maps_ref, front_ref, *refs):
    sources, out_ref = refs[: len(bases)], refs[len(bases)]
    low_ref, high_ref, place_ref = refs[len(bases) + 1 :]
    step = pl.program_id(0)
    steps = pl.num_programs(0)
    per_step = front_ref.shape[1] // LANES
    map_blocks = maps_ref.shape[1]
    blocks = steps * per_step
    first_row = scalars[len(bases) * (blocks + 1)]
    lane = lax.broadcasted_iota(jnp.int32, low_ref.shape, 1)
    row = lax.broadcasted_iota(jnp.int32, low_ref.shape, 0)
    wanted = first_row + (step * per_step + row) * LANES + lane
    for j in range(per_step):
        out_ref[0, :, j * LANES : (j + 1) * LANES] = front_ref[:, j * LANES : (j + 1) * LANES]
    for index, source in enumerate(sources):
        map_index = bases[index]
        source_blocks = source.shape[1] // LANES
        offset = scalars[len(bases) * blocks + index]
        blocks_at = []
        for j in range(per_step):
            start = scalars[index * blocks + step * per_step + j]
            at = jnp.minimum(start // LANES, map_blocks - 1)
            after = jnp.minimum(at + 1, map_blocks - 1)
            low_ref[j : j + 1, :] = maps_ref[map_index, pl.ds(at, 1), :]
            high_ref[j : j + 1, :] = jnp.where(at + 1 < map_blocks, maps_ref[map_index, pl.ds(after, 1), :], BIG)
            blocks_at.append(at)
        low, high = low_ref[...], high_ref[...]

        def pick(at):
            inner = at & (LANES - 1)
            return jnp.where(
                at < LANES, jnp.take_along_axis(low, inner, axis=1), jnp.take_along_axis(high, inner, axis=1)
            )

        place = jnp.zeros(low_ref.shape, jnp.int32)
        width = LANES
        while width >= 1:
            place = jnp.where(pick(place + (width - 1)) < wanted, place + width, place)
            width //= 2
        place_ref[...] = jnp.where(pick(place) == wanted, place, -1)
        for j in range(per_step):
            at = blocks_at[j] - offset
            inside_low = (at >= 0) & (at < source_blocks)
            inside_high = (at + 1 >= 0) & (at + 1 < source_blocks)
            low_at = pl.multiple_of(jnp.clip(at, 0, source_blocks - 1) * LANES, LANES)
            high_at = pl.multiple_of(jnp.clip(at + 1, 0, source_blocks - 1) * LANES, LANES)
            places = jnp.broadcast_to(place_ref[j : j + 1, :], (source.shape[0], LANES))
            inner = places & (LANES - 1)
            in_low = (places >= 0) & (places < LANES) & inside_low
            in_high = (places >= LANES) & inside_high
            gained = jnp.where(in_low, jnp.take_along_axis(source[:, pl.ds(low_at, LANES)], inner, axis=1), 0.0)
            gained = jnp.where(
                in_high, jnp.take_along_axis(source[:, pl.ds(high_at, LANES)], inner, axis=1), gained
            )
            out_ref[0, :, j * LANES : (j + 1) * LANES] += gained


def extend_add(front, sources, bases, offsets, maps, starts, first_row, steps):
    columns, rows = front.shape
    width = rows // steps
    per_step = width // LANES
    padded = -(-per_step // 8) * 8
    scalars = jnp.concatenate(
        [starts[base] for base in bases] + [jnp.stack(offsets), first_row.reshape(1)]
    ).astype(jnp.int32)
    whole = lambda shape: pl.BlockSpec(shape, lambda i, _: (0,) * len(shape), pipeline_mode=pl.Buffered(1))
    return pl.pallas_call(
        functools.partial(extend_kernel, tuple(bases)),
        out_shape=jax.ShapeDtypeStruct((steps, columns, width), jnp.float32),
        grid_spec=pltpu.PrefetchScalarGridSpec(
            num_scalar_prefetch=1,
            grid=(steps,),
            in_specs=[whole(maps.shape), pl.BlockSpec((columns, width), lambda i, _: (0, i))]
            + [whole(source.shape) for source in sources],
            out_specs=pl.BlockSpec((1, columns, width), lambda i, _: (i, 0, 0)),
            scratch_shapes=[pltpu.VMEM((padded, LANES), jnp.int32)] * 3,
        ),
        compiler_params=pltpu.CompilerParams(vmem_limit_bytes=VMEM_BYTES),
    )(scalars, maps, front, *sources)


def halves(x):
    high = x.astype(jnp.bfloat16)
    return high, (x - high.astype(jnp.float32)).astype(jnp.bfloat16)


def product(left, right, dims):
    left_high, left_low = left
    right_high, right_low = right
    dot = lambda a, b: lax.dot_general(a, b, (dims, ((), ())), preferred_element_type=jnp.float32)
    return dot(left_high, right_high) + (dot(left_high, right_low) + dot(left_low, right_high))


PLAIN = ((1,), (0,))
CROSS = ((1,), (1,))


def factor_kernel(flags, strip_ref, corner_ref, inverse_ref, first_ref, second_ref, fixed_ref):
    place, kept = flags[0], flags[1]
    inverse0 = halves(inverse_ref[0])
    inverse1 = halves(inverse_ref[1])
    pivot0 = halves(strip_ref[:, :PANEL])
    corner = corner_ref[...]
    corner10 = halves(corner[:, 0].reshape(PANEL, PANEL))
    corner01 = halves(corner[:, 1].reshape(PANEL, PANEL))
    first = product(pivot0, inverse0, CROSS)
    lowered = product(halves(first), corner10, PLAIN)
    pivot1 = strip_ref[:, PANEL : 2 * PANEL] - jnp.where(kept == 1, lowered, 0.0)
    second = product(halves(pivot1), inverse1, CROSS)
    second = jnp.where(place == 1, -inverse_ref[1].T, second)
    crossed = product(halves(second), corner01, PLAIN)
    fixed = product(halves(crossed), inverse0, CROSS)
    first = jnp.where(place == 0, -inverse_ref[0].T, jnp.where(place == 1, 0.0, first))
    first_ref[...] = first
    second_ref[...] = second
    fixed_ref[...] = fixed


def factor(flags, strip, corner, inverse):
    square = jax.ShapeDtypeStruct((PANEL, PANEL), jnp.float32)
    return pl.pallas_call(
        factor_kernel,
        out_shape=(square, square, square),
        grid_spec=pltpu.PrefetchScalarGridSpec(
            num_scalar_prefetch=1,
            grid=(1,),
            in_specs=[
                pl.BlockSpec(strip.shape, lambda i, _: (0, 0)),
                pl.BlockSpec(corner.shape[:3] + (PANEL,), lambda i, _: (0, 0, 0, corner.shape[3] // PANEL - 1)),
                pl.BlockSpec(inverse.shape, lambda i, _: (0, 0, 0)),
            ],
            out_specs=[pl.BlockSpec((PANEL, PANEL), lambda i, _: (0, 0))] * 3,
        ),
        compiler_params=pltpu.CompilerParams(vmem_limit_bytes=VMEM_BYTES),
    )(flags, strip, corner, inverse)


def update_kernel(flags, block_ref, panels_ref, first_ref, second_ref, fixed_ref, out_ref):
    tile = pl.program_id(0)
    keep, use_first, use_fixed, use_second = (flags[4 * tile + i] == 1 for i in range(4))
    left0 = first_ref[...] - jnp.where(use_fixed, fixed_ref[...], 0.0)
    left0 = halves(jnp.where(use_first, left0, 0.0))
    left1 = halves(jnp.where(use_second, second_ref[...], 0.0))
    panel = panels_ref[...]
    right0 = halves(panel[:, 0].reshape(PANEL, PANEL))
    right1 = halves(panel[:, 1].reshape(PANEL, PANEL))
    update = product(left0, right0, PLAIN) + product(left1, right1, PLAIN)
    out_ref[...] = (jnp.where(keep, block_ref[...], 0.0) - update).T


def update(flags, block, panels, first, second, fixed):
    tiles = block.shape[1] // PANEL
    square = pl.BlockSpec((PANEL, PANEL), lambda i, _: (0, 0))
    return pl.pallas_call(
        update_kernel,
        out_shape=jax.ShapeDtypeStruct(block.shape[::-1], jnp.float32),
        grid_spec=pltpu.PrefetchScalarGridSpec(
            num_scalar_prefetch=1,
            grid=(tiles,),
            in_specs=[
                pl.BlockSpec((PANEL, PANEL), lambda i, _: (0, i)),
                pl.BlockSpec(panels.shape[:3] + (PANEL,), lambda i, _: (0, 0, 0, i)),
                square,
                square,
                square,
            ],
            out_specs=pl.BlockSpec((PANEL, PANEL), lambda i, _: (i, 0)),
        ),
        compiler_params=pltpu.CompilerParams(vmem_limit_bytes=VMEM_BYTES),
    )(flags, block, panels, first, second, fixed)


def local(front_entries, child_blocks, row_maps, pivot_inverses, tile_mask):
    thin, half_rows = front_entries.shape[2:]
    child_rows = child_blocks.shape[4]
    grid_rows = lax.axis_size("row")
    grid_cols = lax.axis_size("col")
    side = lax.axis_index("subcube")
    row_place = lax.axis_index("row")
    place = lax.axis_index("col")
    row_count = half_rows // grid_rows
    own = child_blocks[0, 0, 0]

    mask_here = jnp.pad(tile_mask.astype(jnp.float32).reshape(1, -1), ((0, 0), (0, LANES - tile_mask.shape[0])))
    masks = lax.all_gather(mask_here, ("subcube", "row", "col"), axis=0, tiled=True)
    masks = (masks.reshape(2, grid_rows, grid_cols, LANES)[..., : tile_mask.shape[0]] > 0.5).astype(jnp.int32)
    inverse = lax.all_gather(pivot_inverses, "row", axis=0)
    chunks = thin // 8
    inverse = inverse.reshape(grid_rows, PANELS, chunks, 8, PANEL).transpose(1, 2, 0, 3, 4).reshape(PANELS, PANEL, PANEL)

    window = -(-(child_rows * 13 // 24) // LANES) * LANES
    rest = child_rows - window
    swap = [(0, 1), (1, 0)]
    to_send = jnp.where(side == 0, own[:, rest:], own[:, :window])
    received = lax.ppermute(to_send, "subcube", swap)

    first_row = (side * half_rows).astype(jnp.int32)
    own_map = lax.dynamic_index_in_dim(row_maps, side, 0, keepdims=False)
    other_map = lax.dynamic_index_in_dim(row_maps, 1 - side, 0, keepdims=False)
    maps = jnp.stack([own_map, other_map])
    edges = first_row + LANES * jnp.arange(half_rows // LANES, dtype=jnp.int32)
    starts = jnp.sum((maps[:, None, :] < edges[None, :, None]).astype(jnp.int32), axis=2)
    maps = maps.reshape(2, child_rows // LANES, LANES)
    lower = jnp.sum((row_maps < half_rows).astype(jnp.int32), axis=1)
    spill = (child_rows - lower[0] > window) | (lower[1] > window)
    zero = jnp.zeros((), jnp.int32)
    window_at = jnp.where(side == 0, 0, rest // LANES).astype(jnp.int32)
    rest_at = jnp.where(side == 0, window // LANES, 0).astype(jnp.int32)
    front = front_entries[0, 0]
    assembled = extend_add(front, [own, received], [0, 1], [zero, window_at], maps, starts, first_row, grid_rows)

    def add_rest(blocks):
        more = lax.ppermute(jnp.where(side == 0, own[:, :rest], own[:, window:]), "subcube", swap)
        flat = blocks.transpose(1, 0, 2).reshape(thin, half_rows)
        return extend_add(flat, [more], [1], [rest_at], maps, starts, first_row, grid_rows)

    assembled = lax.cond(spill, add_rest, lambda blocks: blocks, assembled)

    strip_here = assembled[0, :, : PANELS * PANEL]
    strip_there = lax.ppermute(strip_here, "subcube", [(0, 1)])
    strip_here = jnp.where(side == 0, strip_here, strip_there)
    strip = lax.all_gather(strip_here, "row", axis=0, tiled=True)

    flat = assembled.reshape(grid_rows, chunks, 8, row_count)
    mine = jnp.where(place // 2 == 0, flat[:, 0], 0.0)
    for chunk in range(1, chunks):
        sent = lax.ppermute(flat[:, chunk], "col", [(k, 2 * chunk + k) for k in range(PANELS)])
        mine = mine + sent
    corner_here = jnp.where(place % 2 == 0, mine[0, :, PANEL : 2 * PANEL], mine[0, :, :PANEL])
    corner_there = lax.ppermute(corner_here, "subcube", [(0, 1)])
    corner_here = jnp.where(side == 0, corner_here, corner_there)
    mine = jnp.concatenate([mine, jnp.broadcast_to(corner_here[None], (grid_rows,) + corner_here.shape)], axis=2)
    mine = lax.all_to_all(mine, "row", split_axis=0, concat_axis=0, tiled=True)
    assembled, mine = lax.optimization_barrier((assembled, mine))
    panels = lax.all_gather(mine.reshape(thin, -1), "col", axis=0, tiled=True)
    panels = panels.reshape(chunks, PANELS, thin, -1)

    block = lax.all_to_all(assembled, "row", split_axis=0, concat_axis=0, tiled=True)
    block = block.reshape(PANEL, row_count)

    kept = lax.dynamic_index_in_dim(masks[0, 0, :, 1], place, 0, keepdims=False)
    first, second, fixed = factor(jnp.stack([place, kept]).astype(jnp.int32), strip, panels, inverse)

    tiles = row_count // PANEL
    tile_ids = (side * grid_rows + row_place) * tiles + jnp.arange(tiles, dtype=jnp.int32)
    own_mask = tile_mask[:, 0] == 1
    side_masks = lax.dynamic_index_in_dim(masks[:, :, 1], side, 0, keepdims=False)
    cross_mask = lax.dynamic_index_in_dim(side_masks, row_place, 0, keepdims=False) == 1
    is0, is1 = place == 0, place == 1
    keep = jnp.where(is0, False, jnp.where(is1, tile_ids == 0, True))
    use_first = jnp.where(is0, True, jnp.where(is1, tile_ids >= 1, own_mask & (tile_ids >= 1)))
    use_fixed = jnp.where(is0, False, cross_mask & (tile_ids >= jnp.where(is1, 1, 2)))
    use_second = jnp.where(is0, False, jnp.where(is1, tile_ids >= 1, own_mask & (tile_ids >= 2)))
    flags = jnp.stack([keep, use_first, use_fixed, use_second], axis=1).astype(jnp.int32).reshape(-1)
    return update(flags, block, panels, first, second, fixed)


def solution(mesh):
    return jax.shard_map(
        local,
        mesh=mesh,
        in_specs=(
            P("col", "row", None, "subcube"),
            P("subcube", "col", "row", None, None),
            P(),
            P(None, "row", None),
            P(("subcube", "row"), "col"),
        ),
        out_specs=P(("subcube", "row"), "col"),
        check_vma=False,
    )
```

```python
import functools

import jax
import jax.numpy as jnp
from jax import lax
from jax.experimental import pallas as pl
from jax.experimental.pallas import tpu as pltpu
from jax.sharding import PartitionSpec as P

PANEL = 512
PANELS = 2
LANES = 128
BIG = 2**30
VMEM_BYTES = 56 * 2**20


def search_kernel(sections, scalars, maps_ref, places_ref, low_ref, high_ref):
    map_blocks = maps_ref.shape[1]
    at_row = 0
    for section, count in enumerate(sections):
        child = scalars[section]
        first = scalars[len(sections) + section]
        for block in range(count):
            at = jnp.minimum(scalars[2 * len(sections) + at_row + block] // LANES, map_blocks - 1)
            after = jnp.minimum(at + 1, map_blocks - 1)
            row = at_row + block
            low_ref[row : row + 1, :] = maps_ref[child, pl.ds(at, 1), :]
            high_ref[row : row + 1, :] = jnp.where(at + 1 < map_blocks, maps_ref[child, pl.ds(after, 1), :], BIG)
        low, high = low_ref[at_row : at_row + count, :], high_ref[at_row : at_row + count, :]
        lane = lax.broadcasted_iota(jnp.int32, low.shape, 1)
        block_id = lax.broadcasted_iota(jnp.int32, low.shape, 0)
        wanted = first + block_id * LANES + lane

        def pick(at):
            inner = at & (LANES - 1)
            return jnp.where(
                at < LANES, jnp.take_along_axis(low, inner, axis=1), jnp.take_along_axis(high, inner, axis=1)
            )

        place = jnp.zeros(low.shape, jnp.int32)
        width = LANES
        while width >= 1:
            place = jnp.where(pick(place + (width - 1)) < wanted, place + width, place)
            width //= 2
        places_ref[at_row : at_row + count, :] = jnp.where(pick(place) == wanted, place, -1)
        at_row += count


def search(maps, children, firsts, starts):
    sections = tuple(start.shape[0] for start in starts)
    total = sum(sections)
    scalars = jnp.concatenate([jnp.stack(children), jnp.stack(firsts)] + list(starts)).astype(jnp.int32)
    return pl.pallas_call(
        functools.partial(search_kernel, sections),
        out_shape=jax.ShapeDtypeStruct((total, LANES), jnp.int32),
        grid_spec=pltpu.PrefetchScalarGridSpec(
            num_scalar_prefetch=1,
            grid=(1,),
            in_specs=[pl.BlockSpec(maps.shape, lambda i, _: (0, 0, 0))],
            out_specs=pl.BlockSpec((total, LANES), lambda i, _: (0, 0)),
            scratch_shapes=[pltpu.VMEM((total, LANES), jnp.int32)] * 2,
        ),
        compiler_params=pltpu.CompilerParams(vmem_limit_bytes=VMEM_BYTES),
    )(scalars, maps)


def extend_kernel(first_place, map_blocks, scalars, places_ref, front_ref, source_ref, out_ref):
    step = pl.program_id(0)
    columns, width = out_ref.shape[1:]
    per_step = width // LANES
    source_blocks = source_ref.shape[1] // LANES
    offset = scalars[scalars.shape[0] - 1]
    for j in range(per_step):
        block = step * per_step + j
        at = jnp.minimum(scalars[block] // LANES, map_blocks - 1) - offset
        inside_low = (at >= 0) & (at < source_blocks)
        inside_high = (at + 1 >= 0) & (at + 1 < source_blocks)
        low_at = pl.multiple_of(jnp.clip(at, 0, source_blocks - 1) * LANES, LANES)
        high_at = pl.multiple_of(jnp.clip(at + 1, 0, source_blocks - 1) * LANES, LANES)
        place = jnp.broadcast_to(places_ref[pl.ds(first_place + block, 1), :], (columns, LANES))
        inner = place & (LANES - 1)
        in_low = (place >= 0) & (place < LANES) & inside_low
        in_high = (place >= LANES) & inside_high
        here = slice(j * LANES, (j + 1) * LANES)
        gained = jnp.where(in_low, jnp.take_along_axis(source_ref[:, pl.ds(low_at, LANES)], inner, axis=1), 0.0)
        gained = jnp.where(
            in_high, jnp.take_along_axis(source_ref[:, pl.ds(high_at, LANES)], inner, axis=1), gained
        )
        out_ref[0, :, here] = front_ref[..., here].reshape(columns, LANES) + gained


def extend_add(front, source, places, first_place, starts, offset, map_blocks, steps):
    if front.ndim == 2:
        columns, rows = front.shape
        width = rows // steps
        front_spec = pl.BlockSpec((columns, width), lambda i, _: (0, i))
    else:
        columns, width = front.shape[1:]
        front_spec = pl.BlockSpec((1, columns, width), lambda i, _: (i, 0, 0))
    scalars = jnp.concatenate([starts, offset.reshape(1)]).astype(jnp.int32)
    whole = lambda shape: pl.BlockSpec(shape, lambda i, _: (0,) * len(shape), pipeline_mode=pl.Buffered(1))
    return pl.pallas_call(
        functools.partial(extend_kernel, first_place, map_blocks),
        out_shape=jax.ShapeDtypeStruct((steps, columns, width), jnp.float32),
        grid_spec=pltpu.PrefetchScalarGridSpec(
            num_scalar_prefetch=1,
            grid=(steps,),
            in_specs=[whole(places.shape), front_spec, whole(source.shape)],
            out_specs=pl.BlockSpec((1, columns, width), lambda i, _: (i, 0, 0)),
        ),
        compiler_params=pltpu.CompilerParams(vmem_limit_bytes=VMEM_BYTES),
    )(scalars, places, front, source)


def halves(x):
    high = x.astype(jnp.bfloat16)
    return high, (x - high.astype(jnp.float32)).astype(jnp.bfloat16)


def product(left, right, dims):
    left_high, left_low = left
    right_high, right_low = right
    dot = lambda a, b: lax.dot_general(a, b, (dims, ((), ())), preferred_element_type=jnp.float32)
    return dot(left_high, right_high) + (dot(left_high, right_low) + dot(left_low, right_high))


PLAIN = ((1,), (0,))
CROSS = ((1,), (1,))


def factor_kernel(flags, gathered_ref, corner_ref, first_ref, second_ref, fixed_ref):
    place, kept = flags[0], flags[1]
    gathered = gathered_ref[...]
    thin = (gathered.shape[1] - 8) // 2
    strip = gathered[:, :thin].reshape(PANEL, 2 * PANEL)
    pieces = gathered[:, thin : 2 * thin]
    inverse = jnp.concatenate([pieces[:, 8 * q : 8 * q + 8].reshape(PANEL * 8 // thin, 2 * PANEL) for q in range(thin // 8)])
    inverse0, inverse1 = inverse[:, :PANEL], inverse[:, PANEL:]
    halves0, halves1 = halves(inverse0), halves(inverse1)
    corner10 = halves(corner_ref[:, 0, :, :PANEL].reshape(PANEL, PANEL))
    corner01 = halves(corner_ref[:, 1, :, :PANEL].reshape(PANEL, PANEL))
    first = product(halves(strip[:, :PANEL]), halves0, CROSS)
    lowered = product(halves(first), corner10, PLAIN)
    pivot1 = strip[:, PANEL:] - jnp.where(kept == 1, lowered, 0.0)
    second = product(halves(pivot1), halves1, CROSS)
    second = jnp.where(place == 1, -inverse1.T, second)
    crossed = product(halves(second), corner01, PLAIN)
    fixed = product(halves(crossed), halves0, CROSS)
    first_ref[...] = jnp.where(place == 0, -inverse0.T, jnp.where(place == 1, 0.0, first))
    second_ref[...] = second
    fixed_ref[...] = fixed


def factor(flags, gathered, corner):
    square = jax.ShapeDtypeStruct((PANEL, PANEL), jnp.float32)
    return pl.pallas_call(
        factor_kernel,
        out_shape=(square, square, square),
        grid_spec=pltpu.PrefetchScalarGridSpec(
            num_scalar_prefetch=1,
            grid=(1,),
            in_specs=[
                pl.BlockSpec(gathered.shape, lambda i, _: (0, 0, 0)),
                pl.BlockSpec(corner.shape, lambda i, _: (0, 0, 0, 0)),
            ],
            out_specs=[pl.BlockSpec((PANEL, PANEL), lambda i, _: (0, 0))] * 3,
        ),
        compiler_params=pltpu.CompilerParams(vmem_limit_bytes=VMEM_BYTES),
    )(flags, gathered, corner)


def update_kernel(flags, block_ref, panels_ref, first_ref, second_ref, fixed_ref, out_ref):
    tile = pl.program_id(0)
    keep, use_first, use_fixed, use_second = (flags[4 * tile + i] == 1 for i in range(4))
    left0 = first_ref[...] - jnp.where(use_fixed, fixed_ref[...], 0.0)
    left0 = halves(jnp.where(use_first, left0, 0.0))
    left1 = halves(jnp.where(use_second, second_ref[...], 0.0))
    panel = panels_ref[...]
    right0 = halves(panel[:, 0].reshape(PANEL, PANEL))
    right1 = halves(panel[:, 1].reshape(PANEL, PANEL))
    update = product(left0, right0, PLAIN) + product(left1, right1, PLAIN)
    out_ref[...] = (jnp.where(keep, block_ref[...], 0.0) - update).T


def update(flags, block, panels, first, second, fixed):
    tiles = block.shape[1] // PANEL
    square = pl.BlockSpec((PANEL, PANEL), lambda i, _: (0, 0))
    return pl.pallas_call(
        update_kernel,
        out_shape=jax.ShapeDtypeStruct(block.shape[::-1], jnp.float32),
        grid_spec=pltpu.PrefetchScalarGridSpec(
            num_scalar_prefetch=1,
            grid=(tiles,),
            in_specs=[
                pl.BlockSpec((PANEL, PANEL), lambda i, _: (0, i)),
                pl.BlockSpec(panels.shape[:3] + (PANEL,), lambda i, _: (0, 0, 0, i)),
                square,
                square,
                square,
            ],
            out_specs=pl.BlockSpec((PANEL, PANEL), lambda i, _: (i, 0)),
        ),
        compiler_params=pltpu.CompilerParams(vmem_limit_bytes=VMEM_BYTES),
    )(flags, block, panels, first, second, fixed)


def local(front_entries, child_blocks, row_maps, pivot_inverses, tile_mask):
    thin, half_rows = front_entries.shape[2:]
    child_rows = child_blocks.shape[4]
    grid_rows = lax.axis_size("row")
    grid_cols = lax.axis_size("col")
    side = lax.axis_index("subcube")
    row_place = lax.axis_index("row")
    place = lax.axis_index("col")
    row_count = half_rows // grid_rows
    chunks = thin // 8
    pivot_rows = PANELS * PANEL
    own = child_blocks[0, 0, 0]
    front = front_entries[0, 0]
    one = jnp.ones((), jnp.int32)

    window = -(-(child_rows * 13 // 24) // LANES) * LANES
    rest = child_rows - window
    to_send = jnp.where(side == 0, own[:, rest:], own[:, :window])
    swap = lambda cols: [(s * grid_cols + c, (1 - s) * grid_cols + c) for s in range(2) for c in cols]
    panel_cols, other_cols = range(PANELS), range(PANELS, grid_cols)
    exchange = lambda x, cols: lax.ppermute(x, ("subcube", "col"), swap(cols))
    received_panel = exchange(to_send, panel_cols)

    map_blocks = child_rows // LANES
    blocks = half_rows // LANES
    strip_blocks = pivot_rows // LANES
    first_row = (side * half_rows).astype(jnp.int32)
    own_map = lax.dynamic_index_in_dim(row_maps, side, 0, keepdims=False)
    other_map = lax.dynamic_index_in_dim(row_maps, 1 - side, 0, keepdims=False)
    count = lambda maps, edges: jnp.sum((maps[:, None, :] < edges[None, :, None]).astype(jnp.int32), axis=2)
    edges = LANES * jnp.arange(blocks, dtype=jnp.int32)
    starts = count(jnp.stack([own_map, other_map]), first_row + edges)
    strip_starts = count(row_maps[1:2], edges[:strip_blocks])[0]
    places = search(
        row_maps.reshape(2, map_blocks, LANES),
        [side.astype(jnp.int32), (1 - side).astype(jnp.int32), one],
        [first_row, first_row, one * 0],
        [starts[0], starts[1], strip_starts],
    )
    lower = jnp.sum((row_maps < half_rows).astype(jnp.int32), axis=1)
    spill = (child_rows - lower[0] > window) | (lower[1] > window)
    window_at = jnp.where(side == 0, 0, rest // LANES).astype(jnp.int32)
    rest_at = jnp.where(side == 0, window // LANES, 0).astype(jnp.int32)
    assembled_own = extend_add(front, own, places, 0, starts[0], one * 0, map_blocks, grid_rows)

    def add_other(base, received, cols):
        def add_rest(x):
            more = exchange(jnp.where(side == 0, own[:, :rest], own[:, window:]), cols)
            return extend_add(x, more, places, blocks, starts[1], rest_at, map_blocks, grid_rows)

        added = extend_add(base, received, places, blocks, starts[1], window_at, map_blocks, grid_rows)
        return lax.cond(spill, add_rest, lambda x: x, added)

    masks_here = tile_mask.astype(jnp.float32)[:, 0]
    mask_rows = jnp.zeros((8, pivot_rows), jnp.float32).at[0, : tile_mask.shape[0]].set(masks_here)
    prefix = own[:, :pivot_rows]
    base_here = assembled_own[0, :, :pivot_rows]
    strip_sent = jnp.concatenate([jnp.where(side == 0, base_here, prefix), mask_rows])
    strip_got = lax.ppermute(strip_sent, "subcube", [(0, 1), (1, 0)])
    strip = extend_add(
        jnp.where(side == 0, base_here, strip_got[:thin]),
        jnp.where(side == 0, strip_got[:thin], prefix),
        places, 2 * blocks, strip_starts, one * 0, map_blocks, 1,
    )[0]
    first_masks = jnp.where(side == 0, mask_rows, strip_got[thin:])

    to_chips = lambda chunk: [(k, PANELS * chunk + k) for k in range(PANELS)]

    def scatter(pieces):
        mine = jnp.where(place // PANELS == 0, pieces[0], 0.0)
        for chunk in range(1, chunks):
            mine = mine + lax.ppermute(pieces[chunk], "col", to_chips(chunk))
        return mine

    corner_source = jnp.where(place == 0, strip[:, PANEL:], strip[:, :PANEL])
    corner_here = scatter([corner_source[8 * q : 8 * q + 8] for q in range(chunks)])
    pieces = jnp.concatenate([pivot_inverses[k] for k in range(PANELS)], axis=1)
    tail = jnp.concatenate([corner_here, first_masks[:, :PANEL]], axis=1)
    gathered = lax.all_gather(jnp.concatenate([strip, pieces, tail]), "row", axis=0)
    corner = gathered[:, 2 * thin :, :PANEL].reshape(thin, PANEL)
    mask_lanes = jnp.broadcast_to(mask_rows[:1, :LANES], (thin, LANES))
    corner = lax.all_gather(jnp.concatenate([corner, mask_lanes], axis=1), "col", axis=0, tiled=True)
    corner = corner.reshape(chunks, PANELS, thin, PANEL + LANES)
    kept = gathered[0, 2 * thin, PANEL + 1] > 0.5
    cross_mask = corner[0, 1, 0, PANEL : PANEL + tile_mask.shape[0]] > 0.5

    assembled_panel = add_other(assembled_own, received_panel, panel_cols)
    to_send, received_panel = lax.optimization_barrier((to_send, received_panel))
    received_other = exchange(to_send, other_cols)
    flat = assembled_panel.reshape(grid_rows, chunks, 8, row_count)
    mine = scatter([flat[:, q] for q in range(chunks)])
    mine = lax.all_to_all(mine, "row", split_axis=0, concat_axis=0, tiled=True)
    panels = lax.all_gather(mine.reshape(thin, row_count), "col", axis=0, tiled=True)
    panels = panels.reshape(chunks, PANELS, thin, row_count)

    assembled = add_other(assembled_panel, received_other, other_cols)
    assembled, mine = lax.optimization_barrier((assembled, mine))
    block = lax.all_to_all(assembled, "row", split_axis=0, concat_axis=0, tiled=True)
    block = block.reshape(PANEL, row_count)

    first, second, fixed = factor(jnp.stack([place, kept.astype(place.dtype)]).astype(jnp.int32), gathered, corner)

    tiles = row_count // PANEL
    tile_ids = (side * grid_rows + row_place) * tiles + jnp.arange(tiles, dtype=jnp.int32)
    own_mask = tile_mask[:, 0] == 1
    is0, is1 = place == 0, place == 1
    keep = jnp.where(is0, False, jnp.where(is1, tile_ids == 0, True))
    use_first = jnp.where(is0, True, jnp.where(is1, tile_ids >= 1, own_mask & (tile_ids >= 1)))
    use_fixed = jnp.where(is0, False, cross_mask & (tile_ids >= jnp.where(is1, 1, 2)))
    use_second = jnp.where(is0, False, jnp.where(is1, tile_ids >= 1, own_mask & (tile_ids >= 2)))
    flags = jnp.stack([keep, use_first, use_fixed, use_second], axis=1).astype(jnp.int32).reshape(-1)
    return update(flags, block, panels, first, second, fixed)


def solution(mesh):
    return jax.shard_map(
        local,
        mesh=mesh,
        in_specs=(
            P("col", "row", None, "subcube"),
            P("subcube", "col", "row", None, None),
            P(),
            P(None, "row", None),
            P(("subcube", "row"), "col"),
        ),
        out_specs=P(("subcube", "row"), "col"),
        check_vma=False,
    )
```

```python
import functools

import jax
import jax.numpy as jnp
from jax import lax
from jax.experimental import pallas as pl
from jax.experimental.pallas import tpu as pltpu
from jax.sharding import PartitionSpec as P

PANEL = 512
PANELS = 2
LANES = 128
BIG = 2**30
VMEM_BYTES = 56 * 2**20


def search_kernel(sections, scalars, maps_ref, places_ref, low_ref, high_ref):
    map_blocks = maps_ref.shape[1]
    at_row = 0
    for section, count in enumerate(sections):
        child = scalars[section]
        first = scalars[len(sections) + section]
        for block in range(count):
            at = jnp.minimum(scalars[2 * len(sections) + at_row + block] // LANES, map_blocks - 1)
            after = jnp.minimum(at + 1, map_blocks - 1)
            row = at_row + block
            low_ref[row : row + 1, :] = maps_ref[child, pl.ds(at, 1), :]
            high_ref[row : row + 1, :] = jnp.where(at + 1 < map_blocks, maps_ref[child, pl.ds(after, 1), :], BIG)
        low, high = low_ref[at_row : at_row + count, :], high_ref[at_row : at_row + count, :]
        lane = lax.broadcasted_iota(jnp.int32, low.shape, 1)
        block_id = lax.broadcasted_iota(jnp.int32, low.shape, 0)
        wanted = first + block_id * LANES + lane

        def pick(at):
            inner = at & (LANES - 1)
            return jnp.where(
                at < LANES, jnp.take_along_axis(low, inner, axis=1), jnp.take_along_axis(high, inner, axis=1)
            )

        place = jnp.zeros(low.shape, jnp.int32)
        width = LANES
        while width >= 1:
            place = jnp.where(pick(place + (width - 1)) < wanted, place + width, place)
            width //= 2
        places_ref[at_row : at_row + count, :] = jnp.where(pick(place) == wanted, place, -1)
        at_row += count


def search(maps, children, firsts, starts):
    sections = tuple(start.shape[0] for start in starts)
    total = sum(sections)
    scalars = jnp.concatenate([jnp.stack(children), jnp.stack(firsts)] + list(starts)).astype(jnp.int32)
    return pl.pallas_call(
        functools.partial(search_kernel, sections),
        out_shape=jax.ShapeDtypeStruct((total, LANES), jnp.int32),
        grid_spec=pltpu.PrefetchScalarGridSpec(
            num_scalar_prefetch=1,
            grid=(1,),
            in_specs=[pl.BlockSpec(maps.shape, lambda i, _: (0, 0, 0))],
            out_specs=pl.BlockSpec((total, LANES), lambda i, _: (0, 0)),
            scratch_shapes=[pltpu.VMEM((total, LANES), jnp.int32)] * 2,
        ),
        compiler_params=pltpu.CompilerParams(vmem_limit_bytes=VMEM_BYTES),
    )(scalars, maps)


def extend_kernel(first_place, map_blocks, scalars, places_ref, front_ref, source_ref, out_ref, *piece_refs):
    step = pl.program_id(0)
    columns = out_ref.shape[1]
    per_step = out_ref.shape[2] // LANES
    source_blocks = source_ref.shape[1] // LANES
    offset = scalars[scalars.shape[0] - 1]
    lane = lax.broadcasted_iota(jnp.int32, (8, LANES), 1)
    for j in range(per_step):
        block = step * per_step + j
        start = scalars[block]
        at = jnp.minimum(start // LANES, map_blocks - 1)
        split = jnp.where(start // LANES < map_blocks, start & (LANES - 1), LANES)
        at = at - offset
        inside_low = (at >= 0) & (at < source_blocks)
        inside_high = (at + 1 >= 0) & (at + 1 < source_blocks)
        low_at = pl.multiple_of(jnp.clip(at, 0, source_blocks - 1) * LANES, LANES)
        high_at = pl.multiple_of(jnp.clip(at + 1, 0, source_blocks - 1) * LANES, LANES)
        place = jnp.broadcast_to(places_ref[pl.ds(first_place + block, 1), :], (8, LANES))
        inner = place & (LANES - 1)
        hit = ((place >= 0) & (place < LANES) & inside_low) | ((place >= LANES) & inside_high)
        from_low = lane >= split
        here = slice(j * LANES, (j + 1) * LANES)
        for row in range(0, columns, 8):
            rows = slice(row, row + 8)
            merged = jnp.where(from_low, source_ref[rows, pl.ds(low_at, LANES)], source_ref[rows, pl.ds(high_at, LANES)])
            gained = jnp.where(hit, jnp.take_along_axis(merged, inner, axis=1), 0.0)
            value = front_ref[..., rows, here].reshape(8, LANES) + gained
            out_ref[0, rows, here] = value
            if piece_refs:
                piece_refs[row // 8][0, :, here] = value


def extend_add(front, source, places, first_place, starts, offset, map_blocks, steps, part=0, pieces=0):
    columns = source.shape[0]
    if front.ndim == 2:
        width = front.shape[1] // steps
        front_spec = pl.BlockSpec((columns, width), lambda i, _: (0, i))
    else:
        width = front.shape[2]
        front_spec = pl.BlockSpec((1, columns, width), lambda i, _: (i, part, 0))
    scalars = jnp.concatenate([starts, offset.reshape(1)]).astype(jnp.int32)
    whole = lambda shape: pl.BlockSpec(shape, lambda i, _: (0,) * len(shape), pipeline_mode=pl.Buffered(1))
    sizes = [columns] + [8] * pieces
    outs = pl.pallas_call(
        functools.partial(extend_kernel, first_place, map_blocks),
        out_shape=[jax.ShapeDtypeStruct((steps, size, width), jnp.float32) for size in sizes],
        grid_spec=pltpu.PrefetchScalarGridSpec(
            num_scalar_prefetch=1,
            grid=(steps,),
            in_specs=[whole(places.shape), front_spec, whole(source.shape)],
            out_specs=[pl.BlockSpec((1, size, width), lambda i, _: (i, 0, 0)) for size in sizes],
        ),
        compiler_params=pltpu.CompilerParams(vmem_limit_bytes=VMEM_BYTES),
    )(scalars, places, front, source)
    return outs if pieces else outs[0]


def halves(x):
    high = x.astype(jnp.bfloat16)
    return high, (x - high.astype(jnp.float32)).astype(jnp.bfloat16)


def product(left, right, dims):
    left_high, left_low = left
    right_high, right_low = right
    dot = lambda a, b: lax.dot_general(a, b, (dims, ((), ())), preferred_element_type=jnp.float32)
    return dot(left_high, right_high) + (dot(left_high, right_low) + dot(left_low, right_high))


PLAIN = ((1,), (0,))
CROSS = ((1,), (1,))


def factor_kernel(flags, gathered_ref, first_ref, second_ref, fixed_ref):
    place, kept = flags[0], flags[1]
    thin = (gathered_ref.shape[1] - 8) // 3
    by_chip = lambda x: jnp.concatenate([x[:, 8 * q : 8 * q + 8].reshape(-1, x.shape[2]) for q in range(thin // 8)])
    strip = gathered_ref[:, :thin].reshape(PANEL, 2 * PANEL)
    corner = by_chip(gathered_ref[:, thin : 2 * thin])
    inverse = by_chip(gathered_ref[:, 2 * thin : 3 * thin])
    inverse0, inverse1 = inverse[:, :PANEL], inverse[:, PANEL:]
    halves0, halves1 = halves(inverse0), halves(inverse1)
    corner10, corner01 = halves(corner[:, :PANEL]), halves(corner[:, PANEL:])
    first = product(halves(strip[:, :PANEL]), halves0, CROSS)
    lowered = product(halves(first), corner10, PLAIN)
    pivot1 = strip[:, PANEL:] - jnp.where(kept == 1, lowered, 0.0)
    second = product(halves(pivot1), halves1, CROSS)
    second = jnp.where(place == 1, -inverse1.T, second)
    crossed = product(halves(second), corner01, PLAIN)
    fixed = product(halves(crossed), halves0, CROSS)
    first_ref[...] = jnp.where(place == 0, -inverse0.T, jnp.where(place == 1, 0.0, first))
    second_ref[...] = second
    fixed_ref[...] = fixed


def factor(flags, gathered):
    square = jax.ShapeDtypeStruct((PANEL, PANEL), jnp.float32)
    return pl.pallas_call(
        factor_kernel,
        out_shape=(square, square, square),
        grid_spec=pltpu.PrefetchScalarGridSpec(
            num_scalar_prefetch=1,
            grid=(1,),
            in_specs=[pl.BlockSpec(gathered.shape, lambda i, _: (0, 0, 0))],
            out_specs=[pl.BlockSpec((PANEL, PANEL), lambda i, _: (0, 0))] * 3,
        ),
        compiler_params=pltpu.CompilerParams(vmem_limit_bytes=VMEM_BYTES),
    )(flags, gathered)


def update_kernel(flags, *refs):
    part_refs, (panels_ref, first_ref, second_ref, fixed_ref, out_ref) = refs[:-5], refs[-5:]
    tile = pl.program_id(0)
    keep, use_first, use_fixed, use_second = (flags[4 * tile + i] == 1 for i in range(4))
    left0 = first_ref[...] - jnp.where(use_fixed, fixed_ref[...], 0.0)
    left0 = halves(jnp.where(use_first, left0, 0.0))
    left1 = halves(jnp.where(use_second, second_ref[...], 0.0))
    panel = panels_ref[...]
    right0 = halves(panel[:, 0].reshape(PANEL, PANEL))
    right1 = halves(panel[:, 1].reshape(PANEL, PANEL))
    update = product(left0, right0, PLAIN) + product(left1, right1, PLAIN)
    block = jnp.concatenate([part[...] for part in part_refs], axis=1).reshape(PANEL, PANEL)
    out_ref[...] = (jnp.where(keep, block, 0.0) - update).T


def update(flags, parts, panels, first, second, fixed):
    rows = panels.shape[3]
    square = pl.BlockSpec((PANEL, PANEL), lambda i, _: (0, 0))
    return pl.pallas_call(
        update_kernel,
        out_shape=jax.ShapeDtypeStruct((rows, PANEL), jnp.float32),
        grid_spec=pltpu.PrefetchScalarGridSpec(
            num_scalar_prefetch=1,
            grid=(rows // PANEL,),
            in_specs=[pl.BlockSpec(part.shape[:2] + (PANEL,), lambda i, _: (0, 0, i)) for part in parts]
            + [
                pl.BlockSpec(panels.shape[:3] + (PANEL,), lambda i, _: (0, 0, 0, i)),
                square,
                square,
                square,
            ],
            out_specs=pl.BlockSpec((PANEL, PANEL), lambda i, _: (i, 0)),
        ),
        compiler_params=pltpu.CompilerParams(vmem_limit_bytes=VMEM_BYTES),
    )(flags, *parts, panels, first, second, fixed)


def local(front_entries, child_blocks, row_maps, pivot_inverses, tile_mask):
    thin, half_rows = front_entries.shape[2:]
    child_rows = child_blocks.shape[4]
    grid_rows = lax.axis_size("row")
    side = lax.axis_index("subcube")
    row_place = lax.axis_index("row")
    place = lax.axis_index("col")
    row_count = half_rows // grid_rows
    chunks = thin // 8
    pivot_rows = PANELS * PANEL
    own = child_blocks[0, 0, 0]
    front = front_entries[0, 0]
    zero = jnp.zeros((), jnp.int32)
    exchange = lambda x: lax.ppermute(x, "subcube", [(0, 1), (1, 0)])

    window = -(-(child_rows * 13 // 24) // LANES) * LANES
    rest = child_rows - window
    parts = chunks // 2
    share = thin // parts
    received = []
    for p in range(parts):
        late, early = own[p * share : (p + 1) * share, rest:], own[p * share : (p + 1) * share, :window]
        received.append(exchange(jnp.where(side == 0, late, early)))

    map_blocks = child_rows // LANES
    blocks = half_rows // LANES
    strip_blocks = pivot_rows // LANES
    maps = row_maps.reshape(2, map_blocks, LANES)
    count = lambda maps, edges: jnp.sum((maps[:, None, :] < edges[None, :, None]).astype(jnp.int32), axis=2)
    edges = LANES * jnp.arange(blocks, dtype=jnp.int32)
    strip_starts = count(row_maps, edges[:strip_blocks])
    strip_places = search(maps, [zero, zero + 1], [zero, zero], [strip_starts[0], strip_starts[1]])
    strip_add = lambda base, child, t: extend_add(
        base, child, strip_places, t * strip_blocks, strip_starts[t], zero, map_blocks, 1
    )[0]
    mask_rows = jnp.zeros((8, pivot_rows), jnp.float32)
    mask_rows = mask_rows.at[0, : tile_mask.shape[0]].set(tile_mask.astype(jnp.float32)[:, 0])
    prefix = own[:, :pivot_rows]
    base = strip_add(front[:, :pivot_rows], prefix, 0)
    got = exchange(jnp.concatenate([jnp.where(side == 0, base, prefix), mask_rows]))
    strip = strip_add(jnp.where(side == 0, base, got[:thin]), jnp.where(side == 0, got[:thin], prefix), 1)
    first_masks = jnp.where(side == 0, mask_rows, got[thin:])

    def to_chips(pieces):
        mine = jnp.where(place // PANELS == 0, pieces[0], 0.0)
        for chunk in range(1, chunks):
            pairs = [(k, PANELS * chunk + k) for k in range(PANELS)]
            mine = mine + lax.ppermute(pieces[chunk], "col", pairs)
        return mine

    corner = jnp.where(place == 0, strip[:, PANEL:], strip[:, :PANEL])
    corner, received[2] = lax.optimization_barrier((corner, received[2]))
    corner = to_chips([jnp.concatenate([corner, mask_rows[:, :PANEL]])] * chunks)
    corner, received[1] = lax.optimization_barrier((corner, received[1]))
    other = lax.ppermute(corner, "col", [(c, c ^ 1) for c in range(lax.axis_size("col"))])
    core0 = place % PANELS == 0
    corner = jnp.concatenate([jnp.where(core0, corner, other), jnp.where(core0, other, corner)], axis=1)
    cross_mask = corner[thin, PANEL : PANEL + tile_mask.shape[0]] > 0.5
    inverse = jnp.concatenate([pivot_inverses[k] for k in range(PANELS)], axis=1)
    gathered = lax.all_gather(jnp.concatenate([strip, corner[:thin], inverse, first_masks]), "row", axis=0)
    kept = gathered[0, 3 * thin, 1] > 0.5

    first_row = (side * half_rows).astype(jnp.int32)
    own_map = lax.dynamic_index_in_dim(row_maps, side, 0, keepdims=False)
    other_map = lax.dynamic_index_in_dim(row_maps, 1 - side, 0, keepdims=False)
    starts = count(jnp.stack([own_map, other_map]), first_row + edges)
    places = search(
        maps,
        [side.astype(jnp.int32), (1 - side).astype(jnp.int32)],
        [first_row, first_row],
        [starts[0], starts[1]],
    )
    lower = jnp.sum((row_maps < half_rows).astype(jnp.int32), axis=1)
    spill = (child_rows - lower[0] > window) | (lower[1] > window)
    window_at = jnp.where(side == 0, 0, rest // LANES).astype(jnp.int32)
    rest_at = jnp.where(side == 0, window // LANES, 0).astype(jnp.int32)
    add = functools.partial(extend_add, places=places, map_blocks=map_blocks, steps=grid_rows)
    base = add(front, own, first_place=0, starts=starts[0], offset=zero)
    add_other = functools.partial(add, first_place=blocks, starts=starts[1])

    def add_rest(base):
        more = exchange(jnp.where(side == 0, own[:, :rest], own[:, window:]))
        return add_other(base, more, offset=rest_at)

    base = lax.cond(spill, add_rest, lambda x: x, base)

    across = lambda x: lax.all_to_all(x, "row", split_axis=0, concat_axis=0, tiled=True)
    wholes, pieces = [], []
    for p in range(parts):
        whole, *halves_of = add_other(base, received[p], offset=window_at, part=p, pieces=2)
        wholes.append(whole)
        pieces += halves_of
    mine = across(to_chips(pieces))
    panels = lax.all_gather(mine.reshape(thin, row_count), "col", axis=0, tiled=True)
    panels = panels.reshape(chunks, PANELS, thin, row_count)
    late = parts // 2
    *last, mine = lax.optimization_barrier((*wholes[late:], mine))
    moved = [across(x) for x in wholes[:late]] + [across(x) for x in last]

    first, second, fixed = factor(jnp.stack([place, kept.astype(place.dtype)]).astype(jnp.int32), gathered)

    tiles = row_count // PANEL
    tile_ids = (side * grid_rows + row_place) * tiles + jnp.arange(tiles, dtype=jnp.int32)
    own_mask = tile_mask[:, 0] == 1
    is0, is1 = place == 0, place == 1
    keep = jnp.where(is0, False, jnp.where(is1, tile_ids == 0, True))
    use_first = jnp.where(is0, True, jnp.where(is1, tile_ids >= 1, own_mask & (tile_ids >= 1)))
    use_fixed = jnp.where(is0, False, cross_mask & (tile_ids >= jnp.where(is1, 1, 2)))
    use_second = jnp.where(is0, False, jnp.where(is1, tile_ids >= 1, own_mask & (tile_ids >= 2)))
    flags = jnp.stack([keep, use_first, use_fixed, use_second], axis=1).astype(jnp.int32).reshape(-1)
    return update(flags, moved, panels, first, second, fixed)


def solution(mesh):
    return jax.shard_map(
        local,
        mesh=mesh,
        in_specs=(
            P("col", "row", None, "subcube"),
            P("subcube", "col", "row", None, None),
            P(),
            P(None, "row", None),
            P(("subcube", "row"), "col"),
        ),
        out_specs=P(("subcube", "row"), "col"),
        check_vma=False,
    )
```

```python
import functools

import jax
import jax.numpy as jnp
from jax import lax
from jax.experimental import pallas as pl
from jax.experimental.pallas import tpu as pltpu
from jax.sharding import PartitionSpec as P

PANEL = 512
PANELS = 2
LANES = 128
BIG = 2**30
VMEM_BYTES = 56 * 2**20


def search_kernel(sections, scalars, maps_ref, places_ref, low_ref, high_ref):
    map_blocks = maps_ref.shape[1]
    at_row = 0
    for section, count in enumerate(sections):
        child = scalars[section]
        first = scalars[len(sections) + section]
        for block in range(count):
            at = jnp.minimum(scalars[2 * len(sections) + at_row + block] // LANES, map_blocks - 1)
            after = jnp.minimum(at + 1, map_blocks - 1)
            row = at_row + block
            low_ref[row : row + 1, :] = maps_ref[child, pl.ds(at, 1), :]
            high_ref[row : row + 1, :] = jnp.where(at + 1 < map_blocks, maps_ref[child, pl.ds(after, 1), :], BIG)
        low, high = low_ref[at_row : at_row + count, :], high_ref[at_row : at_row + count, :]
        lane = lax.broadcasted_iota(jnp.int32, low.shape, 1)
        block_id = lax.broadcasted_iota(jnp.int32, low.shape, 0)
        wanted = first + block_id * LANES + lane

        def pick(at):
            inner = at & (LANES - 1)
            return jnp.where(
                at < LANES, jnp.take_along_axis(low, inner, axis=1), jnp.take_along_axis(high, inner, axis=1)
            )

        place = jnp.zeros(low.shape, jnp.int32)
        width = LANES
        while width >= 1:
            place = jnp.where(pick(place + (width - 1)) < wanted, place + width, place)
            width //= 2
        places_ref[at_row : at_row + count, :] = jnp.where(pick(place) == wanted, place, -1)
        at_row += count


def search(maps, children, firsts, starts):
    sections = tuple(start.shape[0] for start in starts)
    total = sum(sections)
    scalars = jnp.concatenate([jnp.stack(children), jnp.stack(firsts)] + list(starts)).astype(jnp.int32)
    return pl.pallas_call(
        functools.partial(search_kernel, sections),
        out_shape=jax.ShapeDtypeStruct((total, LANES), jnp.int32),
        grid_spec=pltpu.PrefetchScalarGridSpec(
            num_scalar_prefetch=1,
            grid=(1,),
            in_specs=[pl.BlockSpec(maps.shape, lambda i, _: (0, 0, 0))],
            out_specs=pl.BlockSpec((total, LANES), lambda i, _: (0, 0)),
            scratch_shapes=[pltpu.VMEM((total, LANES), jnp.int32)] * 2,
        ),
        compiler_params=pltpu.CompilerParams(vmem_limit_bytes=VMEM_BYTES),
    )(scalars, maps)


def extend_kernel(first_place, map_blocks, scalars, places_ref, front_ref, source_ref, out_ref, *piece_refs):
    step = pl.program_id(0)
    columns = out_ref.shape[1]
    per_step = out_ref.shape[2] // LANES
    source_blocks = source_ref.shape[1] // LANES
    offset = scalars[scalars.shape[0] - 1]
    lane = lax.broadcasted_iota(jnp.int32, (8, LANES), 1)
    group = max(1, 256 // columns)
    for group_start in range(0, per_step, group):
        gained = {}
        members = range(group_start, min(per_step, group_start + group))
        for j in members:
            block = step * per_step + j
            start = scalars[block]
            at = jnp.minimum(start // LANES, map_blocks - 1)
            split = jnp.where(start // LANES < map_blocks, start & (LANES - 1), LANES)
            at = at - offset
            inside_low = (at >= 0) & (at < source_blocks)
            inside_high = (at + 1 >= 0) & (at + 1 < source_blocks)
            low_at = pl.multiple_of(jnp.clip(at, 0, source_blocks - 1) * LANES, LANES)
            high_at = pl.multiple_of(jnp.clip(at + 1, 0, source_blocks - 1) * LANES, LANES)
            place = jnp.broadcast_to(places_ref[pl.ds(first_place + block, 1), :], (8, LANES))
            inner = place & (LANES - 1)
            hit = ((place >= 0) & (place < LANES) & inside_low) | ((place >= LANES) & inside_high)
            from_low = lane >= split
            for row in range(0, columns, 8):
                rows = slice(row, row + 8)
                merged = jnp.where(
                    from_low, source_ref[rows, pl.ds(low_at, LANES)], source_ref[rows, pl.ds(high_at, LANES)]
                )
                gained[j, row] = jnp.where(hit, jnp.take_along_axis(merged, inner, axis=1), 0.0)
        for j in members:
            here = slice(j * LANES, (j + 1) * LANES)
            for row in range(0, columns, 8):
                rows = slice(row, row + 8)
                value = front_ref[..., rows, here].reshape(8, LANES) + gained[j, row]
                out_ref[0, rows, here] = value
                if piece_refs:
                    piece_refs[row // 8][0, :, here] = value


def extend_add(front, source, places, first_place, starts, offset, map_blocks, steps, width, columns=None, part=0, pieces=0):
    columns = source.shape[0] if columns is None else columns
    if front.ndim == 2:
        front_spec = pl.BlockSpec((columns, width), lambda i, _: (part, i))
    else:
        front_spec = pl.BlockSpec((1, columns, width), lambda i, _: (i, 0, 0))
    source_width = min(source.shape[1], map_blocks * LANES if steps > 1 else width)
    scalars = jnp.concatenate([starts, offset.reshape(1)]).astype(jnp.int32)
    whole = lambda shape, row=0: pl.BlockSpec(shape, lambda i, _: (row, 0), pipeline_mode=pl.Buffered(1))
    sizes = [columns] + [8] * pieces
    outs = pl.pallas_call(
        functools.partial(extend_kernel, first_place, map_blocks),
        out_shape=[jax.ShapeDtypeStruct((steps, size, width), jnp.float32) for size in sizes],
        grid_spec=pltpu.PrefetchScalarGridSpec(
            num_scalar_prefetch=1,
            grid=(steps,),
            in_specs=[whole(places.shape), front_spec, whole((columns, source_width), part)],
            out_specs=[pl.BlockSpec((1, size, width), lambda i, _: (i, 0, 0)) for size in sizes],
        ),
        compiler_params=pltpu.CompilerParams(vmem_limit_bytes=VMEM_BYTES),
    )(scalars, places, front, source)
    return outs if pieces else outs[0]


def halves(x):
    high = x.astype(jnp.bfloat16)
    return high, (x - high.astype(jnp.float32)).astype(jnp.bfloat16)


def product(left, right, dims):
    left_high, left_low = left
    right_high, right_low = right
    dot = lambda a, b: lax.dot_general(a, b, (dims, ((), ())), preferred_element_type=jnp.float32)
    return dot(left_high, right_high) + (dot(left_high, right_low) + dot(left_low, right_high))


PLAIN = ((1,), (0,))
CROSS = ((1,), (1,))


def factor_kernel(order, flags, gathered_ref, inverse_ref, first_ref, second_ref, fixed_ref):
    place, kept = flags[0], flags[1]
    thin = inverse_ref.shape[1]
    by_chip = lambda x: jnp.concatenate([x[:, 8 * q : 8 * q + 8].reshape(-1, x.shape[2]) for q in order])
    strip = gathered_ref[:, :thin].reshape(PANEL, 2 * PANEL)
    corner = by_chip(gathered_ref[:, thin : 2 * thin])
    inverse = by_chip(inverse_ref[...])
    inverse0, inverse1 = inverse[:, :PANEL], inverse[:, PANEL:]
    halves0, halves1 = halves(inverse0), halves(inverse1)
    corner10, corner01 = halves(corner[:, :PANEL]), halves(corner[:, PANEL:])
    first = product(halves(strip[:, :PANEL]), halves0, CROSS)
    lowered = product(halves(first), corner10, PLAIN)
    pivot1 = strip[:, PANEL:] - jnp.where(kept == 1, lowered, 0.0)
    second = product(halves(pivot1), halves1, CROSS)
    second = jnp.where(place == 1, -inverse1.T, second)
    crossed = product(halves(second), corner01, PLAIN)
    fixed = product(halves(crossed), halves0, CROSS)
    first_ref[...] = jnp.where(place == 0, -inverse0.T, jnp.where(place == 1, 0.0, first))
    second_ref[...] = second
    fixed_ref[...] = fixed


def factor(order, flags, gathered, inverse):
    square = jax.ShapeDtypeStruct((PANEL, PANEL), jnp.float32)
    return pl.pallas_call(
        functools.partial(factor_kernel, order),
        out_shape=(square, square, square),
        grid_spec=pltpu.PrefetchScalarGridSpec(
            num_scalar_prefetch=1,
            grid=(1,),
            in_specs=[pl.BlockSpec(x.shape, lambda i, _: (0, 0, 0)) for x in (gathered, inverse)],
            out_specs=[pl.BlockSpec((PANEL, PANEL), lambda i, _: (0, 0))] * 3,
        ),
        compiler_params=pltpu.CompilerParams(vmem_limit_bytes=VMEM_BYTES),
    )(flags, gathered, inverse)


def update_kernel(flags, *refs):
    part_refs, (panels_ref, first_ref, second_ref, fixed_ref, out_ref) = refs[:-5], refs[-5:]
    tile = pl.program_id(0)
    keep, use_first, use_fixed, use_second = (flags[4 * tile + i] == 1 for i in range(4))
    left0 = first_ref[...] - jnp.where(use_fixed, fixed_ref[...], 0.0)
    left0 = halves(jnp.where(use_first, left0, 0.0))
    left1 = halves(jnp.where(use_second, second_ref[...], 0.0))
    panel = panels_ref[...]
    right0 = halves(panel[:, 0].reshape(PANEL, PANEL))
    right1 = halves(panel[:, 1].reshape(PANEL, PANEL))
    update = product(left0, right0, PLAIN) + product(left1, right1, PLAIN)
    block = jnp.concatenate([part[...] for part in part_refs], axis=1).reshape(PANEL, PANEL)
    out_ref[...] = (jnp.where(keep, block, 0.0) - update).T


def update(flags, parts, panels, first, second, fixed):
    rows = panels.shape[3]
    square = pl.BlockSpec((PANEL, PANEL), lambda i, _: (0, 0))
    return pl.pallas_call(
        update_kernel,
        out_shape=jax.ShapeDtypeStruct((rows, PANEL), jnp.float32),
        grid_spec=pltpu.PrefetchScalarGridSpec(
            num_scalar_prefetch=1,
            grid=(rows // PANEL,),
            in_specs=[pl.BlockSpec(part.shape[:2] + (PANEL,), lambda i, _: (0, 0, i)) for part in parts]
            + [
                pl.BlockSpec(panels.shape[:3] + (PANEL,), lambda i, _: (0, 0, 0, i)),
                square,
                square,
                square,
            ],
            out_specs=pl.BlockSpec((PANEL, PANEL), lambda i, _: (i, 0)),
        ),
        compiler_params=pltpu.CompilerParams(vmem_limit_bytes=VMEM_BYTES),
    )(flags, *parts, panels, first, second, fixed)


def local(front_entries, child_blocks, row_maps, pivot_inverses, tile_mask):
    thin, half_rows = front_entries.shape[2:]
    child_rows = child_blocks.shape[4]
    grid_rows = lax.axis_size("row")
    side = lax.axis_index("subcube")
    row_place = lax.axis_index("row")
    place = lax.axis_index("col")
    row_count = half_rows // grid_rows
    chunks = thin // 8
    pivot_rows = PANELS * PANEL
    own = child_blocks[0, 0, 0]
    front = front_entries[0, 0]
    zero = jnp.zeros((), jnp.int32)
    exchange = lambda x: lax.ppermute(x, "subcube", [(0, 1), (1, 0)])

    inverse = lax.all_gather(jnp.concatenate([pivot_inverses[k] for k in range(PANELS)], axis=1), "row", axis=0)

    window = -(-(child_rows * 13 // 24) // LANES) * LANES
    rest = child_rows - window
    tail = thin // 4
    parts = [(thin - tail, thin), (0, thin - tail)]
    received = [exchange(jnp.where(side == 0, own[a:b, rest:], own[a:b, :window])) for a, b in parts]

    map_blocks = child_rows // LANES
    blocks = half_rows // LANES
    strip_blocks = pivot_rows // LANES
    maps = row_maps.reshape(2, map_blocks, LANES)
    count = lambda maps, edges: jnp.sum((maps[:, None, :] < edges[None, :, None]).astype(jnp.int32), axis=2)
    edges = LANES * jnp.arange(blocks, dtype=jnp.int32)
    strip_starts = count(row_maps, edges[:strip_blocks])
    strip_places = search(maps, [zero, zero + 1], [zero, zero], [strip_starts[0], strip_starts[1]])
    strip_add = lambda base, child, t: extend_add(
        base, child, strip_places, t * strip_blocks, strip_starts[t], zero, map_blocks, 1, pivot_rows
    )[0]
    mask_rows = jnp.zeros((8, pivot_rows), jnp.float32)
    mask_rows = mask_rows.at[0, : tile_mask.shape[0]].set(tile_mask.astype(jnp.float32)[:, 0])
    prefix = own[:, :pivot_rows]
    base = strip_add(front, own, 0)
    got = exchange(jnp.concatenate([jnp.where(side == 0, base, prefix), mask_rows]))
    got, received[0] = lax.optimization_barrier((got, received[0]))
    strip = strip_add(jnp.where(side == 0, base, got[:thin]), jnp.where(side == 0, got[:thin], prefix), 1)
    first_masks = jnp.where(side == 0, mask_rows, got[thin:])

    cols = lax.axis_size("col")
    corner = jnp.where(place == 0, strip[:, PANEL:], strip[:, :PANEL])
    corner = jnp.where(place < PANELS, jnp.concatenate([corner, mask_rows[:, :PANEL]]), 0.0)
    reach = cols // 2
    while reach >= PANELS:
        pairs = [(c, c + reach) for c in range(cols) if c % (2 * reach) < PANELS]
        corner = corner + lax.ppermute(corner, "col", pairs)
        reach //= 2
    corner, received[1], inverse = lax.optimization_barrier((corner, received[1], inverse))
    other = lax.ppermute(corner, "col", [(c, c ^ 1) for c in range(cols)])
    core0 = place % PANELS == 0
    corner = jnp.concatenate([jnp.where(core0, corner, other), jnp.where(core0, other, corner)], axis=1)
    cross_mask = corner[thin, PANEL : PANEL + tile_mask.shape[0]] > 0.5
    gathered = lax.all_gather(jnp.concatenate([strip, corner[:thin], first_masks]), "row", axis=0)
    kept = gathered[0, 2 * thin, 1] > 0.5

    first_row = (side * half_rows).astype(jnp.int32)
    own_map = lax.dynamic_index_in_dim(row_maps, side, 0, keepdims=False)
    other_map = lax.dynamic_index_in_dim(row_maps, 1 - side, 0, keepdims=False)
    starts = count(jnp.stack([own_map, other_map]), first_row + edges)
    places = search(
        maps,
        [side.astype(jnp.int32), (1 - side).astype(jnp.int32)],
        [first_row, first_row],
        [starts[0], starts[1]],
    )
    lower = jnp.sum((row_maps < half_rows).astype(jnp.int32), axis=1)
    spill = (child_rows - lower[0] > window) | (lower[1] > window)
    window_at = jnp.where(side == 0, 0, rest // LANES).astype(jnp.int32)
    rest_at = jnp.where(side == 0, window // LANES, 0).astype(jnp.int32)
    add = functools.partial(extend_add, places=places, map_blocks=map_blocks, steps=grid_rows, width=row_count)
    add_own = functools.partial(add, first_place=0, starts=starts[0], offset=zero)
    add_other = functools.partial(add, first_place=blocks, starts=starts[1])
    bases = [add_own(front, own, columns=b - a, part=a // (b - a)) for a, b in parts]

    def add_rest(bases):
        more = exchange(jnp.where(side == 0, own[:, :rest], own[:, window:]))
        return tuple(
            add_other(base, more, offset=rest_at, columns=b - a, part=a // (b - a)) for base, (a, b) in zip(bases, parts)
        )

    bases = lax.cond(spill, add_rest, lambda x: x, tuple(bases))

    across = lambda x: lax.all_to_all(x, "row", split_axis=0, concat_axis=0, tiled=True)
    wholes, pieces = [], {}
    for base, part, (a, b) in zip(bases, received, parts):
        whole, *chunk_list = add_other(base, part, offset=window_at, pieces=(b - a) // 8)
        wholes.append(whole)
        pieces.update({a // 8 + i: chunk for i, chunk in enumerate(chunk_list)})
    order = list(range(chunks))
    middle = chunks // 2
    order[middle : middle + 2], order[-2:] = order[-2:], order[middle : middle + 2]
    mine = jnp.where(place // PANELS == 0, pieces[order[0]], 0.0)
    for chip in range(1, chunks):
        pairs = [(k, PANELS * chip + k) for k in range(PANELS)]
        mine = mine + lax.ppermute(pieces[order[chip]], "col", pairs)
    moved = [across(wholes[0])]
    mine, moved[0] = lax.optimization_barrier((mine, moved[0]))
    mine = across(mine)
    panels = lax.all_gather(mine.reshape(thin, row_count), "col", axis=0, tiled=True)
    panels = panels.reshape(chunks, PANELS, thin, row_count)
    last, mine = lax.optimization_barrier((wholes[1], mine))
    moved.append(across(last))

    first, second, fixed = factor(
        order, jnp.stack([place, kept.astype(place.dtype)]).astype(jnp.int32), gathered, inverse
    )

    tiles = row_count // PANEL
    tile_ids = (side * grid_rows + row_place) * tiles + jnp.arange(tiles, dtype=jnp.int32)
    own_mask = tile_mask[:, 0] == 1
    is0, is1 = place == 0, place == 1
    keep = jnp.where(is0, False, jnp.where(is1, tile_ids == 0, True))
    use_first = jnp.where(is0, True, jnp.where(is1, tile_ids >= 1, own_mask & (tile_ids >= 1)))
    use_fixed = jnp.where(is0, False, cross_mask & (tile_ids >= jnp.where(is1, 1, 2)))
    use_second = jnp.where(is0, False, jnp.where(is1, tile_ids >= 1, own_mask & (tile_ids >= 2)))
    flags = jnp.stack([keep, use_first, use_fixed, use_second], axis=1).astype(jnp.int32).reshape(-1)
    return update(flags, moved[::-1], panels, first, second, fixed)


def solution(mesh):
    return jax.shard_map(
        local,
        mesh=mesh,
        in_specs=(
            P("col", "row", None, "subcube"),
            P("subcube", "col", "row", None, None),
            P(),
            P(None, "row", None),
            P(("subcube", "row"), "col"),
        ),
        out_specs=P(("subcube", "row"), "col"),
        check_vma=False,
    )
```

```python
import functools

import jax
import jax.numpy as jnp
from jax import lax
from jax.experimental import pallas as pl
from jax.experimental.pallas import tpu as pltpu
from jax.sharding import PartitionSpec as P

PANEL = 512
PANELS = 2
LANES = 128
BIG = 2**30
VMEM_BYTES = 56 * 2**20


def search_kernel(sections, scalars, maps_ref, places_ref, low_ref, high_ref):
    map_blocks = maps_ref.shape[1]
    at_row = 0
    for section, count in enumerate(sections):
        child = scalars[section]
        first = scalars[len(sections) + section]
        for block in range(count):
            at = jnp.minimum(scalars[2 * len(sections) + at_row + block] // LANES, map_blocks - 1)
            after = jnp.minimum(at + 1, map_blocks - 1)
            row = at_row + block
            low_ref[row : row + 1, :] = maps_ref[child, pl.ds(at, 1), :]
            high_ref[row : row + 1, :] = jnp.where(at + 1 < map_blocks, maps_ref[child, pl.ds(after, 1), :], BIG)
        low, high = low_ref[at_row : at_row + count, :], high_ref[at_row : at_row + count, :]
        lane = lax.broadcasted_iota(jnp.int32, low.shape, 1)
        block_id = lax.broadcasted_iota(jnp.int32, low.shape, 0)
        wanted = first + block_id * LANES + lane

        def pick(at):
            inner = at & (LANES - 1)
            return jnp.where(
                at < LANES, jnp.take_along_axis(low, inner, axis=1), jnp.take_along_axis(high, inner, axis=1)
            )

        place = jnp.zeros(low.shape, jnp.int32)
        width = LANES
        while width >= 1:
            place = jnp.where(pick(place + (width - 1)) < wanted, place + width, place)
            width //= 2
        places_ref[at_row : at_row + count, :] = jnp.where(pick(place) == wanted, place, -1)
        at_row += count


def search(maps, children, firsts, starts):
    sections = tuple(start.shape[0] for start in starts)
    total = sum(sections)
    scalars = jnp.concatenate([jnp.stack(children), jnp.stack(firsts)] + list(starts)).astype(jnp.int32)
    return pl.pallas_call(
        functools.partial(search_kernel, sections),
        out_shape=jax.ShapeDtypeStruct((total, LANES), jnp.int32),
        grid_spec=pltpu.PrefetchScalarGridSpec(
            num_scalar_prefetch=1,
            grid=(1,),
            in_specs=[pl.BlockSpec(maps.shape, lambda i, _: (0, 0, 0))],
            out_specs=pl.BlockSpec((total, LANES), lambda i, _: (0, 0)),
            scratch_shapes=[pltpu.VMEM((total, LANES), jnp.int32)] * 2,
        ),
        compiler_params=pltpu.CompilerParams(vmem_limit_bytes=VMEM_BYTES),
    )(scalars, maps)


def extend_kernel(first_place, map_blocks, scalars, places_ref, front_ref, source_ref, out_ref, *piece_refs):
    step = pl.program_id(0)
    groups, columns, width = out_ref.shape
    per_group = width // LANES
    source_blocks = source_ref.shape[1] // LANES
    offset = scalars[scalars.shape[0] - 1]
    lane = lax.broadcasted_iota(jnp.int32, (8, LANES), 1)
    for j in range(groups * per_group):
        block = step * groups * per_group + j
        start = scalars[block]
        at = jnp.minimum(start // LANES, map_blocks - 1)
        split = jnp.where(start // LANES < map_blocks, start & (LANES - 1), LANES)
        at = at - offset
        inside_low = (at >= 0) & (at < source_blocks)
        inside_high = (at + 1 >= 0) & (at + 1 < source_blocks)
        low_at = pl.multiple_of(jnp.clip(at, 0, source_blocks - 1) * LANES, LANES)
        high_at = pl.multiple_of(jnp.clip(at + 1, 0, source_blocks - 1) * LANES, LANES)
        place = jnp.broadcast_to(places_ref[pl.ds(first_place + block, 1), :], (8, LANES))
        inner = place & (LANES - 1)
        hit = ((place >= 0) & (place < LANES) & inside_low) | ((place >= LANES) & inside_high)
        from_low = lane >= split
        group = j // per_group
        here = slice(j % per_group * LANES, (j % per_group + 1) * LANES)
        for row in range(0, columns, 8):
            rows = slice(row, row + 8)
            merged = jnp.where(from_low, source_ref[rows, pl.ds(low_at, LANES)], source_ref[rows, pl.ds(high_at, LANES)])
            gained = jnp.where(hit, jnp.take_along_axis(merged, inner, axis=1), 0.0)
            if len(front_ref.shape) == 2:
                value = front_ref[rows, j * LANES : (j + 1) * LANES] + gained
            else:
                value = front_ref[group, rows, here] + gained
            out_ref[group, rows, here] = value
            if piece_refs:
                piece_refs[row // 8][group, :, here] = value


def extend_add(front, source, places, first_place, starts, offset, map_blocks, groups, width, columns=None, part=0, pieces=0):
    columns = source.shape[0] if columns is None else columns
    steps = 2 if groups % 2 == 0 else 1
    per_step = groups // steps
    if front.ndim == 2:
        front_spec = pl.BlockSpec((columns, per_step * width), lambda i, _: (part, i))
    else:
        front_spec = pl.BlockSpec((per_step, columns, width), lambda i, _: (i, part, 0))
    source_part = part if source.shape[0] > columns else 0
    source_width = min(source.shape[1], map_blocks * LANES if groups > 1 else width)
    scalars = jnp.concatenate([starts, offset.reshape(1)]).astype(jnp.int32)
    whole = lambda shape, row=0: pl.BlockSpec(shape, lambda i, _: (row, 0), pipeline_mode=pl.Buffered(1))
    sizes = [columns] + [8] * pieces
    outs = pl.pallas_call(
        functools.partial(extend_kernel, first_place, map_blocks),
        out_shape=[jax.ShapeDtypeStruct((groups, size, width), jnp.float32) for size in sizes],
        grid_spec=pltpu.PrefetchScalarGridSpec(
            num_scalar_prefetch=1,
            grid=(steps,),
            in_specs=[whole(places.shape), front_spec, whole((columns, source_width), source_part)],
            out_specs=[pl.BlockSpec((per_step, size, width), lambda i, _: (i, 0, 0)) for size in sizes],
        ),
        compiler_params=pltpu.CompilerParams(vmem_limit_bytes=VMEM_BYTES),
    )(scalars, places, front, source)
    return outs if pieces else outs[0]


def halves(x):
    high = x.astype(jnp.bfloat16)
    return high, (x - high.astype(jnp.float32)).astype(jnp.bfloat16)


def product(left, right, dims):
    left_high, left_low = left
    right_high, right_low = right
    dot = lambda a, b: lax.dot_general(a, b, (dims, ((), ())), preferred_element_type=jnp.float32)
    return dot(left_high, right_high) + (dot(left_high, right_low) + dot(left_low, right_high))


PLAIN = ((1,), (0,))
CROSS = ((1,), (1,))


def factor_kernel(order, flags, gathered_ref, inverse_ref, first_ref, second_ref, fixed_ref):
    place, kept = flags[0], flags[1]
    thin = inverse_ref.shape[1]
    by_chip = lambda x: jnp.concatenate([x[:, 8 * q : 8 * q + 8].reshape(-1, x.shape[2]) for q in order])
    strip = gathered_ref[:, :thin].reshape(PANEL, 2 * PANEL)
    corner = by_chip(gathered_ref[:, thin : 2 * thin])
    inverse = by_chip(inverse_ref[...])
    inverse0, inverse1 = inverse[:, :PANEL], inverse[:, PANEL:]
    halves0, halves1 = halves(inverse0), halves(inverse1)
    corner10, corner01 = halves(corner[:, :PANEL]), halves(corner[:, PANEL:])
    first = product(halves(strip[:, :PANEL]), halves0, CROSS)
    lowered = product(halves(first), corner10, PLAIN)
    pivot1 = strip[:, PANEL:] - jnp.where(kept == 1, lowered, 0.0)
    second = product(halves(pivot1), halves1, CROSS)
    second = jnp.where(place == 1, -inverse1.T, second)
    crossed = product(halves(second), corner01, PLAIN)
    fixed = product(halves(crossed), halves0, CROSS)
    first_ref[...] = jnp.where(place == 0, -inverse0.T, jnp.where(place == 1, 0.0, first))
    second_ref[...] = second
    fixed_ref[...] = fixed


def factor(order, flags, gathered, inverse):
    square = jax.ShapeDtypeStruct((PANEL, PANEL), jnp.float32)
    return pl.pallas_call(
        functools.partial(factor_kernel, order),
        out_shape=(square, square, square),
        grid_spec=pltpu.PrefetchScalarGridSpec(
            num_scalar_prefetch=1,
            grid=(1,),
            in_specs=[pl.BlockSpec(x.shape, lambda i, _: (0, 0, 0)) for x in (gathered, inverse)],
            out_specs=[pl.BlockSpec((PANEL, PANEL), lambda i, _: (0, 0))] * 3,
        ),
        compiler_params=pltpu.CompilerParams(vmem_limit_bytes=VMEM_BYTES),
    )(flags, gathered, inverse)


def update_kernel(flags, *refs):
    part_refs, (panels_ref, first_ref, second_ref, fixed_ref, out_ref) = refs[:-5], refs[-5:]
    tile = pl.program_id(0)
    keep, use_first, use_fixed, use_second = (flags[4 * tile + i] == 1 for i in range(4))
    left0 = first_ref[...] - jnp.where(use_fixed, fixed_ref[...], 0.0)
    left0 = halves(jnp.where(use_first, left0, 0.0))
    left1 = halves(jnp.where(use_second, second_ref[...], 0.0))
    panel = panels_ref[...]
    right0 = halves(panel[:, 0].reshape(PANEL, PANEL))
    right1 = halves(panel[:, 1].reshape(PANEL, PANEL))
    update = product(left0, right0, PLAIN) + product(left1, right1, PLAIN)
    block = jnp.concatenate([part[...] for part in part_refs], axis=1).reshape(PANEL, PANEL)
    out_ref[...] = (jnp.where(keep, block, 0.0) - update).T


def update(flags, parts, panels, first, second, fixed):
    rows = panels.shape[3]
    square = pl.BlockSpec((PANEL, PANEL), lambda i, _: (0, 0))
    return pl.pallas_call(
        update_kernel,
        out_shape=jax.ShapeDtypeStruct((rows, PANEL), jnp.float32),
        grid_spec=pltpu.PrefetchScalarGridSpec(
            num_scalar_prefetch=1,
            grid=(rows // PANEL,),
            in_specs=[pl.BlockSpec(part.shape[:2] + (PANEL,), lambda i, _: (0, 0, i)) for part in parts]
            + [
                pl.BlockSpec(panels.shape[:3] + (PANEL,), lambda i, _: (0, 0, 0, i)),
                square,
                square,
                square,
            ],
            out_specs=pl.BlockSpec((PANEL, PANEL), lambda i, _: (i, 0)),
        ),
        compiler_params=pltpu.CompilerParams(vmem_limit_bytes=VMEM_BYTES),
    )(flags, *parts, panels, first, second, fixed)


def local(front_entries, child_blocks, row_maps, pivot_inverses, tile_mask):
    thin, half_rows = front_entries.shape[2:]
    child_rows = child_blocks.shape[4]
    grid_rows = lax.axis_size("row")
    side = lax.axis_index("subcube")
    row_place = lax.axis_index("row")
    place = lax.axis_index("col")
    row_count = half_rows // grid_rows
    chunks = thin // 8
    pivot_rows = PANELS * PANEL
    own = child_blocks[0, 0, 0]
    front = front_entries[0, 0]
    zero = jnp.zeros((), jnp.int32)
    exchange = lambda x: lax.ppermute(x, "subcube", [(0, 1), (1, 0)])

    inverse = lax.all_gather(jnp.concatenate([pivot_inverses[k] for k in range(PANELS)], axis=1), "row", axis=0)

    window = -(-(child_rows * 13 // 24) // LANES) * LANES
    rest = child_rows - window
    parts = [(thin // 2, thin), (0, thin // 2)]
    first_sent, last_sent = [jnp.where(side == 0, own[a:b, rest:], own[a:b, :window]) for a, b in parts]
    received = [exchange(first_sent)]
    last_sent, received[0] = lax.optimization_barrier((last_sent, received[0]))
    received.append(exchange(last_sent))

    map_blocks = child_rows // LANES
    blocks = half_rows // LANES
    strip_blocks = pivot_rows // LANES
    maps = row_maps.reshape(2, map_blocks, LANES)
    count = lambda maps, edges: jnp.sum((maps[:, None, :] < edges[None, :, None]).astype(jnp.int32), axis=2)
    edges = LANES * jnp.arange(blocks, dtype=jnp.int32)
    strip_starts = count(row_maps, edges[:strip_blocks])
    strip_places = search(maps, [zero, zero + 1], [zero, zero], [strip_starts[0], strip_starts[1]])
    strip_add = lambda base, child, t: extend_add(
        base, child, strip_places, t * strip_blocks, strip_starts[t], zero, map_blocks, 1, pivot_rows
    )[0]
    mask_rows = jnp.zeros((8, pivot_rows), jnp.float32)
    mask_rows = mask_rows.at[0, : tile_mask.shape[0]].set(tile_mask.astype(jnp.float32)[:, 0])
    prefix = own[:, :pivot_rows]
    base = strip_add(front, own, 0)
    got = exchange(jnp.concatenate([jnp.where(side == 0, base, prefix), mask_rows]))

    first_row = (side * half_rows).astype(jnp.int32)
    own_map = lax.dynamic_index_in_dim(row_maps, side, 0, keepdims=False)
    other_map = lax.dynamic_index_in_dim(row_maps, 1 - side, 0, keepdims=False)
    starts = count(jnp.stack([own_map, other_map]), first_row + edges)
    places = search(
        maps,
        [side.astype(jnp.int32), (1 - side).astype(jnp.int32)],
        [first_row, first_row],
        [starts[0], starts[1]],
    )
    lower = jnp.sum((row_maps < half_rows).astype(jnp.int32), axis=1)
    spill = (child_rows - lower[0] > window) | (lower[1] > window)
    window_at = jnp.where(side == 0, 0, rest // LANES).astype(jnp.int32)
    rest_at = jnp.where(side == 0, window // LANES, 0).astype(jnp.int32)
    add = functools.partial(extend_add, places=places, map_blocks=map_blocks, groups=grid_rows, width=row_count)
    add_other = functools.partial(add, first_place=blocks, starts=starts[1])
    base_sum = add(front, own, first_place=0, starts=starts[0], offset=zero)

    def add_rest(base_sum):
        more = exchange(jnp.where(side == 0, own[:, :rest], own[:, window:]))
        return add_other(base_sum, more, offset=rest_at)

    base_sum = lax.cond(spill, add_rest, lambda x: x, base_sum)

    got, received[0], base_sum = lax.optimization_barrier((got, received[0], base_sum))
    strip = strip_add(jnp.where(side == 0, base, got[:thin]), jnp.where(side == 0, got[:thin], prefix), 1)
    first_masks = jnp.where(side == 0, mask_rows, got[thin:])

    wholes, pieces = [], {}

    def assemble(index):
        a, b = parts[index]
        size = b - a
        whole, *chunk_list = add_other(
            base_sum, received[index], offset=window_at, columns=size, part=a // size, pieces=size // 8
        )
        wholes.append(whole)
        pieces.update({a // 8 + i: chunk for i, chunk in enumerate(chunk_list)})

    assemble(0)
    strip, wholes[0] = lax.optimization_barrier((strip, wholes[0]))

    cols = lax.axis_size("col")
    corner = jnp.where(place == 0, strip[:, PANEL:], strip[:, :PANEL])
    corner = jnp.where(place < PANELS, jnp.concatenate([corner, mask_rows[:, :PANEL]]), 0.0)
    reach = cols // 2
    while reach >= PANELS:
        pairs = [(c, c + reach) for c in range(cols) if c % (2 * reach) < PANELS]
        corner = corner + lax.ppermute(corner, "col", pairs)
        reach //= 2
    corner, received[1], inverse = lax.optimization_barrier((corner, received[1], inverse))
    other = lax.ppermute(corner, "col", [(c, c ^ 1) for c in range(cols)])
    core0 = place % PANELS == 0
    corner = jnp.concatenate([jnp.where(core0, corner, other), jnp.where(core0, other, corner)], axis=1)
    cross_mask = corner[thin, PANEL : PANEL + tile_mask.shape[0]] > 0.5
    gathered = lax.all_gather(jnp.concatenate([strip, corner[:thin], first_masks]), "row", axis=0)
    kept = gathered[0, 2 * thin, 1] > 0.5

    across = lambda x: lax.all_to_all(x, "row", split_axis=0, concat_axis=0, tiled=True)
    assemble(1)
    order = [0, 1] + list(range(chunks // 2, chunks)) + list(range(2, chunks // 2))
    mine = jnp.where(place // PANELS == 0, pieces[order[0]], 0.0)
    for chip in range(1, chunks):
        pairs = [(k, PANELS * chip + k) for k in range(PANELS)]
        mine = mine + lax.ppermute(pieces[order[chip]], "col", pairs)
    moved = [across(wholes[0])]
    mine, moved[0] = lax.optimization_barrier((mine, moved[0]))
    mine = across(mine)
    panels = lax.all_gather(mine.reshape(thin, row_count), "col", axis=0, tiled=True)
    panels = panels.reshape(chunks, PANELS, thin, row_count)
    last, mine = lax.optimization_barrier((wholes[1], mine))
    moved.append(across(last))

    first, second, fixed = factor(
        order, jnp.stack([place, kept.astype(place.dtype)]).astype(jnp.int32), gathered, inverse
    )

    tiles = row_count // PANEL
    tile_ids = (side * grid_rows + row_place) * tiles + jnp.arange(tiles, dtype=jnp.int32)
    own_mask = tile_mask[:, 0] == 1
    is0, is1 = place == 0, place == 1
    keep = jnp.where(is0, False, jnp.where(is1, tile_ids == 0, True))
    use_first = jnp.where(is0, True, jnp.where(is1, tile_ids >= 1, own_mask & (tile_ids >= 1)))
    use_fixed = jnp.where(is0, False, cross_mask & (tile_ids >= jnp.where(is1, 1, 2)))
    use_second = jnp.where(is0, False, jnp.where(is1, tile_ids >= 1, own_mask & (tile_ids >= 2)))
    flags = jnp.stack([keep, use_first, use_fixed, use_second], axis=1).astype(jnp.int32).reshape(-1)
    return update(flags, moved[::-1], panels, first, second, fixed)


def solution(mesh):
    return jax.shard_map(
        local,
        mesh=mesh,
        in_specs=(
            P("col", "row", None, "subcube"),
            P("subcube", "col", "row", None, None),
            P(),
            P(None, "row", None),
            P(("subcube", "row"), "col"),
        ),
        out_specs=P(("subcube", "row"), "col"),
        check_vma=False,
    )
```

```python
import functools

import jax
import jax.numpy as jnp
from jax import lax
from jax.experimental import pallas as pl
from jax.experimental.pallas import tpu as pltpu
from jax.sharding import PartitionSpec as P

PANEL = 512
PANELS = 2
LANES = 128
BIG = 2**30
VMEM_BYTES = 56 * 2**20


def search_kernel(sections, scalars, maps_ref, places_ref, low_ref, high_ref):
    map_blocks = maps_ref.shape[1]
    at_row = 0
    for section, count in enumerate(sections):
        child = scalars[section]
        first = scalars[len(sections) + section]
        for block in range(count):
            at = jnp.minimum(scalars[2 * len(sections) + at_row + block] // LANES, map_blocks - 1)
            after = jnp.minimum(at + 1, map_blocks - 1)
            row = at_row + block
            low_ref[row : row + 1, :] = maps_ref[child, pl.ds(at, 1), :]
            high_ref[row : row + 1, :] = jnp.where(at + 1 < map_blocks, maps_ref[child, pl.ds(after, 1), :], BIG)
        low, high = low_ref[at_row : at_row + count, :], high_ref[at_row : at_row + count, :]
        lane = lax.broadcasted_iota(jnp.int32, low.shape, 1)
        block_id = lax.broadcasted_iota(jnp.int32, low.shape, 0)
        wanted = first + block_id * LANES + lane

        def pick(at):
            inner = at & (LANES - 1)
            return jnp.where(
                at < LANES, jnp.take_along_axis(low, inner, axis=1), jnp.take_along_axis(high, inner, axis=1)
            )

        place = jnp.zeros(low.shape, jnp.int32)
        width = LANES
        while width >= 1:
            place = jnp.where(pick(place + (width - 1)) < wanted, place + width, place)
            width //= 2
        places_ref[at_row : at_row + count, :] = jnp.where(pick(place) == wanted, place, -1)
        at_row += count


def search(maps, children, firsts, starts):
    sections = tuple(start.shape[0] for start in starts)
    total = sum(sections)
    scalars = jnp.concatenate([jnp.stack(children), jnp.stack(firsts)] + list(starts)).astype(jnp.int32)
    return pl.pallas_call(
        functools.partial(search_kernel, sections),
        out_shape=jax.ShapeDtypeStruct((total, LANES), jnp.int32),
        grid_spec=pltpu.PrefetchScalarGridSpec(
            num_scalar_prefetch=1,
            grid=(1,),
            in_specs=[pl.BlockSpec(maps.shape, lambda i, _: (0, 0, 0))],
            out_specs=pl.BlockSpec((total, LANES), lambda i, _: (0, 0)),
            scratch_shapes=[pltpu.VMEM((total, LANES), jnp.int32)] * 2,
        ),
        compiler_params=pltpu.CompilerParams(vmem_limit_bytes=VMEM_BYTES),
    )(scalars, maps)


def extend_kernel(first_place, map_blocks, scalars, places_ref, front_ref, source_ref, *refs):
    tail_ref, out_ref, piece_refs = (refs[0], refs[1], refs[2:]) if len(refs) > 1 else (None, refs[0], ())
    step = pl.program_id(0)
    groups, columns, width = out_ref.shape
    per_group = width // LANES
    source_blocks = source_ref.shape[1] // LANES
    offset = scalars[scalars.shape[0] - 1]
    lane = lax.broadcasted_iota(jnp.int32, (8, LANES), 1)
    for j in range(groups * per_group):
        block = step * groups * per_group + j
        start = scalars[block]
        at = jnp.minimum(start // LANES, map_blocks - 1)
        split = jnp.where(start // LANES < map_blocks, start & (LANES - 1), LANES)
        at = at - offset
        inside_low = (at >= 0) & (at < source_blocks)
        inside_high = (at + 1 >= 0) & (at + 1 < source_blocks)
        low_at = pl.multiple_of(jnp.clip(at, 0, source_blocks - 1) * LANES, LANES)
        high_at = pl.multiple_of(jnp.clip(at + 1, 0, source_blocks - 1) * LANES, LANES)
        place = jnp.broadcast_to(places_ref[pl.ds(first_place + block, 1), :], (8, LANES))
        inner = place & (LANES - 1)
        hit = ((place >= 0) & (place < LANES) & inside_low) | ((place >= LANES) & inside_high)
        from_low = lane >= split
        group = j // per_group
        here = slice(j % per_group * LANES, (j % per_group + 1) * LANES)
        for row in range(0, columns, 8):
            rows = slice(row, row + 8)
            merged = jnp.where(from_low, source_ref[rows, pl.ds(low_at, LANES)], source_ref[rows, pl.ds(high_at, LANES)])
            gained = jnp.where(hit, jnp.take_along_axis(merged, inner, axis=1), 0.0)
            if len(front_ref.shape) == 2:
                value = front_ref[rows, j * LANES : (j + 1) * LANES] + gained
            else:
                value = front_ref[group, rows, here] + gained
            out_ref[group, rows, here] = value
            if piece_refs:
                piece_refs[row // 8][group, :, here] = value
    for index, piece_ref in enumerate(piece_refs):
        rows = slice(8 * index, 8 * index + 8)
        for group in range(groups):
            lanes = pl.ds(pl.multiple_of((step * groups + group) * LANES, LANES), LANES)
            piece_ref[group, :, width:] = tail_ref[rows, lanes]


def extend_add(front, source, places, first_place, starts, offset, map_blocks, groups, width, columns=None, part=0, tail=None):
    columns = source.shape[0] if columns is None else columns
    steps = 2 if groups % 2 == 0 else 1
    per_step = groups // steps
    if front.ndim == 2:
        front_spec = pl.BlockSpec((columns, per_step * width), lambda i, _: (part, i))
    else:
        front_spec = pl.BlockSpec((per_step, columns, width), lambda i, _: (i, part, 0))
    source_part = part if source.shape[0] > columns else 0
    source_width = min(source.shape[1], map_blocks * LANES if groups > 1 else width)
    scalars = jnp.concatenate([starts, offset.reshape(1)]).astype(jnp.int32)
    whole = lambda shape, row=0: pl.BlockSpec(shape, lambda i, _: (row, 0), pipeline_mode=pl.Buffered(1))
    shapes = [(columns, width)]
    inputs, in_specs = [places, front, source], [whole(places.shape), front_spec, whole((columns, source_width), source_part)]
    if tail is not None:
        shapes += [(8, width + LANES)] * (columns // 8)
        inputs.append(tail)
        in_specs.append(whole((columns, tail.shape[1]), part))
    outs = pl.pallas_call(
        functools.partial(extend_kernel, first_place, map_blocks),
        out_shape=[jax.ShapeDtypeStruct((groups,) + shape, jnp.float32) for shape in shapes],
        grid_spec=pltpu.PrefetchScalarGridSpec(
            num_scalar_prefetch=1,
            grid=(steps,),
            in_specs=in_specs,
            out_specs=[pl.BlockSpec((per_step,) + shape, lambda i, _: (i, 0, 0)) for shape in shapes],
        ),
        compiler_params=pltpu.CompilerParams(vmem_limit_bytes=VMEM_BYTES),
    )(scalars, *inputs)
    return outs[0] if tail is None else outs


def halves(x):
    high = x.astype(jnp.bfloat16)
    return high, (x - high.astype(jnp.float32)).astype(jnp.bfloat16)


def product(left, right, dims):
    left_high, left_low = left
    right_high, right_low = right
    dot = lambda a, b: lax.dot_general(a, b, (dims, ((), ())), preferred_element_type=jnp.float32)
    return dot(left_high, right_high) + (dot(left_high, right_low) + dot(left_low, right_high))


PLAIN = ((1,), (0,))
CROSS = ((1,), (1,))


def factor_kernel(order, flags, gathered_ref, inverse_ref, corner_ref, first_ref, second_ref, fixed_ref):
    place, kept = flags[0], flags[1]
    thin = inverse_ref.shape[1]
    by_chip = lambda x: jnp.concatenate([x[:, 8 * q : 8 * q + 8].reshape(-1, x.shape[2]) for q in order])
    strip = gathered_ref[:, :thin].reshape(PANEL, 2 * PANEL)
    inverse = by_chip(inverse_ref[...])
    inverse0, inverse1 = inverse[:, :PANEL], inverse[:, PANEL:]
    halves0, halves1 = halves(inverse0), halves(inverse1)
    corner = corner_ref[...]
    corner10, corner01 = (halves(corner[:, k].reshape(PANEL, PANEL)) for k in range(PANELS))
    first = product(halves(strip[:, :PANEL]), halves0, CROSS)
    lowered = product(halves(first), corner10, PLAIN)
    pivot1 = strip[:, PANEL:] - jnp.where(kept == 1, lowered, 0.0)
    second = product(halves(pivot1), halves1, CROSS)
    second = jnp.where(place == 1, -inverse1.T, second)
    crossed = product(halves(second), corner01, PLAIN)
    fixed = product(halves(crossed), halves0, CROSS)
    first_ref[...] = jnp.where(place == 0, -inverse0.T, jnp.where(place == 1, 0.0, first))
    second_ref[...] = second
    fixed_ref[...] = fixed


def factor(order, flags, gathered, inverse, panels):
    square = jax.ShapeDtypeStruct((PANEL, PANEL), jnp.float32)
    return pl.pallas_call(
        functools.partial(factor_kernel, order),
        out_shape=(square, square, square),
        grid_spec=pltpu.PrefetchScalarGridSpec(
            num_scalar_prefetch=1,
            grid=(1,),
            in_specs=[pl.BlockSpec(x.shape, lambda i, _: (0, 0, 0)) for x in (gathered, inverse)]
            + [pl.BlockSpec(panels.shape[:3] + (PANEL,), lambda i, _: (0, 0, 0, panels.shape[3] // PANEL - 1))],
            out_specs=[pl.BlockSpec((PANEL, PANEL), lambda i, _: (0, 0))] * 3,
        ),
        compiler_params=pltpu.CompilerParams(vmem_limit_bytes=VMEM_BYTES),
    )(flags, gathered, inverse, panels)


def update_kernel(flags, *refs):
    part_refs, (panels_ref, first_ref, second_ref, fixed_ref, out_ref) = refs[:-5], refs[-5:]
    tile = pl.program_id(0)
    keep, use_first, use_fixed, use_second = (flags[4 * tile + i] == 1 for i in range(4))
    left0 = first_ref[...] - jnp.where(use_fixed, fixed_ref[...], 0.0)
    left0 = halves(jnp.where(use_first, left0, 0.0))
    left1 = halves(jnp.where(use_second, second_ref[...], 0.0))
    panel = panels_ref[...]
    right0 = halves(panel[:, 0].reshape(PANEL, PANEL))
    right1 = halves(panel[:, 1].reshape(PANEL, PANEL))
    update = product(left0, right0, PLAIN) + product(left1, right1, PLAIN)
    block = jnp.concatenate([part[...] for part in part_refs], axis=1).reshape(PANEL, PANEL)
    out_ref[...] = (jnp.where(keep, block, 0.0) - update).T


def update(flags, parts, panels, first, second, fixed):
    rows = parts[0].shape[2]
    square = pl.BlockSpec((PANEL, PANEL), lambda i, _: (0, 0))
    return pl.pallas_call(
        update_kernel,
        out_shape=jax.ShapeDtypeStruct((rows, PANEL), jnp.float32),
        grid_spec=pltpu.PrefetchScalarGridSpec(
            num_scalar_prefetch=1,
            grid=(rows // PANEL,),
            in_specs=[pl.BlockSpec(part.shape[:2] + (PANEL,), lambda i, _: (0, 0, i)) for part in parts]
            + [
                pl.BlockSpec(panels.shape[:3] + (PANEL,), lambda i, _: (0, 0, 0, i)),
                square,
                square,
                square,
            ],
            out_specs=pl.BlockSpec((PANEL, PANEL), lambda i, _: (i, 0)),
        ),
        compiler_params=pltpu.CompilerParams(vmem_limit_bytes=VMEM_BYTES),
    )(flags, *parts, panels, first, second, fixed)


def local(front_entries, child_blocks, row_maps, pivot_inverses, tile_mask):
    thin, half_rows = front_entries.shape[2:]
    child_rows = child_blocks.shape[4]
    grid_rows = lax.axis_size("row")
    side = lax.axis_index("subcube")
    row_place = lax.axis_index("row")
    place = lax.axis_index("col")
    row_count = half_rows // grid_rows
    chunks = thin // 8
    pivot_rows = PANELS * PANEL
    own = child_blocks[0, 0, 0]
    front = front_entries[0, 0]
    zero = jnp.zeros((), jnp.int32)
    exchange = lambda x: lax.ppermute(x, "subcube", [(0, 1), (1, 0)])

    inverse = lax.all_gather(jnp.concatenate([pivot_inverses[k] for k in range(PANELS)], axis=1), "row", axis=0)

    window = -(-(child_rows * 13 // 24) // LANES) * LANES
    rest = child_rows - window
    parts = [(thin // 2, thin), (0, thin // 2)]
    first_sent, last_sent = [jnp.where(side == 0, own[a:b, rest:], own[a:b, :window]) for a, b in parts]
    received = [exchange(first_sent)]
    last_sent, received[0] = lax.optimization_barrier((last_sent, received[0]))
    received.append(exchange(last_sent))

    map_blocks = child_rows // LANES
    blocks = half_rows // LANES
    strip_blocks = pivot_rows // LANES
    maps = row_maps.reshape(2, map_blocks, LANES)
    count = lambda maps, edges: jnp.sum((maps[:, None, :] < edges[None, :, None]).astype(jnp.int32), axis=2)
    edges = LANES * jnp.arange(blocks, dtype=jnp.int32)
    strip_starts = count(row_maps, edges[:strip_blocks])
    strip_places = search(maps, [zero, zero + 1], [zero, zero], [strip_starts[0], strip_starts[1]])
    strip_add = lambda base, child, t: extend_add(
        base, child, strip_places, t * strip_blocks, strip_starts[t], zero, map_blocks, 1, pivot_rows
    )[0]
    mask_rows = jnp.zeros((8, pivot_rows), jnp.float32)
    mask_rows = mask_rows.at[0, : tile_mask.shape[0]].set(tile_mask.astype(jnp.float32)[:, 0])
    prefix = own[:, :pivot_rows]
    base = strip_add(front, own, 0)
    got = exchange(jnp.concatenate([jnp.where(side == 0, base, prefix), mask_rows]))

    first_row = (side * half_rows).astype(jnp.int32)
    own_map = lax.dynamic_index_in_dim(row_maps, side, 0, keepdims=False)
    other_map = lax.dynamic_index_in_dim(row_maps, 1 - side, 0, keepdims=False)
    starts = count(jnp.stack([own_map, other_map]), first_row + edges)
    places = search(
        maps,
        [side.astype(jnp.int32), (1 - side).astype(jnp.int32)],
        [first_row, first_row],
        [starts[0], starts[1]],
    )
    lower = jnp.sum((row_maps < half_rows).astype(jnp.int32), axis=1)
    spill = (child_rows - lower[0] > window) | (lower[1] > window)
    window_at = jnp.where(side == 0, 0, rest // LANES).astype(jnp.int32)
    rest_at = jnp.where(side == 0, window // LANES, 0).astype(jnp.int32)
    add = functools.partial(extend_add, places=places, map_blocks=map_blocks, groups=grid_rows, width=row_count)
    add_other = functools.partial(add, first_place=blocks, starts=starts[1])
    base_sum = add(front, own, first_place=0, starts=starts[0], offset=zero)

    def add_rest(base_sum):
        more = exchange(jnp.where(side == 0, own[:, :rest], own[:, window:]))
        return add_other(base_sum, more, offset=rest_at)

    base_sum = lax.cond(spill, add_rest, lambda x: x, base_sum)

    got, received[0], base_sum = lax.optimization_barrier((got, received[0], base_sum))
    strip = strip_add(jnp.where(side == 0, base, got[:thin]), jnp.where(side == 0, got[:thin], prefix), 1)
    first_masks = jnp.where(side == 0, mask_rows, got[thin:])

    strip, inverse = lax.optimization_barrier((strip, inverse))
    gathered = lax.all_gather(jnp.concatenate([strip, first_masks]), "row", axis=0)
    kept = gathered[0, thin, 1] > 0.5

    corner = jnp.where(place == 0, strip[:, PANEL:], strip[:, :PANEL])
    tail = jnp.concatenate([corner, jnp.broadcast_to(mask_rows[:1, :PANEL], (thin, PANEL))], axis=1)
    wholes, pieces = [], {}
    for (a, b), part in zip(parts, received):
        size = b - a
        whole, *chunk_list = add_other(base_sum, part, offset=window_at, columns=size, part=a // size, tail=tail)
        wholes.append(whole)
        pieces.update({a // 8 + i: chunk for i, chunk in enumerate(chunk_list)})

    across = lambda x: lax.all_to_all(x, "row", split_axis=0, concat_axis=0, tiled=True)
    order = [0, 1] + list(range(chunks // 2, chunks)) + list(range(2, chunks // 2))
    mine = jnp.where(place // PANELS == 0, pieces[order[0]], 0.0)
    for chip in range(1, chunks):
        pairs = [(k, PANELS * chip + k) for k in range(PANELS)]
        mine = mine + lax.ppermute(pieces[order[chip]], "col", pairs)
    tails = mine[:, :, row_count:]
    core0 = place % PANELS == 0
    masks_there = lax.ppermute(tails[PANEL // LANES], "col", [(c, c ^ 1) for c in range(lax.axis_size("col"))])
    cross_mask = jnp.where(core0, masks_there, tails[PANEL // LANES])[0, : tile_mask.shape[0]] > 0.5
    corner = tails[: PANEL // LANES].transpose(1, 0, 2).reshape(1, 8, PANEL)
    mine = jnp.concatenate([mine[:, :, :row_count], jnp.broadcast_to(corner, (grid_rows, 8, PANEL))], axis=2)
    moved = [across(wholes[0])]
    mine, moved[0] = lax.optimization_barrier((mine, moved[0]))
    mine = across(mine)
    panels = lax.all_gather(mine.reshape(thin, -1), "col", axis=0, tiled=True)
    panels = panels.reshape(chunks, PANELS, thin, -1)
    last, mine = lax.optimization_barrier((wholes[1], mine))
    moved.append(across(last))

    first, second, fixed = factor(
        order, jnp.stack([place, kept.astype(place.dtype)]).astype(jnp.int32), gathered, inverse, panels
    )

    tiles = row_count // PANEL
    tile_ids = (side * grid_rows + row_place) * tiles + jnp.arange(tiles, dtype=jnp.int32)
    own_mask = tile_mask[:, 0] == 1
    is0, is1 = place == 0, place == 1
    keep = jnp.where(is0, False, jnp.where(is1, tile_ids == 0, True))
    use_first = jnp.where(is0, True, jnp.where(is1, tile_ids >= 1, own_mask & (tile_ids >= 1)))
    use_fixed = jnp.where(is0, False, cross_mask & (tile_ids >= jnp.where(is1, 1, 2)))
    use_second = jnp.where(is0, False, jnp.where(is1, tile_ids >= 1, own_mask & (tile_ids >= 2)))
    flags = jnp.stack([keep, use_first, use_fixed, use_second], axis=1).astype(jnp.int32).reshape(-1)
    return update(flags, moved[::-1], panels, first, second, fixed)


def solution(mesh):
    return jax.shard_map(
        local,
        mesh=mesh,
        in_specs=(
            P("col", "row", None, "subcube"),
            P("subcube", "col", "row", None, None),
            P(),
            P(None, "row", None),
            P(("subcube", "row"), "col"),
        ),
        out_specs=P(("subcube", "row"), "col"),
        check_vma=False,
    )
```

```python
import functools

import jax
import jax.numpy as jnp
from jax import lax
from jax.experimental import pallas as pl
from jax.experimental.pallas import tpu as pltpu
from jax.sharding import PartitionSpec as P

PANEL = 512
PANELS = 2
LANES = 128
BIG = 2**30
VMEM_BYTES = 56 * 2**20


def search_kernel(sections, scalars, maps_ref, places_ref, low_ref, high_ref):
    map_blocks = maps_ref.shape[1]
    at_row = 0
    for section, count in enumerate(sections):
        child = scalars[section]
        first = scalars[len(sections) + section]
        for block in range(count):
            at = jnp.minimum(scalars[2 * len(sections) + at_row + block] // LANES, map_blocks - 1)
            after = jnp.minimum(at + 1, map_blocks - 1)
            row = at_row + block
            low_ref[row : row + 1, :] = maps_ref[child, pl.ds(at, 1), :]
            high_ref[row : row + 1, :] = jnp.where(at + 1 < map_blocks, maps_ref[child, pl.ds(after, 1), :], BIG)
        low, high = low_ref[at_row : at_row + count, :], high_ref[at_row : at_row + count, :]
        lane = lax.broadcasted_iota(jnp.int32, low.shape, 1)
        block_id = lax.broadcasted_iota(jnp.int32, low.shape, 0)
        wanted = first + block_id * LANES + lane

        def pick(at):
            inner = at & (LANES - 1)
            return jnp.where(
                at < LANES, jnp.take_along_axis(low, inner, axis=1), jnp.take_along_axis(high, inner, axis=1)
            )

        place = jnp.zeros(low.shape, jnp.int32)
        width = LANES
        while width >= 1:
            place = jnp.where(pick(place + (width - 1)) < wanted, place + width, place)
            width //= 2
        places_ref[at_row : at_row + count, :] = jnp.where(pick(place) == wanted, place, -1)
        at_row += count


def search(maps, children, firsts, starts):
    sections = tuple(start.shape[0] for start in starts)
    total = sum(sections)
    scalars = jnp.concatenate([jnp.stack(children), jnp.stack(firsts)] + list(starts)).astype(jnp.int32)
    return pl.pallas_call(
        functools.partial(search_kernel, sections),
        out_shape=jax.ShapeDtypeStruct((total, LANES), jnp.int32),
        grid_spec=pltpu.PrefetchScalarGridSpec(
            num_scalar_prefetch=1,
            grid=(1,),
            in_specs=[pl.BlockSpec(maps.shape, lambda i, _: (0, 0, 0))],
            out_specs=pl.BlockSpec((total, LANES), lambda i, _: (0, 0)),
            scratch_shapes=[pltpu.VMEM((total, LANES), jnp.int32)] * 2,
        ),
        compiler_params=pltpu.CompilerParams(vmem_limit_bytes=VMEM_BYTES),
    )(scalars, maps)


def extend_kernel(first_place, map_blocks, scalars, places_ref, front_ref, source_ref, *refs):
    tail_ref, out_ref, piece_refs = (refs[0], refs[1], refs[2:]) if len(refs) > 1 else (None, refs[0], ())
    step = pl.program_id(0)
    groups, columns, width = out_ref.shape
    per_group = width // LANES
    source_blocks = source_ref.shape[1] // LANES
    offset = scalars[scalars.shape[0] - 1]
    lane = lax.broadcasted_iota(jnp.int32, (8, LANES), 1)
    for j in range(groups * per_group):
        block = step * groups * per_group + j
        start = scalars[block]
        at = jnp.minimum(start // LANES, map_blocks - 1)
        split = jnp.where(start // LANES < map_blocks, start & (LANES - 1), LANES)
        at = at - offset
        inside_low = (at >= 0) & (at < source_blocks)
        inside_high = (at + 1 >= 0) & (at + 1 < source_blocks)
        low_at = pl.multiple_of(jnp.clip(at, 0, source_blocks - 1) * LANES, LANES)
        high_at = pl.multiple_of(jnp.clip(at + 1, 0, source_blocks - 1) * LANES, LANES)
        place = jnp.broadcast_to(places_ref[pl.ds(first_place + block, 1), :], (8, LANES))
        inner = place & (LANES - 1)
        hit = ((place >= 0) & (place < LANES) & inside_low) | ((place >= LANES) & inside_high)
        from_low = lane >= split
        group = j // per_group
        here = slice(j % per_group * LANES, (j % per_group + 1) * LANES)
        for row in range(0, columns, 8):
            rows = slice(row, row + 8)
            merged = jnp.where(from_low, source_ref[rows, pl.ds(low_at, LANES)], source_ref[rows, pl.ds(high_at, LANES)])
            gained = jnp.where(hit, jnp.take_along_axis(merged, inner, axis=1), 0.0)
            if len(front_ref.shape) == 2:
                value = front_ref[rows, j * LANES : (j + 1) * LANES] + gained
            else:
                value = front_ref[group, rows, here] + gained
            out_ref[group, rows, here] = value
            if piece_refs:
                piece_refs[row // 8][group, :, here] = value
    for index, piece_ref in enumerate(piece_refs):
        rows = slice(8 * index, 8 * index + 8)
        for group in range(groups):
            lanes = pl.ds(pl.multiple_of((step * groups + group) * LANES, LANES), LANES)
            piece_ref[group, :, width:] = tail_ref[rows, lanes]


def extend_add(front, source, places, first_place, starts, offset, map_blocks, groups, width, columns=None, part=0, tail=None):
    columns = source.shape[0] if columns is None else columns
    steps = 2 if groups % 2 == 0 else 1
    per_step = groups // steps
    if front.ndim == 2:
        front_spec = pl.BlockSpec((columns, per_step * width), lambda i, _: (part, i))
    else:
        front_spec = pl.BlockSpec((per_step, columns, width), lambda i, _: (i, part, 0))
    source_part = part if source.shape[0] > columns else 0
    source_width = min(source.shape[1], map_blocks * LANES if groups > 1 else width)
    scalars = jnp.concatenate([starts, offset.reshape(1)]).astype(jnp.int32)
    whole = lambda shape, row=0: pl.BlockSpec(shape, lambda i, _: (row, 0), pipeline_mode=pl.Buffered(1))
    shapes = [(columns, width)]
    inputs, in_specs = [places, front, source], [whole(places.shape), front_spec, whole((columns, source_width), source_part)]
    if tail is not None:
        shapes += [(8, width + LANES)] * (columns // 8)
        inputs.append(tail)
        in_specs.append(whole((columns, tail.shape[1]), part))
    outs = pl.pallas_call(
        functools.partial(extend_kernel, first_place, map_blocks),
        out_shape=[jax.ShapeDtypeStruct((groups,) + shape, jnp.float32) for shape in shapes],
        grid_spec=pltpu.PrefetchScalarGridSpec(
            num_scalar_prefetch=1,
            grid=(steps,),
            in_specs=in_specs,
            out_specs=[pl.BlockSpec((per_step,) + shape, lambda i, _: (i, 0, 0)) for shape in shapes],
        ),
        compiler_params=pltpu.CompilerParams(vmem_limit_bytes=VMEM_BYTES),
    )(scalars, *inputs)
    return outs[0] if tail is None else outs


def halves(x):
    high = x.astype(jnp.bfloat16)
    return high, (x - high.astype(jnp.float32)).astype(jnp.bfloat16)


def product(left, right, dims):
    left_high, left_low = left
    right_high, right_low = right
    dot = lambda a, b: lax.dot_general(a, b, (dims, ((), ())), preferred_element_type=jnp.float32)
    return dot(left_high, right_high) + (dot(left_high, right_low) + dot(left_low, right_high))


PLAIN = ((1,), (0,))
CROSS = ((1,), (1,))


def factor_kernel(order, flags, gathered_ref, inverse_ref, corner_ref, first_ref, second_ref, fixed_ref):
    place, kept = flags[0], flags[1]
    thin = inverse_ref.shape[2]
    by_chip = lambda x: jnp.concatenate([x[:, 8 * q : 8 * q + 8].reshape(-1, x.shape[2]) for q in order])
    strip = gathered_ref[:, :thin].reshape(PANEL, 2 * PANEL)
    inverse0, inverse1 = (by_chip(inverse_ref[:, k]) for k in range(PANELS))
    halves0, halves1 = halves(inverse0), halves(inverse1)
    corner = corner_ref[...]
    corner10, corner01 = (halves(corner[:, k].reshape(PANEL, PANEL)) for k in range(PANELS))
    first = product(halves(strip[:, :PANEL]), halves0, CROSS)
    lowered = product(halves(first), corner10, PLAIN)
    pivot1 = strip[:, PANEL:] - jnp.where(kept == 1, lowered, 0.0)
    second = product(halves(pivot1), halves1, CROSS)
    second = jnp.where(place == 1, -inverse1.T, second)
    crossed = product(halves(second), corner01, PLAIN)
    fixed = product(halves(crossed), halves0, CROSS)
    first_ref[...] = jnp.where(place == 0, -inverse0.T, jnp.where(place == 1, 0.0, first))
    second_ref[...] = second
    fixed_ref[...] = fixed


def factor(order, flags, gathered, inverse, panels):
    square = jax.ShapeDtypeStruct((PANEL, PANEL), jnp.float32)
    return pl.pallas_call(
        functools.partial(factor_kernel, order),
        out_shape=(square, square, square),
        grid_spec=pltpu.PrefetchScalarGridSpec(
            num_scalar_prefetch=1,
            grid=(1,),
            in_specs=[
                pl.BlockSpec(gathered.shape, lambda i, _: (0, 0, 0)),
                pl.BlockSpec(inverse.shape, lambda i, _: (0, 0, 0, 0)),
            ]
            + [pl.BlockSpec(panels.shape[:3] + (PANEL,), lambda i, _: (0, 0, 0, panels.shape[3] // PANEL - 1))],
            out_specs=[pl.BlockSpec((PANEL, PANEL), lambda i, _: (0, 0))] * 3,
        ),
        compiler_params=pltpu.CompilerParams(vmem_limit_bytes=VMEM_BYTES),
    )(flags, gathered, inverse, panels)


def update_kernel(first_tile, flags, *refs):
    part_refs, (panels_ref, first_ref, second_ref, fixed_ref), out_ref = refs[:2], refs[2:6], refs[-1]
    tile = first_tile + pl.program_id(0)
    keep, use_first, use_fixed, use_second = (flags[4 * tile + i] == 1 for i in range(4))
    left0 = first_ref[...] - jnp.where(use_fixed, fixed_ref[...], 0.0)
    left0 = halves(jnp.where(use_first, left0, 0.0))
    left1 = halves(jnp.where(use_second, second_ref[...], 0.0))
    panel = panels_ref[...]
    right0 = halves(panel[:, 0].reshape(PANEL, PANEL))
    right1 = halves(panel[:, 1].reshape(PANEL, PANEL))
    update = product(left0, right0, PLAIN) + product(left1, right1, PLAIN)
    block = jnp.concatenate([part[...] for part in part_refs], axis=1).reshape(PANEL, PANEL)
    out_ref[...] = (jnp.where(keep, block, 0.0) - update).T


def update(flags, parts, panels, squares, first_tile, tiles, earlier=None):
    rows = parts[0].shape[2]
    square = pl.BlockSpec((PANEL, PANEL), lambda i, _: (0, 0))
    inputs = [*parts, panels, *squares]
    in_specs = [pl.BlockSpec(part.shape[:2] + (PANEL,), lambda i, _: (0, 0, first_tile + i)) for part in parts]
    in_specs += [pl.BlockSpec(panels.shape[:3] + (PANEL,), lambda i, _: (0, 0, 0, i)), square, square, square]
    aliases = {}
    if earlier is not None:
        inputs.append(earlier)
        in_specs.append(pl.BlockSpec(memory_space=pl.ANY))
        aliases = {len(inputs): 0}
    return pl.pallas_call(
        functools.partial(update_kernel, first_tile),
        out_shape=jax.ShapeDtypeStruct((rows, PANEL), jnp.float32),
        grid_spec=pltpu.PrefetchScalarGridSpec(
            num_scalar_prefetch=1,
            grid=(tiles,),
            in_specs=in_specs,
            out_specs=pl.BlockSpec((PANEL, PANEL), lambda i, _: (first_tile + i, 0)),
        ),
        input_output_aliases=aliases,
        compiler_params=pltpu.CompilerParams(vmem_limit_bytes=VMEM_BYTES),
    )(flags, *inputs)


def local(front_entries, child_blocks, row_maps, pivot_inverses, tile_mask):
    thin, half_rows = front_entries.shape[2:]
    child_rows = child_blocks.shape[4]
    grid_rows = lax.axis_size("row")
    side = lax.axis_index("subcube")
    row_place = lax.axis_index("row")
    place = lax.axis_index("col")
    row_count = half_rows // grid_rows
    chunks = thin // 8
    pivot_rows = PANELS * PANEL
    own = child_blocks[0, 0, 0]
    front = front_entries[0, 0]
    zero = jnp.zeros((), jnp.int32)
    exchange = lambda x: lax.ppermute(x, "subcube", [(0, 1), (1, 0)])

    inverse = lax.all_gather(pivot_inverses, "row", axis=0)

    window = -(-(child_rows * 13 // 24) // LANES) * LANES
    rest = child_rows - window
    parts = [(thin // 2, thin), (0, thin // 2)]
    first_sent, last_sent = [jnp.where(side == 0, own[a:b, rest:], own[a:b, :window]) for a, b in parts]
    received = [exchange(first_sent)]

    map_blocks = child_rows // LANES
    blocks = half_rows // LANES
    strip_blocks = pivot_rows // LANES
    maps = row_maps.reshape(2, map_blocks, LANES)
    count = lambda maps, edges: jnp.sum((maps[:, None, :] < edges[None, :, None]).astype(jnp.int32), axis=2)
    edges = LANES * jnp.arange(blocks, dtype=jnp.int32)
    strip_starts = count(row_maps, edges[:strip_blocks])
    strip_places = search(maps, [zero, zero + 1], [zero, zero], [strip_starts[0], strip_starts[1]])
    strip_add = lambda base, child, t: extend_add(
        base, child, strip_places, t * strip_blocks, strip_starts[t], zero, map_blocks, 1, pivot_rows
    )[0]
    mask_rows = jnp.zeros((8, pivot_rows), jnp.float32)
    mask_rows = mask_rows.at[0, : tile_mask.shape[0]].set(tile_mask.astype(jnp.float32)[:, 0])
    prefix = own[:, :pivot_rows]
    base = strip_add(front, own, 0)
    got = exchange(jnp.concatenate([jnp.where(side == 0, base, prefix), mask_rows]))

    first_row = (side * half_rows).astype(jnp.int32)
    own_map = lax.dynamic_index_in_dim(row_maps, side, 0, keepdims=False)
    other_map = lax.dynamic_index_in_dim(row_maps, 1 - side, 0, keepdims=False)
    starts = count(jnp.stack([own_map, other_map]), first_row + edges)
    places = search(
        maps,
        [side.astype(jnp.int32), (1 - side).astype(jnp.int32)],
        [first_row, first_row],
        [starts[0], starts[1]],
    )
    lower = jnp.sum((row_maps < half_rows).astype(jnp.int32), axis=1)
    spill = (child_rows - lower[0] > window) | (lower[1] > window)
    window_at = jnp.where(side == 0, 0, rest // LANES).astype(jnp.int32)
    rest_at = jnp.where(side == 0, window // LANES, 0).astype(jnp.int32)
    add = functools.partial(extend_add, places=places, map_blocks=map_blocks, groups=grid_rows, width=row_count)
    add_other = functools.partial(add, first_place=blocks, starts=starts[1])
    base_sum = add(front, own, first_place=0, starts=starts[0], offset=zero)

    def add_rest(base_sum):
        more = exchange(jnp.where(side == 0, own[:, :rest], own[:, window:]))
        return add_other(base_sum, more, offset=rest_at)

    base_sum = lax.cond(spill, add_rest, lambda x: x, base_sum)

    got, received[0], base_sum, last_sent = lax.optimization_barrier((got, received[0], base_sum, last_sent))
    received.append(exchange(last_sent))
    strip = strip_add(jnp.where(side == 0, base, got[:thin]), jnp.where(side == 0, got[:thin], prefix), 1)
    first_masks = jnp.where(side == 0, mask_rows, got[thin:])

    corner = jnp.where(place == 0, strip[:, PANEL:], strip[:, :PANEL])
    tail = jnp.concatenate([corner, jnp.broadcast_to(mask_rows[:1, :PANEL], (thin, PANEL))], axis=1)
    wholes, pieces = [], {}

    def assemble(index):
        a, b = parts[index]
        size = b - a
        whole, *chunk_list = add_other(
            base_sum, received[index], offset=window_at, columns=size, part=a // size, tail=tail
        )
        wholes.append(whole)
        pieces.update({a // 8 + i: chunk for i, chunk in enumerate(chunk_list)})

    assemble(0)
    to_gather = jnp.concatenate([strip, first_masks])
    to_gather, inverse, received[1], wholes[0] = lax.optimization_barrier(
        (to_gather, inverse, received[1], wholes[0])
    )
    gathered = lax.all_gather(to_gather, "row", axis=0)
    kept = gathered[0, thin, 1] > 0.5

    assemble(1)

    across = lambda x: lax.all_to_all(x, "row", split_axis=0, concat_axis=0, tiled=True)
    order = [0, 1] + list(range(chunks // 2, chunks)) + list(range(2, chunks // 2))
    mine = jnp.where(place // PANELS == 0, pieces[order[0]], 0.0)
    for chip in range(1, chunks):
        pairs = [(k, PANELS * chip + k) for k in range(PANELS)]
        mine = mine + lax.ppermute(pieces[order[chip]], "col", pairs)
    tails = mine[:, :, row_count:]
    core0 = place % PANELS == 0
    masks_there = lax.ppermute(tails[PANEL // LANES], "col", [(c, c ^ 1) for c in range(lax.axis_size("col"))])
    cross_mask = jnp.where(core0, masks_there, tails[PANEL // LANES])[0, : tile_mask.shape[0]] > 0.5
    corner = tails[: PANEL // LANES].transpose(1, 0, 2).reshape(1, 8, PANEL)
    corner = jnp.broadcast_to(corner, (grid_rows, 8, PANEL))
    cut = row_count - PANEL
    mine = jnp.concatenate([mine[:, :, :cut], corner, mine[:, :, cut:row_count]], axis=2)
    moved = [across(wholes[0])]
    mine, moved[0] = lax.optimization_barrier((mine, moved[0]))
    mine = across(mine)
    mine_flat = mine.reshape(thin, -1)
    gather_panels = lambda x: lax.all_gather(x, "col", axis=0, tiled=True).reshape(chunks, PANELS, thin, -1)
    panels = gather_panels(mine_flat[:, :row_count])
    last_panels = gather_panels(mine_flat[:, row_count:])
    last, mine = lax.optimization_barrier((wholes[1], mine))
    moved.append(across(last))

    first, second, fixed = factor(
        order, jnp.stack([place, kept.astype(place.dtype)]).astype(jnp.int32), gathered, inverse, panels
    )

    tiles = row_count // PANEL
    tile_ids = (side * grid_rows + row_place) * tiles + jnp.arange(tiles, dtype=jnp.int32)
    own_mask = tile_mask[:, 0] == 1
    is0, is1 = place == 0, place == 1
    keep = jnp.where(is0, False, jnp.where(is1, tile_ids == 0, True))
    use_first = jnp.where(is0, True, jnp.where(is1, tile_ids >= 1, own_mask & (tile_ids >= 1)))
    use_fixed = jnp.where(is0, False, cross_mask & (tile_ids >= jnp.where(is1, 1, 2)))
    use_second = jnp.where(is0, False, jnp.where(is1, tile_ids >= 1, own_mask & (tile_ids >= 2)))
    flags = jnp.stack([keep, use_first, use_fixed, use_second], axis=1).astype(jnp.int32).reshape(-1)
    squares = [first, second, fixed]
    begun = update(flags, moved[::-1], panels, squares, 0, tiles - 1)
    return update(flags, moved[::-1], last_panels, squares, tiles - 1, 1, begun)


def solution(mesh):
    return jax.shard_map(
        local,
        mesh=mesh,
        in_specs=(
            P("col", "row", None, "subcube"),
            P("subcube", "col", "row", None, None),
            P(),
            P(None, "row", None),
            P(("subcube", "row"), "col"),
        ),
        out_specs=P(("subcube", "row"), "col"),
        check_vma=False,
    )
```

```python
import functools

import jax
import jax.numpy as jnp
from jax import lax
from jax.experimental import pallas as pl
from jax.experimental.pallas import tpu as pltpu
from jax.sharding import PartitionSpec as P

PANEL = 512
PANELS = 2
LANES = 128
BIG = 2**30
VMEM_BYTES = 56 * 2**20


def search_kernel(sections, scalars, maps_ref, places_ref, low_ref, high_ref):
    map_blocks = maps_ref.shape[1]
    at_row = 0
    for section, count in enumerate(sections):
        child = scalars[section]
        first = scalars[len(sections) + section]
        for block in range(count):
            at = jnp.minimum(scalars[2 * len(sections) + at_row + block] // LANES, map_blocks - 1)
            after = jnp.minimum(at + 1, map_blocks - 1)
            row = at_row + block
            low_ref[row : row + 1, :] = maps_ref[child, pl.ds(at, 1), :]
            high_ref[row : row + 1, :] = jnp.where(at + 1 < map_blocks, maps_ref[child, pl.ds(after, 1), :], BIG)
        low, high = low_ref[at_row : at_row + count, :], high_ref[at_row : at_row + count, :]
        lane = lax.broadcasted_iota(jnp.int32, low.shape, 1)
        block_id = lax.broadcasted_iota(jnp.int32, low.shape, 0)
        wanted = first + block_id * LANES + lane

        def pick(at):
            inner = at & (LANES - 1)
            return jnp.where(
                at < LANES, jnp.take_along_axis(low, inner, axis=1), jnp.take_along_axis(high, inner, axis=1)
            )

        place = jnp.zeros(low.shape, jnp.int32)
        width = LANES
        while width >= 1:
            place = jnp.where(pick(place + (width - 1)) < wanted, place + width, place)
            width //= 2
        places_ref[at_row : at_row + count, :] = jnp.where(pick(place) == wanted, place, -1)
        at_row += count


def search(maps, children, firsts, starts):
    sections = tuple(start.shape[0] for start in starts)
    total = sum(sections)
    scalars = jnp.concatenate([jnp.stack(children), jnp.stack(firsts)] + list(starts)).astype(jnp.int32)
    return pl.pallas_call(
        functools.partial(search_kernel, sections),
        out_shape=jax.ShapeDtypeStruct((total, LANES), jnp.int32),
        grid_spec=pltpu.PrefetchScalarGridSpec(
            num_scalar_prefetch=1,
            grid=(1,),
            in_specs=[pl.BlockSpec(maps.shape, lambda i, _: (0, 0, 0))],
            out_specs=pl.BlockSpec((total, LANES), lambda i, _: (0, 0)),
            scratch_shapes=[pltpu.VMEM((total, LANES), jnp.int32)] * 2,
        ),
        compiler_params=pltpu.CompilerParams(vmem_limit_bytes=VMEM_BYTES),
    )(scalars, maps)


def extend_kernel(first_place, map_blocks, scalars, places_ref, front_ref, source_ref, *refs):
    tail_ref, out_ref, piece_refs = (refs[0], refs[1], refs[2:]) if len(refs) > 1 else (None, refs[0], ())
    step = pl.program_id(0)
    groups, columns, width = out_ref.shape
    per_group = width // LANES
    source_blocks = source_ref.shape[1] // LANES
    offset = scalars[scalars.shape[0] - 1]
    lane = lax.broadcasted_iota(jnp.int32, (8, LANES), 1)
    for j in range(groups * per_group):
        block = step * groups * per_group + j
        start = scalars[block]
        at = jnp.minimum(start // LANES, map_blocks - 1)
        split = jnp.where(start // LANES < map_blocks, start & (LANES - 1), LANES)
        at = at - offset
        inside_low = (at >= 0) & (at < source_blocks)
        inside_high = (at + 1 >= 0) & (at + 1 < source_blocks)
        low_at = pl.multiple_of(jnp.clip(at, 0, source_blocks - 1) * LANES, LANES)
        high_at = pl.multiple_of(jnp.clip(at + 1, 0, source_blocks - 1) * LANES, LANES)
        place = jnp.broadcast_to(places_ref[pl.ds(first_place + block, 1), :], (8, LANES))
        inner = place & (LANES - 1)
        hit = ((place >= 0) & (place < LANES) & inside_low) | ((place >= LANES) & inside_high)
        from_low = lane >= split
        group = j // per_group
        here = slice(j % per_group * LANES, (j % per_group + 1) * LANES)
        for row in range(0, columns, 8):
            rows = slice(row, row + 8)
            merged = jnp.where(from_low, source_ref[rows, pl.ds(low_at, LANES)], source_ref[rows, pl.ds(high_at, LANES)])
            gained = jnp.where(hit, jnp.take_along_axis(merged, inner, axis=1), 0.0)
            if len(front_ref.shape) == 2:
                value = front_ref[rows, j * LANES : (j + 1) * LANES] + gained
            else:
                value = front_ref[group, rows, here] + gained
            out_ref[group, rows, here] = value
            if piece_refs:
                piece_refs[row // 8][group, :, here] = value
    for index, piece_ref in enumerate(piece_refs):
        rows = slice(8 * index, 8 * index + 8)
        for group in range(groups):
            lanes = pl.ds(pl.multiple_of((step * groups + group) * LANES, LANES), LANES)
            piece_ref[group, :, width:] = tail_ref[rows, lanes]


def extend_add(front, source, places, first_place, starts, offset, map_blocks, groups, width, columns=None, part=0, tail=None):
    columns = source.shape[0] if columns is None else columns
    steps = 2 if groups % 2 == 0 else 1
    per_step = groups // steps
    if front.ndim == 2:
        front_spec = pl.BlockSpec((columns, per_step * width), lambda i, _: (part, i))
    else:
        front_spec = pl.BlockSpec((per_step, columns, width), lambda i, _: (i, part, 0))
    source_part = part if source.shape[0] > columns else 0
    source_width = min(source.shape[1], map_blocks * LANES if groups > 1 else width)
    scalars = jnp.concatenate([starts, offset.reshape(1)]).astype(jnp.int32)
    whole = lambda shape, row=0: pl.BlockSpec(shape, lambda i, _: (row, 0), pipeline_mode=pl.Buffered(1))
    shapes = [(columns, width)]
    inputs, in_specs = [places, front, source], [whole(places.shape), front_spec, whole((columns, source_width), source_part)]
    if tail is not None:
        shapes += [(8, width + LANES)] * (columns // 8)
        inputs.append(tail)
        in_specs.append(whole((columns, tail.shape[1]), part))
    outs = pl.pallas_call(
        functools.partial(extend_kernel, first_place, map_blocks),
        out_shape=[jax.ShapeDtypeStruct((groups,) + shape, jnp.float32) for shape in shapes],
        grid_spec=pltpu.PrefetchScalarGridSpec(
            num_scalar_prefetch=1,
            grid=(steps,),
            in_specs=in_specs,
            out_specs=[pl.BlockSpec((per_step,) + shape, lambda i, _: (i, 0, 0)) for shape in shapes],
        ),
        compiler_params=pltpu.CompilerParams(vmem_limit_bytes=VMEM_BYTES),
    )(scalars, *inputs)
    return outs[0] if tail is None else outs


def halves(x):
    high = x.astype(jnp.bfloat16)
    return high, (x - high.astype(jnp.float32)).astype(jnp.bfloat16)


def product(left, right, dims):
    left_high, left_low = left
    right_high, right_low = right
    dot = lambda a, b: lax.dot_general(a, b, (dims, ((), ())), preferred_element_type=jnp.float32)
    return dot(left_high, right_high) + (dot(left_high, right_low) + dot(left_low, right_high))


PLAIN = ((1,), (0,))
CROSS = ((1,), (1,))


def factor_kernel(order, flags, gathered_ref, inverse_ref, corner_ref, first_ref, second_ref, fixed_ref):
    place, kept = flags[0], flags[1]
    thin = inverse_ref.shape[2]
    by_chip = lambda x: jnp.concatenate([x[:, 8 * q : 8 * q + 8].reshape(-1, x.shape[2]) for q in order])
    strip = gathered_ref[:, :thin].reshape(PANEL, 2 * PANEL)
    inverse0, inverse1 = (by_chip(inverse_ref[:, k]) for k in range(PANELS))
    halves0, halves1 = halves(inverse0), halves(inverse1)
    corner = corner_ref[...]
    corner10, corner01 = (halves(corner[:, k].reshape(PANEL, PANEL)) for k in range(PANELS))
    first = product(halves(strip[:, :PANEL]), halves0, CROSS)
    lowered = product(halves(first), corner10, PLAIN)
    pivot1 = strip[:, PANEL:] - jnp.where(kept == 1, lowered, 0.0)
    second = product(halves(pivot1), halves1, CROSS)
    second = jnp.where(place == 1, -inverse1.T, second)
    crossed = product(halves(second), corner01, PLAIN)
    fixed = product(halves(crossed), halves0, CROSS)
    first_ref[...] = jnp.where(place == 0, -inverse0.T, jnp.where(place == 1, 0.0, first))
    second_ref[...] = second
    fixed_ref[...] = fixed


def factor(order, flags, gathered, inverse, panels):
    square = jax.ShapeDtypeStruct((PANEL, PANEL), jnp.float32)
    return pl.pallas_call(
        functools.partial(factor_kernel, order),
        out_shape=(square, square, square),
        grid_spec=pltpu.PrefetchScalarGridSpec(
            num_scalar_prefetch=1,
            grid=(1,),
            in_specs=[
                pl.BlockSpec(gathered.shape, lambda i, _: (0, 0, 0)),
                pl.BlockSpec(inverse.shape, lambda i, _: (0, 0, 0, 0)),
            ]
            + [pl.BlockSpec(panels.shape[:3] + (PANEL,), lambda i, _: (0, 0, 0, panels.shape[3] // PANEL - 1))],
            out_specs=[pl.BlockSpec((PANEL, PANEL), lambda i, _: (0, 0))] * 3,
        ),
        compiler_params=pltpu.CompilerParams(vmem_limit_bytes=VMEM_BYTES),
    )(flags, gathered, inverse, panels)


def update_kernel(flags, *refs):
    part_refs, (panels_ref, first_ref, second_ref, fixed_ref, out_ref) = refs[:-5], refs[-5:]
    tile = pl.program_id(0)
    keep, use_first, use_fixed, use_second = (flags[4 * tile + i] == 1 for i in range(4))
    left0 = first_ref[...] - jnp.where(use_fixed, fixed_ref[...], 0.0)
    left0 = halves(jnp.where(use_first, left0, 0.0))
    left1 = halves(jnp.where(use_second, second_ref[...], 0.0))
    panel = panels_ref[...]
    right0 = halves(panel[:, 0].reshape(PANEL, PANEL))
    right1 = halves(panel[:, 1].reshape(PANEL, PANEL))
    update = product(left0, right0, PLAIN) + product(left1, right1, PLAIN)
    block = jnp.concatenate([part[...] for part in part_refs], axis=1).reshape(PANEL, PANEL)
    out_ref[...] = (jnp.where(keep, block, 0.0) - update).T


def update(flags, parts, panels, first, second, fixed):
    rows = parts[0].shape[2]
    square = pl.BlockSpec((PANEL, PANEL), lambda i, _: (0, 0))
    return pl.pallas_call(
        update_kernel,
        out_shape=jax.ShapeDtypeStruct((rows, PANEL), jnp.float32),
        grid_spec=pltpu.PrefetchScalarGridSpec(
            num_scalar_prefetch=1,
            grid=(rows // PANEL,),
            in_specs=[pl.BlockSpec(part.shape[:2] + (PANEL,), lambda i, _: (0, 0, i)) for part in parts]
            + [
                pl.BlockSpec(panels.shape[:3] + (PANEL,), lambda i, _: (0, 0, 0, i)),
                square,
                square,
                square,
            ],
            out_specs=pl.BlockSpec((PANEL, PANEL), lambda i, _: (i, 0)),
        ),
        compiler_params=pltpu.CompilerParams(vmem_limit_bytes=VMEM_BYTES),
    )(flags, *parts, panels, first, second, fixed)


def local(front_entries, child_blocks, row_maps, pivot_inverses, tile_mask):
    thin, half_rows = front_entries.shape[2:]
    child_rows = child_blocks.shape[4]
    grid_rows = lax.axis_size("row")
    side = lax.axis_index("subcube")
    row_place = lax.axis_index("row")
    place = lax.axis_index("col")
    row_count = half_rows // grid_rows
    chunks = thin // 8
    pivot_rows = PANELS * PANEL
    own = child_blocks[0, 0, 0]
    front = front_entries[0, 0]
    zero = jnp.zeros((), jnp.int32)
    exchange = lambda x: lax.ppermute(x, "subcube", [(0, 1), (1, 0)])

    inverse = lax.all_gather(pivot_inverses, "row", axis=0)

    window = -(-(child_rows * 13 // 24) // LANES) * LANES
    rest = child_rows - window
    share = thin // 4
    parts = [(thin - share, thin), (0, thin - share)]
    first_sent, last_sent = [jnp.where(side == 0, own[a:b, rest:], own[a:b, :window]) for a, b in parts]
    received = [exchange(first_sent)]

    map_blocks = child_rows // LANES
    blocks = half_rows // LANES
    strip_blocks = pivot_rows // LANES
    maps = row_maps.reshape(2, map_blocks, LANES)
    count = lambda maps, edges: jnp.sum((maps[:, None, :] < edges[None, :, None]).astype(jnp.int32), axis=2)
    edges = LANES * jnp.arange(blocks, dtype=jnp.int32)
    strip_starts = count(row_maps, edges[:strip_blocks])
    strip_places = search(maps, [zero, zero + 1], [zero, zero], [strip_starts[0], strip_starts[1]])
    strip_add = lambda base, child, t: extend_add(
        base, child, strip_places, t * strip_blocks, strip_starts[t], zero, map_blocks, 1, pivot_rows
    )[0]
    mask_rows = jnp.zeros((8, pivot_rows), jnp.float32)
    mask_rows = mask_rows.at[0, : tile_mask.shape[0]].set(tile_mask.astype(jnp.float32)[:, 0])
    prefix = own[:, :pivot_rows]
    base = strip_add(front, own, 0)
    got = exchange(jnp.concatenate([jnp.where(side == 0, base, prefix), mask_rows]))

    first_row = (side * half_rows).astype(jnp.int32)
    own_map = lax.dynamic_index_in_dim(row_maps, side, 0, keepdims=False)
    other_map = lax.dynamic_index_in_dim(row_maps, 1 - side, 0, keepdims=False)
    starts = count(jnp.stack([own_map, other_map]), first_row + edges)
    places = search(
        maps,
        [side.astype(jnp.int32), (1 - side).astype(jnp.int32)],
        [first_row, first_row],
        [starts[0], starts[1]],
    )
    lower = jnp.sum((row_maps < half_rows).astype(jnp.int32), axis=1)
    spill = (child_rows - lower[0] > window) | (lower[1] > window)
    window_at = jnp.where(side == 0, 0, rest // LANES).astype(jnp.int32)
    rest_at = jnp.where(side == 0, window // LANES, 0).astype(jnp.int32)
    add = functools.partial(extend_add, places=places, map_blocks=map_blocks, groups=grid_rows, width=row_count)
    add_other = functools.partial(add, first_place=blocks, starts=starts[1])
    base_sum = add(front, own, first_place=0, starts=starts[0], offset=zero)

    def add_rest(base_sum):
        more = exchange(jnp.where(side == 0, own[:, :rest], own[:, window:]))
        return add_other(base_sum, more, offset=rest_at)

    base_sum = lax.cond(spill, add_rest, lambda x: x, base_sum)

    got, received[0], base_sum, last_sent = lax.optimization_barrier((got, received[0], base_sum, last_sent))
    received.append(exchange(last_sent))
    strip = strip_add(jnp.where(side == 0, base, got[:thin]), jnp.where(side == 0, got[:thin], prefix), 1)
    first_masks = jnp.where(side == 0, mask_rows, got[thin:])

    corner = jnp.where(place == 0, strip[:, PANEL:], strip[:, :PANEL])
    tail = jnp.concatenate([corner, jnp.broadcast_to(mask_rows[:1, :PANEL], (thin, PANEL))], axis=1)
    wholes, pieces = [], {}

    def assemble(index):
        a, b = parts[index]
        size = b - a
        whole, *chunk_list = add_other(
            base_sum, received[index], offset=window_at, columns=size, part=a // size, tail=tail
        )
        wholes.append(whole)
        pieces.update({a // 8 + i: chunk for i, chunk in enumerate(chunk_list)})

    assemble(0)
    to_gather = jnp.concatenate([strip, first_masks])
    to_gather, inverse, received[1], wholes[0] = lax.optimization_barrier(
        (to_gather, inverse, received[1], wholes[0])
    )
    gathered = lax.all_gather(to_gather, "row", axis=0)
    kept = gathered[0, thin, 1] > 0.5

    assemble(1)

    across = lambda x: lax.all_to_all(x, "row", split_axis=0, concat_axis=0, tiled=True)
    order = list(range(chunks))
    middle = chunks // 2
    order[middle : middle + 2], order[-2:] = order[-2:], order[middle : middle + 2]
    mine = jnp.where(place // PANELS == 0, pieces[order[0]], 0.0)
    for chip in range(1, chunks):
        pairs = [(k, PANELS * chip + k) for k in range(PANELS)]
        mine = mine + lax.ppermute(pieces[order[chip]], "col", pairs)
    tails = mine[:, :, row_count:]
    core0 = place % PANELS == 0
    masks_there = lax.ppermute(tails[PANEL // LANES], "col", [(c, c ^ 1) for c in range(lax.axis_size("col"))])
    cross_mask = jnp.where(core0, masks_there, tails[PANEL // LANES])[0, : tile_mask.shape[0]] > 0.5
    corner = tails[: PANEL // LANES].transpose(1, 0, 2).reshape(1, 8, PANEL)
    mine = jnp.concatenate([mine[:, :, :row_count], jnp.broadcast_to(corner, (grid_rows, 8, PANEL))], axis=2)
    moved = [across(wholes[0])]
    mine, moved[0] = lax.optimization_barrier((mine, moved[0]))
    mine = across(mine)
    panels = lax.all_gather(mine.reshape(thin, -1), "col", axis=0, tiled=True)
    panels = panels.reshape(chunks, PANELS, thin, -1)
    last, mine = lax.optimization_barrier((wholes[1], mine))
    moved.append(across(last))

    first, second, fixed = factor(
        order, jnp.stack([place, kept.astype(place.dtype)]).astype(jnp.int32), gathered, inverse, panels
    )

    tiles = row_count // PANEL
    tile_ids = (side * grid_rows + row_place) * tiles + jnp.arange(tiles, dtype=jnp.int32)
    own_mask = tile_mask[:, 0] == 1
    is0, is1 = place == 0, place == 1
    keep = jnp.where(is0, False, jnp.where(is1, tile_ids == 0, True))
    use_first = jnp.where(is0, True, jnp.where(is1, tile_ids >= 1, own_mask & (tile_ids >= 1)))
    use_fixed = jnp.where(is0, False, cross_mask & (tile_ids >= jnp.where(is1, 1, 2)))
    use_second = jnp.where(is0, False, jnp.where(is1, tile_ids >= 1, own_mask & (tile_ids >= 2)))
    flags = jnp.stack([keep, use_first, use_fixed, use_second], axis=1).astype(jnp.int32).reshape(-1)
    return update(flags, moved[::-1], panels, first, second, fixed)


def solution(mesh):
    return jax.shard_map(
        local,
        mesh=mesh,
        in_specs=(
            P("col", "row", None, "subcube"),
            P("subcube", "col", "row", None, None),
            P(),
            P(None, "row", None),
            P(("subcube", "row"), "col"),
        ),
        out_specs=P(("subcube", "row"), "col"),
        check_vma=False,
    )
```

```python
import functools

import jax
import jax.numpy as jnp
from jax import lax
from jax.experimental import pallas as pl
from jax.experimental.pallas import tpu as pltpu
from jax.sharding import PartitionSpec as P

PANEL = 512
PANELS = 2
LANES = 128
BIG = 2**30
VMEM_BYTES = 56 * 2**20


def search_kernel(sections, scalars, maps_ref, places_ref, low_ref, high_ref):
    map_blocks = maps_ref.shape[1]
    at_row = 0
    for section, count in enumerate(sections):
        child = scalars[section]
        first = scalars[len(sections) + section]
        for block in range(count):
            at = jnp.minimum(scalars[2 * len(sections) + at_row + block] // LANES, map_blocks - 1)
            after = jnp.minimum(at + 1, map_blocks - 1)
            row = at_row + block
            low_ref[row : row + 1, :] = maps_ref[child, pl.ds(at, 1), :]
            high_ref[row : row + 1, :] = jnp.where(at + 1 < map_blocks, maps_ref[child, pl.ds(after, 1), :], BIG)
        low, high = low_ref[at_row : at_row + count, :], high_ref[at_row : at_row + count, :]
        lane = lax.broadcasted_iota(jnp.int32, low.shape, 1)
        block_id = lax.broadcasted_iota(jnp.int32, low.shape, 0)
        wanted = first + block_id * LANES + lane

        def pick(at):
            inner = at & (LANES - 1)
            return jnp.where(
                at < LANES, jnp.take_along_axis(low, inner, axis=1), jnp.take_along_axis(high, inner, axis=1)
            )

        place = jnp.zeros(low.shape, jnp.int32)
        width = LANES
        while width >= 1:
            place = jnp.where(pick(place + (width - 1)) < wanted, place + width, place)
            width //= 2
        places_ref[at_row : at_row + count, :] = jnp.where(pick(place) == wanted, place, -1)
        at_row += count


def search(maps, children, firsts, starts):
    sections = tuple(start.shape[0] for start in starts)
    total = sum(sections)
    scalars = jnp.concatenate([jnp.stack(children), jnp.stack(firsts)] + list(starts)).astype(jnp.int32)
    return pl.pallas_call(
        functools.partial(search_kernel, sections),
        out_shape=jax.ShapeDtypeStruct((total, LANES), jnp.int32),
        grid_spec=pltpu.PrefetchScalarGridSpec(
            num_scalar_prefetch=1,
            grid=(1,),
            in_specs=[pl.BlockSpec(maps.shape, lambda i, _: (0, 0, 0))],
            out_specs=pl.BlockSpec((total, LANES), lambda i, _: (0, 0)),
            scratch_shapes=[pltpu.VMEM((total, LANES), jnp.int32)] * 2,
        ),
        compiler_params=pltpu.CompilerParams(vmem_limit_bytes=VMEM_BYTES),
    )(scalars, maps)


def extend_kernel(first_place, map_blocks, scalars, places_ref, front_ref, source_ref, *refs):
    tail_ref, out_ref, piece_refs = (refs[0], refs[1], refs[2:]) if len(refs) > 1 else (None, refs[0], ())
    step = pl.program_id(0)
    groups, columns, width = out_ref.shape
    per_group = width // LANES
    source_blocks = source_ref.shape[1] // LANES
    offset = scalars[scalars.shape[0] - 1]
    lane = lax.broadcasted_iota(jnp.int32, (8, LANES), 1)
    for j in range(groups * per_group):
        block = step * groups * per_group + j
        start = scalars[block]
        at = jnp.minimum(start // LANES, map_blocks - 1)
        split = jnp.where(start // LANES < map_blocks, start & (LANES - 1), LANES)
        at = at - offset
        inside_low = (at >= 0) & (at < source_blocks)
        inside_high = (at + 1 >= 0) & (at + 1 < source_blocks)
        low_at = pl.multiple_of(jnp.clip(at, 0, source_blocks - 1) * LANES, LANES)
        high_at = pl.multiple_of(jnp.clip(at + 1, 0, source_blocks - 1) * LANES, LANES)
        place = jnp.broadcast_to(places_ref[pl.ds(first_place + block, 1), :], (8, LANES))
        inner = place & (LANES - 1)
        hit = ((place >= 0) & (place < LANES) & inside_low) | ((place >= LANES) & inside_high)
        from_low = lane >= split
        group = j // per_group
        here = slice(j % per_group * LANES, (j % per_group + 1) * LANES)
        for row in range(0, columns, 8):
            rows = slice(row, row + 8)
            merged = jnp.where(from_low, source_ref[rows, pl.ds(low_at, LANES)], source_ref[rows, pl.ds(high_at, LANES)])
            gained = jnp.where(hit, jnp.take_along_axis(merged, inner, axis=1), 0.0)
            if len(front_ref.shape) == 2:
                value = front_ref[rows, j * LANES : (j + 1) * LANES] + gained
            else:
                value = front_ref[group, rows, here] + gained
            out_ref[group, rows, here] = value
            if piece_refs:
                piece_refs[row // 8][group, :, here] = value
    for index, piece_ref in enumerate(piece_refs):
        rows = slice(8 * index, 8 * index + 8)
        for group in range(groups):
            lanes = pl.ds(pl.multiple_of((step * groups + group) * LANES, LANES), LANES)
            piece_ref[group, :, width:] = tail_ref[rows, lanes]


def extend_add(front, source, places, first_place, starts, offset, map_blocks, groups, width, columns=None, part=0, tail=None):
    columns = source.shape[0] if columns is None else columns
    steps = 2 if groups % 2 == 0 else 1
    per_step = groups // steps
    if front.ndim == 2:
        front_spec = pl.BlockSpec((columns, per_step * width), lambda i, _: (part, i))
    else:
        front_spec = pl.BlockSpec((per_step, columns, width), lambda i, _: (i, part, 0))
    source_part = part if source.shape[0] > columns else 0
    source_width = min(source.shape[1], map_blocks * LANES if groups > 1 else width)
    scalars = jnp.concatenate([starts, offset.reshape(1)]).astype(jnp.int32)
    whole = lambda shape, row=0: pl.BlockSpec(shape, lambda i, _: (row, 0), pipeline_mode=pl.Buffered(1))
    shapes = [(columns, width)]
    inputs, in_specs = [places, front, source], [whole(places.shape), front_spec, whole((columns, source_width), source_part)]
    if tail is not None:
        shapes += [(8, width + LANES)] * (columns // 8)
        inputs.append(tail)
        in_specs.append(whole((columns, tail.shape[1]), part))
    outs = pl.pallas_call(
        functools.partial(extend_kernel, first_place, map_blocks),
        out_shape=[jax.ShapeDtypeStruct((groups,) + shape, jnp.float32) for shape in shapes],
        grid_spec=pltpu.PrefetchScalarGridSpec(
            num_scalar_prefetch=1,
            grid=(steps,),
            in_specs=in_specs,
            out_specs=[pl.BlockSpec((per_step,) + shape, lambda i, _: (i, 0, 0)) for shape in shapes],
        ),
        compiler_params=pltpu.CompilerParams(vmem_limit_bytes=VMEM_BYTES),
    )(scalars, *inputs)
    return outs[0] if tail is None else outs


def halves(x):
    high = x.astype(jnp.bfloat16)
    return high, (x - high.astype(jnp.float32)).astype(jnp.bfloat16)


def product(left, right, dims):
    left_high, left_low = left
    right_high, right_low = right
    dot = lambda a, b: lax.dot_general(a, b, (dims, ((), ())), preferred_element_type=jnp.float32)
    return dot(left_high, right_high) + (dot(left_high, right_low) + dot(left_low, right_high))


PLAIN = ((1,), (0,))
CROSS = ((1,), (1,))


def factor_kernel(order, flags, gathered_ref, inverse_ref, corner_ref, first_ref, second_ref, fixed_ref):
    place, kept = flags[0], flags[1]
    thin = inverse_ref.shape[2]
    by_chip = lambda x: jnp.concatenate([x[:, 8 * q : 8 * q + 8].reshape(-1, x.shape[2]) for q in order])
    strip = gathered_ref[:, :thin].reshape(PANEL, 2 * PANEL)
    inverse0, inverse1 = (by_chip(inverse_ref[:, k]) for k in range(PANELS))
    halves0, halves1 = halves(inverse0), halves(inverse1)
    corner = corner_ref[...]
    corner10, corner01 = (halves(corner[:, k].reshape(PANEL, PANEL)) for k in range(PANELS))
    first = product(halves(strip[:, :PANEL]), halves0, CROSS)
    lowered = product(halves(first), corner10, PLAIN)
    pivot1 = strip[:, PANEL:] - jnp.where(kept == 1, lowered, 0.0)
    second = product(halves(pivot1), halves1, CROSS)
    second = jnp.where(place == 1, -inverse1.T, second)
    crossed = product(halves(second), corner01, PLAIN)
    fixed = product(halves(crossed), halves0, CROSS)
    first_ref[...] = jnp.where(place == 0, -inverse0.T, jnp.where(place == 1, 0.0, first))
    second_ref[...] = second
    fixed_ref[...] = fixed


def factor(order, flags, gathered, inverse, panels):
    square = jax.ShapeDtypeStruct((PANEL, PANEL), jnp.float32)
    return pl.pallas_call(
        functools.partial(factor_kernel, order),
        out_shape=(square, square, square),
        grid_spec=pltpu.PrefetchScalarGridSpec(
            num_scalar_prefetch=1,
            grid=(1,),
            in_specs=[
                pl.BlockSpec(gathered.shape, lambda i, _: (0, 0, 0)),
                pl.BlockSpec(inverse.shape, lambda i, _: (0, 0, 0, 0)),
            ]
            + [pl.BlockSpec(panels.shape[:3] + (PANEL,), lambda i, _: (0, 0, 0, panels.shape[3] // PANEL - 1))],
            out_specs=[pl.BlockSpec((PANEL, PANEL), lambda i, _: (0, 0))] * 3,
        ),
        compiler_params=pltpu.CompilerParams(vmem_limit_bytes=VMEM_BYTES),
    )(flags, gathered, inverse, panels)


def update_kernel(flags, panels_ref, first_ref, second_ref, fixed_ref, out_ref):
    tile = pl.program_id(0)
    use_first, use_fixed, use_second = (flags[4 * tile + i] == 1 for i in range(1, 4))
    left0 = first_ref[...] - jnp.where(use_fixed, fixed_ref[...], 0.0)
    left0 = halves(jnp.where(use_first, left0, 0.0))
    left1 = halves(jnp.where(use_second, second_ref[...], 0.0))
    panel = panels_ref[...]
    right0 = halves(panel[:, 0].reshape(PANEL, PANEL))
    right1 = halves(panel[:, 1].reshape(PANEL, PANEL))
    out_ref[...] = (product(left0, right0, PLAIN) + product(left1, right1, PLAIN)).T


def update(flags, rows, panels, first, second, fixed):
    square = pl.BlockSpec((PANEL, PANEL), lambda i, _: (0, 0))
    return pl.pallas_call(
        update_kernel,
        out_shape=jax.ShapeDtypeStruct((rows, PANEL), jnp.float32),
        grid_spec=pltpu.PrefetchScalarGridSpec(
            num_scalar_prefetch=1,
            grid=(rows // PANEL,),
            in_specs=[pl.BlockSpec(panels.shape[:3] + (PANEL,), lambda i, _: (0, 0, 0, i)), square, square, square],
            out_specs=pl.BlockSpec((PANEL, PANEL), lambda i, _: (i, 0)),
        ),
        compiler_params=pltpu.CompilerParams(vmem_limit_bytes=VMEM_BYTES),
    )(flags, panels, first, second, fixed)


def finish_kernel(flags, block_ref, update_ref, out_ref):
    keep = flags[4 * pl.program_id(0)] == 1
    out_ref[...] = jnp.where(keep, block_ref[...], 0.0).T - update_ref[...]


def finish(flags, block, lost):
    tile = pl.BlockSpec((PANEL, PANEL), lambda i, _: (i, 0))
    return pl.pallas_call(
        finish_kernel,
        out_shape=jax.ShapeDtypeStruct(lost.shape, jnp.float32),
        grid_spec=pltpu.PrefetchScalarGridSpec(
            num_scalar_prefetch=1,
            grid=(lost.shape[0] // PANEL,),
            in_specs=[pl.BlockSpec((PANEL, PANEL), lambda i, _: (0, i)), tile],
            out_specs=tile,
        ),
        compiler_params=pltpu.CompilerParams(vmem_limit_bytes=VMEM_BYTES),
    )(flags, block, lost)


def local(front_entries, child_blocks, row_maps, pivot_inverses, tile_mask):
    thin, half_rows = front_entries.shape[2:]
    child_rows = child_blocks.shape[4]
    grid_rows = lax.axis_size("row")
    side = lax.axis_index("subcube")
    row_place = lax.axis_index("row")
    place = lax.axis_index("col")
    row_count = half_rows // grid_rows
    chunks = thin // 8
    pivot_rows = PANELS * PANEL
    own = child_blocks[0, 0, 0]
    front = front_entries[0, 0]
    zero = jnp.zeros((), jnp.int32)
    exchange = lambda x: lax.ppermute(x, "subcube", [(0, 1), (1, 0)])

    inverse = lax.all_gather(pivot_inverses, "row", axis=0)

    window = -(-(child_rows * 13 // 24) // LANES) * LANES
    rest = child_rows - window
    share = thin // 4
    parts = [(thin - share, thin), (0, thin - share)]
    first_sent, last_sent = [jnp.where(side == 0, own[a:b, rest:], own[a:b, :window]) for a, b in parts]
    received = [exchange(first_sent)]

    map_blocks = child_rows // LANES
    blocks = half_rows // LANES
    strip_blocks = pivot_rows // LANES
    maps = row_maps.reshape(2, map_blocks, LANES)
    count = lambda maps, edges: jnp.sum((maps[:, None, :] < edges[None, :, None]).astype(jnp.int32), axis=2)
    edges = LANES * jnp.arange(blocks, dtype=jnp.int32)
    strip_starts = count(row_maps, edges[:strip_blocks])
    strip_places = search(maps, [zero, zero + 1], [zero, zero], [strip_starts[0], strip_starts[1]])
    strip_add = lambda base, child, t: extend_add(
        base, child, strip_places, t * strip_blocks, strip_starts[t], zero, map_blocks, 1, pivot_rows
    )[0]
    mask_rows = jnp.zeros((8, pivot_rows), jnp.float32)
    mask_rows = mask_rows.at[0, : tile_mask.shape[0]].set(tile_mask.astype(jnp.float32)[:, 0])
    prefix = own[:, :pivot_rows]
    base = strip_add(front, own, 0)
    got = exchange(jnp.concatenate([jnp.where(side == 0, base, prefix), mask_rows]))

    first_row = (side * half_rows).astype(jnp.int32)
    own_map = lax.dynamic_index_in_dim(row_maps, side, 0, keepdims=False)
    other_map = lax.dynamic_index_in_dim(row_maps, 1 - side, 0, keepdims=False)
    starts = count(jnp.stack([own_map, other_map]), first_row + edges)
    places = search(
        maps,
        [side.astype(jnp.int32), (1 - side).astype(jnp.int32)],
        [first_row, first_row],
        [starts[0], starts[1]],
    )
    lower = jnp.sum((row_maps < half_rows).astype(jnp.int32), axis=1)
    spill = (child_rows - lower[0] > window) | (lower[1] > window)
    window_at = jnp.where(side == 0, 0, rest // LANES).astype(jnp.int32)
    rest_at = jnp.where(side == 0, window // LANES, 0).astype(jnp.int32)
    add = functools.partial(extend_add, places=places, map_blocks=map_blocks, groups=grid_rows, width=row_count)
    add_other = functools.partial(add, first_place=blocks, starts=starts[1])
    base_sum = add(front, own, first_place=0, starts=starts[0], offset=zero)

    def add_rest(base_sum):
        more = exchange(jnp.where(side == 0, own[:, :rest], own[:, window:]))
        return add_other(base_sum, more, offset=rest_at)

    base_sum = lax.cond(spill, add_rest, lambda x: x, base_sum)

    got, received[0], base_sum, last_sent = lax.optimization_barrier((got, received[0], base_sum, last_sent))
    received.append(exchange(last_sent))
    strip = strip_add(jnp.where(side == 0, base, got[:thin]), jnp.where(side == 0, got[:thin], prefix), 1)
    first_masks = jnp.where(side == 0, mask_rows, got[thin:])

    corner = jnp.where(place == 0, strip[:, PANEL:], strip[:, :PANEL])
    tail = jnp.concatenate([corner, jnp.broadcast_to(mask_rows[:1, :PANEL], (thin, PANEL))], axis=1)
    wholes, pieces = [], {}

    def assemble(index):
        a, b = parts[index]
        size = b - a
        whole, *chunk_list = add_other(
            base_sum, received[index], offset=window_at, columns=size, part=a // size, tail=tail
        )
        wholes.append(whole)
        pieces.update({a // 8 + i: chunk for i, chunk in enumerate(chunk_list)})

    assemble(0)
    to_gather = jnp.concatenate([strip, first_masks])
    to_gather, inverse, received[1], wholes[0] = lax.optimization_barrier(
        (to_gather, inverse, received[1], wholes[0])
    )
    gathered = lax.all_gather(to_gather, "row", axis=0)
    kept = gathered[0, thin, 1] > 0.5

    assemble(1)

    across = lambda x: lax.all_to_all(x, "row", split_axis=0, concat_axis=0, tiled=True)
    order = list(range(chunks))
    middle = chunks // 2
    order[middle : middle + 2], order[-2:] = order[-2:], order[middle : middle + 2]
    whole = jnp.concatenate(wholes[::-1], axis=1)
    pieces[order[1]], whole = lax.optimization_barrier((pieces[order[1]], whole))
    mine = jnp.where(place // PANELS == 0, pieces[order[0]], 0.0)
    for chip in range(1, chunks):
        pairs = [(k, PANELS * chip + k) for k in range(PANELS)]
        mine = mine + lax.ppermute(pieces[order[chip]], "col", pairs)
    tails = mine[:, :, row_count:]
    core0 = place % PANELS == 0
    masks_there = lax.ppermute(tails[PANEL // LANES], "col", [(c, c ^ 1) for c in range(lax.axis_size("col"))])
    cross_mask = jnp.where(core0, masks_there, tails[PANEL // LANES])[0, : tile_mask.shape[0]] > 0.5
    corner = tails[: PANEL // LANES].transpose(1, 0, 2).reshape(1, 8, PANEL)
    mine = jnp.concatenate([mine[:, :, :row_count], jnp.broadcast_to(corner, (grid_rows, 8, PANEL))], axis=2)
    mine = across(mine)
    panels = lax.all_gather(mine.reshape(thin, -1), "col", axis=0, tiled=True)
    panels = panels.reshape(chunks, PANELS, thin, -1)
    whole, mine = lax.optimization_barrier((whole, mine))
    block = across(whole).reshape(PANEL, row_count)

    first, second, fixed = factor(
        order, jnp.stack([place, kept.astype(place.dtype)]).astype(jnp.int32), gathered, inverse, panels
    )

    tiles = row_count // PANEL
    tile_ids = (side * grid_rows + row_place) * tiles + jnp.arange(tiles, dtype=jnp.int32)
    own_mask = tile_mask[:, 0] == 1
    is0, is1 = place == 0, place == 1
    keep = jnp.where(is0, False, jnp.where(is1, tile_ids == 0, True))
    use_first = jnp.where(is0, True, jnp.where(is1, tile_ids >= 1, own_mask & (tile_ids >= 1)))
    use_fixed = jnp.where(is0, False, cross_mask & (tile_ids >= jnp.where(is1, 1, 2)))
    use_second = jnp.where(is0, False, jnp.where(is1, tile_ids >= 1, own_mask & (tile_ids >= 2)))
    flags = jnp.stack([keep, use_first, use_fixed, use_second], axis=1).astype(jnp.int32).reshape(-1)
    lost = update(flags, row_count, panels, first, second, fixed)
    return finish(flags, block, lost)


def solution(mesh):
    return jax.shard_map(
        local,
        mesh=mesh,
        in_specs=(
            P("col", "row", None, "subcube"),
            P("subcube", "col", "row", None, None),
            P(),
            P(None, "row", None),
            P(("subcube", "row"), "col"),
        ),
        out_specs=P(("subcube", "row"), "col"),
        check_vma=False,
    )
```

```python
import functools

import jax
import jax.numpy as jnp
from jax import lax
from jax.experimental import pallas as pl
from jax.experimental.pallas import tpu as pltpu
from jax.sharding import PartitionSpec as P

PANEL = 512
PANELS = 2
LANES = 128
BIG = 2**30
VMEM_BYTES = 56 * 2**20


def search_kernel(sections, scalars, maps_ref, places_ref, low_ref, high_ref):
    map_blocks = maps_ref.shape[1]
    at_row = 0
    for section, count in enumerate(sections):
        child = scalars[section]
        first = scalars[len(sections) + section]
        for block in range(count):
            at = jnp.minimum(scalars[2 * len(sections) + at_row + block] // LANES, map_blocks - 1)
            after = jnp.minimum(at + 1, map_blocks - 1)
            row = at_row + block
            low_ref[row : row + 1, :] = maps_ref[child, pl.ds(at, 1), :]
            high_ref[row : row + 1, :] = jnp.where(at + 1 < map_blocks, maps_ref[child, pl.ds(after, 1), :], BIG)
        low, high = low_ref[at_row : at_row + count, :], high_ref[at_row : at_row + count, :]
        lane = lax.broadcasted_iota(jnp.int32, low.shape, 1)
        block_id = lax.broadcasted_iota(jnp.int32, low.shape, 0)
        wanted = first + block_id * LANES + lane

        def pick(at):
            inner = at & (LANES - 1)
            return jnp.where(
                at < LANES, jnp.take_along_axis(low, inner, axis=1), jnp.take_along_axis(high, inner, axis=1)
            )

        place = jnp.zeros(low.shape, jnp.int32)
        width = LANES
        while width >= 1:
            place = jnp.where(pick(place + (width - 1)) < wanted, place + width, place)
            width //= 2
        places_ref[at_row : at_row + count, :] = jnp.where(pick(place) == wanted, place, -1)
        at_row += count


def search(maps, children, firsts, starts):
    sections = tuple(start.shape[0] for start in starts)
    total = sum(sections)
    scalars = jnp.concatenate([jnp.stack(children), jnp.stack(firsts)] + list(starts)).astype(jnp.int32)
    return pl.pallas_call(
        functools.partial(search_kernel, sections),
        out_shape=jax.ShapeDtypeStruct((total, LANES), jnp.int32),
        grid_spec=pltpu.PrefetchScalarGridSpec(
            num_scalar_prefetch=1,
            grid=(1,),
            in_specs=[pl.BlockSpec(maps.shape, lambda i, _: (0, 0, 0))],
            out_specs=pl.BlockSpec((total, LANES), lambda i, _: (0, 0)),
            scratch_shapes=[pltpu.VMEM((total, LANES), jnp.int32)] * 2,
        ),
        compiler_params=pltpu.CompilerParams(vmem_limit_bytes=VMEM_BYTES),
    )(scalars, maps)


def extend_kernel(first_place, map_blocks, scalars, places_ref, front_ref, source_ref, *refs):
    tail_ref, out_ref, piece_refs = (refs[0], refs[1], refs[2:]) if len(refs) > 1 else (None, refs[0], ())
    step = pl.program_id(0)
    groups, columns, width = out_ref.shape
    per_group = width // LANES
    source_blocks = source_ref.shape[1] // LANES
    offset = scalars[scalars.shape[0] - 1]
    lane = lax.broadcasted_iota(jnp.int32, (8, LANES), 1)
    for j in range(groups * per_group):
        block = step * groups * per_group + j
        start = scalars[block]
        at = jnp.minimum(start // LANES, map_blocks - 1)
        split = jnp.where(start // LANES < map_blocks, start & (LANES - 1), LANES)
        at = at - offset
        inside_low = (at >= 0) & (at < source_blocks)
        inside_high = (at + 1 >= 0) & (at + 1 < source_blocks)
        low_at = pl.multiple_of(jnp.clip(at, 0, source_blocks - 1) * LANES, LANES)
        high_at = pl.multiple_of(jnp.clip(at + 1, 0, source_blocks - 1) * LANES, LANES)
        place = jnp.broadcast_to(places_ref[pl.ds(first_place + block, 1), :], (8, LANES))
        inner = place & (LANES - 1)
        hit = ((place >= 0) & (place < LANES) & inside_low) | ((place >= LANES) & inside_high)
        from_low = lane >= split
        group = j // per_group
        here = slice(j % per_group * LANES, (j % per_group + 1) * LANES)
        for row in range(0, columns, 8):
            rows = slice(row, row + 8)
            merged = jnp.where(from_low, source_ref[rows, pl.ds(low_at, LANES)], source_ref[rows, pl.ds(high_at, LANES)])
            gained = jnp.where(hit, jnp.take_along_axis(merged, inner, axis=1), 0.0)
            if len(front_ref.shape) == 2:
                value = front_ref[rows, j * LANES : (j + 1) * LANES] + gained
            else:
                value = front_ref[group, rows, here] + gained
            out_ref[group, rows, here] = value
            if piece_refs:
                piece_refs[row // 8][group, :, here] = value
    for index, piece_ref in enumerate(piece_refs):
        rows = slice(8 * index, 8 * index + 8)
        for group in range(groups):
            lanes = pl.ds(pl.multiple_of((step * groups + group) * LANES, LANES), LANES)
            piece_ref[group, :, width:] = tail_ref[rows, lanes]


def extend_add(front, source, places, first_place, starts, offset, map_blocks, groups, width, columns=None, part=0, tail=None):
    columns = source.shape[0] if columns is None else columns
    steps = 2 if groups % 2 == 0 else 1
    per_step = groups // steps
    if front.ndim == 2:
        front_spec = pl.BlockSpec((columns, per_step * width), lambda i, _: (part, i))
    else:
        front_spec = pl.BlockSpec((per_step, columns, width), lambda i, _: (i, part, 0))
    source_part = part if source.shape[0] > columns else 0
    source_width = min(source.shape[1], map_blocks * LANES if groups > 1 else width)
    scalars = jnp.concatenate([starts, offset.reshape(1)]).astype(jnp.int32)
    whole = lambda shape, row=0: pl.BlockSpec(shape, lambda i, _: (row, 0), pipeline_mode=pl.Buffered(1))
    shapes = [(columns, width)]
    inputs, in_specs = [places, front, source], [whole(places.shape), front_spec, whole((columns, source_width), source_part)]
    if tail is not None:
        shapes += [(8, width + LANES)] * (columns // 8)
        inputs.append(tail)
        in_specs.append(whole((columns, tail.shape[1]), part))
    outs = pl.pallas_call(
        functools.partial(extend_kernel, first_place, map_blocks),
        out_shape=[jax.ShapeDtypeStruct((groups,) + shape, jnp.float32) for shape in shapes],
        grid_spec=pltpu.PrefetchScalarGridSpec(
            num_scalar_prefetch=1,
            grid=(steps,),
            in_specs=in_specs,
            out_specs=[pl.BlockSpec((per_step,) + shape, lambda i, _: (i, 0, 0)) for shape in shapes],
        ),
        compiler_params=pltpu.CompilerParams(vmem_limit_bytes=VMEM_BYTES),
    )(scalars, *inputs)
    return outs[0] if tail is None else outs


def halves(x):
    high = x.astype(jnp.bfloat16)
    return high, (x - high.astype(jnp.float32)).astype(jnp.bfloat16)


def product(left, right, dims):
    left_high, left_low = left
    right_high, right_low = right
    dot = lambda a, b: lax.dot_general(a, b, (dims, ((), ())), preferred_element_type=jnp.float32)
    return dot(left_high, right_high) + (dot(left_high, right_low) + dot(left_low, right_high))


PLAIN = ((1,), (0,))
CROSS = ((1,), (1,))


def factor_kernel(order, flags, gathered_ref, inverse_ref, corner_ref, first_ref, second_ref, fixed_ref):
    place, kept = flags[0], flags[1]
    thin = inverse_ref.shape[2]
    by_chip = lambda x: jnp.concatenate([x[:, 8 * q : 8 * q + 8].reshape(-1, x.shape[2]) for q in order])
    strip = gathered_ref[:, :thin].reshape(PANEL, 2 * PANEL)
    inverse0, inverse1 = (by_chip(inverse_ref[:, k]) for k in range(PANELS))
    halves0, halves1 = halves(inverse0), halves(inverse1)
    corner = corner_ref[...]
    corner10, corner01 = (halves(corner[:, k].reshape(PANEL, PANEL)) for k in range(PANELS))
    first = product(halves(strip[:, :PANEL]), halves0, CROSS)
    lowered = product(halves(first), corner10, PLAIN)
    pivot1 = strip[:, PANEL:] - jnp.where(kept == 1, lowered, 0.0)
    second = product(halves(pivot1), halves1, CROSS)
    second = jnp.where(place == 1, -inverse1.T, second)
    crossed = product(halves(second), corner01, PLAIN)
    fixed = product(halves(crossed), halves0, CROSS)
    first_ref[...] = jnp.where(place == 0, -inverse0.T, jnp.where(place == 1, 0.0, first))
    second_ref[...] = second
    fixed_ref[...] = fixed


def factor(order, flags, gathered, inverse, panels):
    square = jax.ShapeDtypeStruct((PANEL, PANEL), jnp.float32)
    return pl.pallas_call(
        functools.partial(factor_kernel, order),
        out_shape=(square, square, square),
        grid_spec=pltpu.PrefetchScalarGridSpec(
            num_scalar_prefetch=1,
            grid=(1,),
            in_specs=[
                pl.BlockSpec(gathered.shape, lambda i, _: (0, 0, 0)),
                pl.BlockSpec(inverse.shape, lambda i, _: (0, 0, 0, 0)),
            ]
            + [pl.BlockSpec(panels.shape[:3] + (PANEL,), lambda i, _: (0, 0, 0, panels.shape[3] // PANEL - 1))],
            out_specs=[pl.BlockSpec((PANEL, PANEL), lambda i, _: (0, 0))] * 3,
        ),
        compiler_params=pltpu.CompilerParams(vmem_limit_bytes=VMEM_BYTES),
    )(flags, gathered, inverse, panels)


def update_kernel(flags, panels_ref, first_ref, second_ref, fixed_ref, out_ref):
    tile = pl.program_id(0)
    use_first, use_fixed, use_second = (flags[4 * tile + i] == 1 for i in range(1, 4))
    left0 = first_ref[...] - jnp.where(use_fixed, fixed_ref[...], 0.0)
    left0 = halves(jnp.where(use_first, left0, 0.0))
    left1 = halves(jnp.where(use_second, second_ref[...], 0.0))
    panel = panels_ref[...]
    right0 = halves(panel[:, 0].reshape(PANEL, PANEL))
    right1 = halves(panel[:, 1].reshape(PANEL, PANEL))
    out_ref[...] = (product(left0, right0, PLAIN) + product(left1, right1, PLAIN)).T


def update(flags, rows, panels, first, second, fixed):
    square = pl.BlockSpec((PANEL, PANEL), lambda i, _: (0, 0))
    return pl.pallas_call(
        update_kernel,
        out_shape=jax.ShapeDtypeStruct((rows, PANEL), jnp.float32),
        grid_spec=pltpu.PrefetchScalarGridSpec(
            num_scalar_prefetch=1,
            grid=(rows // PANEL,),
            in_specs=[pl.BlockSpec(panels.shape[:3] + (PANEL,), lambda i, _: (0, 0, 0, i)), square, square, square],
            out_specs=pl.BlockSpec((PANEL, PANEL), lambda i, _: (i, 0)),
        ),
        compiler_params=pltpu.CompilerParams(vmem_limit_bytes=VMEM_BYTES),
    )(flags, panels, first, second, fixed)


def finish_kernel(flags, block_ref, update_ref, out_ref):
    keep = flags[4 * pl.program_id(0)] == 1
    out_ref[...] = jnp.where(keep, block_ref[...], 0.0).T - update_ref[...]


def finish(flags, block, lost):
    tile = pl.BlockSpec((PANEL, PANEL), lambda i, _: (i, 0))
    return pl.pallas_call(
        finish_kernel,
        out_shape=jax.ShapeDtypeStruct(lost.shape, jnp.float32),
        grid_spec=pltpu.PrefetchScalarGridSpec(
            num_scalar_prefetch=1,
            grid=(lost.shape[0] // PANEL,),
            in_specs=[pl.BlockSpec((PANEL, PANEL), lambda i, _: (0, i)), tile],
            out_specs=tile,
        ),
        compiler_params=pltpu.CompilerParams(vmem_limit_bytes=VMEM_BYTES),
    )(flags, block, lost)


def local(front_entries, child_blocks, row_maps, pivot_inverses, tile_mask):
    thin, half_rows = front_entries.shape[2:]
    child_rows = child_blocks.shape[4]
    grid_rows = lax.axis_size("row")
    side = lax.axis_index("subcube")
    row_place = lax.axis_index("row")
    place = lax.axis_index("col")
    row_count = half_rows // grid_rows
    chunks = thin // 8
    pivot_rows = PANELS * PANEL
    own = child_blocks[0, 0, 0]
    front = front_entries[0, 0]
    zero = jnp.zeros((), jnp.int32)
    exchange = lambda x: lax.ppermute(x, "subcube", [(0, 1), (1, 0)])

    inverse = lax.all_gather(pivot_inverses, "row", axis=0)

    window = -(-(child_rows * 13 // 24) // LANES) * LANES
    rest = child_rows - window
    share = thin // 4
    parts = [(thin - share, thin), (0, thin - share)]
    first_sent, last_sent = [jnp.where(side == 0, own[a:b, rest:], own[a:b, :window]) for a, b in parts]
    received = [exchange(first_sent)]

    map_blocks = child_rows // LANES
    blocks = half_rows // LANES
    strip_blocks = pivot_rows // LANES
    maps = row_maps.reshape(2, map_blocks, LANES)
    count = lambda maps, edges: jnp.sum((maps[:, None, :] < edges[None, :, None]).astype(jnp.int32), axis=2)
    edges = LANES * jnp.arange(blocks, dtype=jnp.int32)
    strip_starts = count(row_maps[1:], edges[:strip_blocks])[0]
    mask_rows = jnp.zeros((8, pivot_rows), jnp.float32)
    mask_rows = mask_rows.at[0, : tile_mask.shape[0]].set(tile_mask.astype(jnp.float32)[:, 0])
    prefix = own[:, :pivot_rows]

    first_row = (side * half_rows).astype(jnp.int32)
    own_map = lax.dynamic_index_in_dim(row_maps, side, 0, keepdims=False)
    other_map = lax.dynamic_index_in_dim(row_maps, 1 - side, 0, keepdims=False)
    starts = count(jnp.stack([own_map, other_map]), first_row + edges)
    places = search(
        maps,
        [side.astype(jnp.int32), (1 - side).astype(jnp.int32), zero + 1],
        [first_row, first_row, zero],
        [starts[0], starts[1], strip_starts],
    )
    lower = jnp.sum((row_maps < half_rows).astype(jnp.int32), axis=1)
    spill = (child_rows - lower[0] > window) | (lower[1] > window)
    window_at = jnp.where(side == 0, 0, rest // LANES).astype(jnp.int32)
    rest_at = jnp.where(side == 0, window // LANES, 0).astype(jnp.int32)
    add = functools.partial(extend_add, places=places, map_blocks=map_blocks, groups=grid_rows, width=row_count)
    add_other = functools.partial(add, first_place=blocks, starts=starts[1])
    base_sum = add(front, own, first_place=0, starts=starts[0], offset=zero)

    def add_rest(base_sum):
        more = exchange(jnp.where(side == 0, own[:, :rest], own[:, window:]))
        return add_other(base_sum, more, offset=rest_at)

    base = base_sum[0, :, :pivot_rows]
    strip_sent = jnp.concatenate([jnp.where(side == 0, base, prefix), mask_rows])
    strip_sent, received[0], last_sent = lax.optimization_barrier((strip_sent, received[0], last_sent))
    got = exchange(strip_sent)
    received.append(exchange(last_sent))
    base_sum = lax.cond(spill, add_rest, lambda x: x, base_sum)

    strip = extend_add(
        jnp.where(side == 0, base, got[:thin]), jnp.where(side == 0, got[:thin], prefix),
        places, 2 * blocks, strip_starts, zero, map_blocks, 1, pivot_rows,
    )[0]
    first_masks = jnp.where(side == 0, mask_rows, got[thin:])

    corner = jnp.where(place == 0, strip[:, PANEL:], strip[:, :PANEL])
    tail = jnp.concatenate([corner, jnp.broadcast_to(mask_rows[:1, :PANEL], (thin, PANEL))], axis=1)
    wholes, pieces = [], {}

    def assemble(index):
        a, b = parts[index]
        size = b - a
        whole, *chunk_list = add_other(
            base_sum, received[index], offset=window_at, columns=size, part=a // size, tail=tail
        )
        wholes.append(whole)
        pieces.update({a // 8 + i: chunk for i, chunk in enumerate(chunk_list)})

    assemble(0)
    to_gather = jnp.concatenate([strip, first_masks])
    to_gather, inverse, received[1], wholes[0] = lax.optimization_barrier(
        (to_gather, inverse, received[1], wholes[0])
    )
    gathered = lax.all_gather(to_gather, "row", axis=0)
    kept = gathered[0, thin, 1] > 0.5

    assemble(1)

    across = lambda x: lax.all_to_all(x, "row", split_axis=0, concat_axis=0, tiled=True)
    order = list(range(chunks))
    middle = chunks // 2
    order[middle : middle + 2], order[-2:] = order[-2:], order[middle : middle + 2]
    whole = jnp.concatenate(wholes[::-1], axis=1)
    pieces[order[1]], whole = lax.optimization_barrier((pieces[order[1]], whole))
    mine = jnp.where(place // PANELS == 0, pieces[order[0]], 0.0)
    for chip in range(1, chunks):
        pairs = [(k, PANELS * chip + k) for k in range(PANELS)]
        mine = mine + lax.ppermute(pieces[order[chip]], "col", pairs)
    tails = mine[:, :, row_count:]
    core0 = place % PANELS == 0
    masks_there = lax.ppermute(tails[PANEL // LANES], "col", [(c, c ^ 1) for c in range(lax.axis_size("col"))])
    cross_mask = jnp.where(core0, masks_there, tails[PANEL // LANES])[0, : tile_mask.shape[0]] > 0.5
    corner = tails[: PANEL // LANES].transpose(1, 0, 2).reshape(1, 8, PANEL)
    mine = jnp.concatenate([mine[:, :, :row_count], jnp.broadcast_to(corner, (grid_rows, 8, PANEL))], axis=2)
    mine = across(mine)
    panels = lax.all_gather(mine.reshape(thin, -1), "col", axis=0, tiled=True)
    panels = panels.reshape(chunks, PANELS, thin, -1)
    whole, mine = lax.optimization_barrier((whole, mine))
    block = across(whole).reshape(PANEL, row_count)

    first, second, fixed = factor(
        order, jnp.stack([place, kept.astype(place.dtype)]).astype(jnp.int32), gathered, inverse, panels
    )

    tiles = row_count // PANEL
    tile_ids = (side * grid_rows + row_place) * tiles + jnp.arange(tiles, dtype=jnp.int32)
    own_mask = tile_mask[:, 0] == 1
    is0, is1 = place == 0, place == 1
    keep = jnp.where(is0, False, jnp.where(is1, tile_ids == 0, True))
    use_first = jnp.where(is0, True, jnp.where(is1, tile_ids >= 1, own_mask & (tile_ids >= 1)))
    use_fixed = jnp.where(is0, False, cross_mask & (tile_ids >= jnp.where(is1, 1, 2)))
    use_second = jnp.where(is0, False, jnp.where(is1, tile_ids >= 1, own_mask & (tile_ids >= 2)))
    flags = jnp.stack([keep, use_first, use_fixed, use_second], axis=1).astype(jnp.int32).reshape(-1)
    lost = update(flags, row_count, panels, first, second, fixed)
    return finish(flags, block, lost)


def solution(mesh):
    return jax.shard_map(
        local,
        mesh=mesh,
        in_specs=(
            P("col", "row", None, "subcube"),
            P("subcube", "col", "row", None, None),
            P(),
            P(None, "row", None),
            P(("subcube", "row"), "col"),
        ),
        out_specs=P(("subcube", "row"), "col"),
        check_vma=False,
    )
```

```python
import functools

import jax
import jax.numpy as jnp
from jax import lax
from jax.experimental import pallas as pl
from jax.experimental.pallas import tpu as pltpu
from jax.sharding import PartitionSpec as P

PANEL = 512
PANELS = 2
LANES = 128
BIG = 2**30
VMEM_BYTES = 56 * 2**20


def search_kernel(sections, scalars, maps_ref, places_ref, low_ref, high_ref):
    map_blocks = maps_ref.shape[1]
    at_row = 0
    for section, count in enumerate(sections):
        child = scalars[section]
        first = scalars[len(sections) + section]
        for block in range(count):
            at = jnp.minimum(scalars[2 * len(sections) + at_row + block] // LANES, map_blocks - 1)
            after = jnp.minimum(at + 1, map_blocks - 1)
            row = at_row + block
            low_ref[row : row + 1, :] = maps_ref[child, pl.ds(at, 1), :]
            high_ref[row : row + 1, :] = jnp.where(at + 1 < map_blocks, maps_ref[child, pl.ds(after, 1), :], BIG)
        low, high = low_ref[at_row : at_row + count, :], high_ref[at_row : at_row + count, :]
        lane = lax.broadcasted_iota(jnp.int32, low.shape, 1)
        block_id = lax.broadcasted_iota(jnp.int32, low.shape, 0)
        wanted = first + block_id * LANES + lane

        def pick(at):
            inner = at & (LANES - 1)
            return jnp.where(
                at < LANES, jnp.take_along_axis(low, inner, axis=1), jnp.take_along_axis(high, inner, axis=1)
            )

        place = jnp.zeros(low.shape, jnp.int32)
        width = LANES
        while width >= 1:
            place = jnp.where(pick(place + (width - 1)) < wanted, place + width, place)
            width //= 2
        places_ref[at_row : at_row + count, :] = jnp.where(pick(place) == wanted, place, -1)
        at_row += count


def search(maps, children, firsts, starts):
    sections = tuple(start.shape[0] for start in starts)
    total = sum(sections)
    scalars = jnp.concatenate([jnp.stack(children), jnp.stack(firsts)] + list(starts)).astype(jnp.int32)
    return pl.pallas_call(
        functools.partial(search_kernel, sections),
        out_shape=jax.ShapeDtypeStruct((total, LANES), jnp.int32),
        grid_spec=pltpu.PrefetchScalarGridSpec(
            num_scalar_prefetch=1,
            grid=(1,),
            in_specs=[pl.BlockSpec(maps.shape, lambda i, _: (0, 0, 0))],
            out_specs=pl.BlockSpec((total, LANES), lambda i, _: (0, 0)),
            scratch_shapes=[pltpu.VMEM((total, LANES), jnp.int32)] * 2,
        ),
        compiler_params=pltpu.CompilerParams(vmem_limit_bytes=VMEM_BYTES),
    )(scalars, maps)


def extend_kernel(first_place, map_blocks, scalars, places_ref, front_ref, source_ref, *refs):
    tail_ref, out_ref, piece_refs = (refs[0], refs[1], refs[2:]) if len(refs) > 1 else (None, refs[0], ())
    step = pl.program_id(0)
    groups, columns, width = out_ref.shape
    per_group = width // LANES
    source_blocks = source_ref.shape[1] // LANES
    offset = scalars[scalars.shape[0] - 1]
    lane = lax.broadcasted_iota(jnp.int32, (8, LANES), 1)
    for j in range(groups * per_group):
        block = step * groups * per_group + j
        start = scalars[block]
        at = jnp.minimum(start // LANES, map_blocks - 1)
        split = jnp.where(start // LANES < map_blocks, start & (LANES - 1), LANES)
        at = at - offset
        inside_low = (at >= 0) & (at < source_blocks)
        inside_high = (at + 1 >= 0) & (at + 1 < source_blocks)
        low_at = pl.multiple_of(jnp.clip(at, 0, source_blocks - 1) * LANES, LANES)
        high_at = pl.multiple_of(jnp.clip(at + 1, 0, source_blocks - 1) * LANES, LANES)
        place = jnp.broadcast_to(places_ref[pl.ds(first_place + block, 1), :], (8, LANES))
        inner = place & (LANES - 1)
        hit = ((place >= 0) & (place < LANES) & inside_low) | ((place >= LANES) & inside_high)
        from_low = lane >= split
        group = j // per_group
        here = slice(j % per_group * LANES, (j % per_group + 1) * LANES)
        for row in range(0, columns, 8):
            rows = slice(row, row + 8)
            merged = jnp.where(from_low, source_ref[rows, pl.ds(low_at, LANES)], source_ref[rows, pl.ds(high_at, LANES)])
            gained = jnp.where(hit, jnp.take_along_axis(merged, inner, axis=1), 0.0)
            if len(front_ref.shape) == 2:
                value = front_ref[rows, j * LANES : (j + 1) * LANES] + gained
            else:
                value = front_ref[group, rows, here] + gained
            out_ref[group, rows, here] = value
            if piece_refs:
                piece_refs[row // 8][group, :, here] = value
    for index, piece_ref in enumerate(piece_refs):
        rows = slice(8 * index, 8 * index + 8)
        for group in range(groups):
            lanes = pl.ds(pl.multiple_of((step * groups + group) * LANES, LANES), LANES)
            piece_ref[group, :, width:] = tail_ref[rows, lanes]


def extend_add(front, source, places, first_place, starts, offset, map_blocks, groups, width, columns=None, part=0, tail=None):
    columns = source.shape[0] if columns is None else columns
    steps = 2 if groups % 2 == 0 else 1
    per_step = groups // steps
    if front.ndim == 2:
        front_spec = pl.BlockSpec((columns, per_step * width), lambda i, _: (part, i))
    else:
        front_spec = pl.BlockSpec((per_step, columns, width), lambda i, _: (i, part, 0))
    source_part = part if source.shape[0] > columns else 0
    source_width = min(source.shape[1], map_blocks * LANES if groups > 1 else width)
    scalars = jnp.concatenate([starts, offset.reshape(1)]).astype(jnp.int32)
    whole = lambda shape, row=0: pl.BlockSpec(shape, lambda i, _: (row, 0), pipeline_mode=pl.Buffered(1))
    shapes = [(columns, width)]
    inputs, in_specs = [places, front, source], [whole(places.shape), front_spec, whole((columns, source_width), source_part)]
    if tail is not None:
        shapes += [(8, width + LANES)] * (columns // 8)
        inputs.append(tail)
        in_specs.append(whole((columns, tail.shape[1]), part))
    outs = pl.pallas_call(
        functools.partial(extend_kernel, first_place, map_blocks),
        out_shape=[jax.ShapeDtypeStruct((groups,) + shape, jnp.float32) for shape in shapes],
        grid_spec=pltpu.PrefetchScalarGridSpec(
            num_scalar_prefetch=1,
            grid=(steps,),
            in_specs=in_specs,
            out_specs=[pl.BlockSpec((per_step,) + shape, lambda i, _: (i, 0, 0)) for shape in shapes],
        ),
        compiler_params=pltpu.CompilerParams(vmem_limit_bytes=VMEM_BYTES),
    )(scalars, *inputs)
    return outs[0] if tail is None else outs


def halves(x):
    high = x.astype(jnp.bfloat16)
    return high, (x - high.astype(jnp.float32)).astype(jnp.bfloat16)


def product(left, right, dims):
    left_high, left_low = left
    right_high, right_low = right
    dot = lambda a, b: lax.dot_general(a, b, (dims, ((), ())), preferred_element_type=jnp.float32)
    return dot(left_high, right_high) + (dot(left_high, right_low) + dot(left_low, right_high))


PLAIN = ((1,), (0,))
CROSS = ((1,), (1,))


def factor_kernel(order, flags, gathered_ref, inverse_ref, corner_ref, first_ref, second_ref, fixed_ref):
    place, kept = flags[0], flags[1]
    thin = inverse_ref.shape[2]
    by_chip = lambda x: jnp.concatenate([x[:, 8 * q : 8 * q + 8].reshape(-1, x.shape[2]) for q in order])
    strip = gathered_ref[:, :thin].reshape(PANEL, 2 * PANEL)
    inverse0, inverse1 = (by_chip(inverse_ref[:, k]) for k in range(PANELS))
    halves0, halves1 = halves(inverse0), halves(inverse1)
    corner = corner_ref[...]
    corner10, corner01 = (halves(corner[:, k].reshape(PANEL, PANEL)) for k in range(PANELS))
    first = product(halves(strip[:, :PANEL]), halves0, CROSS)
    lowered = product(halves(first), corner10, PLAIN)
    pivot1 = strip[:, PANEL:] - jnp.where(kept == 1, lowered, 0.0)
    second = product(halves(pivot1), halves1, CROSS)
    second = jnp.where(place == 1, -inverse1.T, second)
    crossed = product(halves(second), corner01, PLAIN)
    fixed = product(halves(crossed), halves0, CROSS)
    first_ref[...] = jnp.where(place == 0, -inverse0.T, jnp.where(place == 1, 0.0, first))
    second_ref[...] = second
    fixed_ref[...] = fixed


def factor(order, flags, gathered, inverse, panels):
    square = jax.ShapeDtypeStruct((PANEL, PANEL), jnp.float32)
    return pl.pallas_call(
        functools.partial(factor_kernel, order),
        out_shape=(square, square, square),
        grid_spec=pltpu.PrefetchScalarGridSpec(
            num_scalar_prefetch=1,
            grid=(1,),
            in_specs=[
                pl.BlockSpec(gathered.shape, lambda i, _: (0, 0, 0)),
                pl.BlockSpec(inverse.shape, lambda i, _: (0, 0, 0, 0)),
            ]
            + [pl.BlockSpec(panels.shape[:3] + (PANEL,), lambda i, _: (0, 0, 0, panels.shape[3] // PANEL - 1))],
            out_specs=[pl.BlockSpec((PANEL, PANEL), lambda i, _: (0, 0))] * 3,
        ),
        compiler_params=pltpu.CompilerParams(vmem_limit_bytes=VMEM_BYTES),
    )(flags, gathered, inverse, panels)


def update_kernel(flags, panels_ref, first_ref, second_ref, fixed_ref, out_ref):
    tile = pl.program_id(0)
    use_first, use_fixed, use_second = (flags[4 * tile + i] == 1 for i in range(1, 4))
    left0 = first_ref[...] - jnp.where(use_fixed, fixed_ref[...], 0.0)
    left0 = halves(jnp.where(use_first, left0, 0.0))
    left1 = halves(jnp.where(use_second, second_ref[...], 0.0))
    panel = panels_ref[...]
    right0 = halves(panel[:, 0].reshape(PANEL, PANEL))
    right1 = halves(panel[:, 1].reshape(PANEL, PANEL))
    out_ref[...] = (product(left0, right0, PLAIN) + product(left1, right1, PLAIN)).T


def update(flags, rows, panels, first, second, fixed):
    square = pl.BlockSpec((PANEL, PANEL), lambda i, _: (0, 0))
    return pl.pallas_call(
        update_kernel,
        out_shape=jax.ShapeDtypeStruct((rows, PANEL), jnp.float32),
        grid_spec=pltpu.PrefetchScalarGridSpec(
            num_scalar_prefetch=1,
            grid=(rows // PANEL,),
            in_specs=[pl.BlockSpec(panels.shape[:3] + (PANEL,), lambda i, _: (0, 0, 0, i)), square, square, square],
            out_specs=pl.BlockSpec((PANEL, PANEL), lambda i, _: (i, 0)),
        ),
        compiler_params=pltpu.CompilerParams(vmem_limit_bytes=VMEM_BYTES),
    )(flags, panels, first, second, fixed)


def finish_kernel(flags, block_ref, update_ref, out_ref):
    keep = flags[4 * pl.program_id(0)] == 1
    out_ref[...] = jnp.where(keep, block_ref[...], 0.0).T - update_ref[...]


def finish(flags, block, lost):
    tile = pl.BlockSpec((PANEL, PANEL), lambda i, _: (i, 0))
    return pl.pallas_call(
        finish_kernel,
        out_shape=jax.ShapeDtypeStruct(lost.shape, jnp.float32),
        grid_spec=pltpu.PrefetchScalarGridSpec(
            num_scalar_prefetch=1,
            grid=(lost.shape[0] // PANEL,),
            in_specs=[pl.BlockSpec((PANEL, PANEL), lambda i, _: (0, i)), tile],
            out_specs=tile,
        ),
        compiler_params=pltpu.CompilerParams(vmem_limit_bytes=VMEM_BYTES),
    )(flags, block, lost)


def local(front_entries, child_blocks, row_maps, pivot_inverses, tile_mask):
    thin, half_rows = front_entries.shape[2:]
    child_rows = child_blocks.shape[4]
    grid_rows = lax.axis_size("row")
    side = lax.axis_index("subcube")
    row_place = lax.axis_index("row")
    place = lax.axis_index("col")
    row_count = half_rows // grid_rows
    chunks = thin // 8
    pivot_rows = PANELS * PANEL
    own = child_blocks[0, 0, 0]
    front = front_entries[0, 0]
    zero = jnp.zeros((), jnp.int32)
    exchange = lambda x: lax.ppermute(x, "subcube", [(0, 1), (1, 0)])

    inverse = lax.all_gather(pivot_inverses, "row", axis=0)

    window = -(-(child_rows * 13 // 24) // LANES) * LANES
    rest = child_rows - window
    share = thin // 2
    parts = [(thin - share, thin), (0, thin - share)]
    first_sent, last_sent = [jnp.where(side == 0, own[a:b, rest:], own[a:b, :window]) for a, b in parts]
    received = [exchange(first_sent)]

    map_blocks = child_rows // LANES
    blocks = half_rows // LANES
    strip_blocks = pivot_rows // LANES
    maps = row_maps.reshape(2, map_blocks, LANES)
    count = lambda maps, edges: jnp.sum((maps[:, None, :] < edges[None, :, None]).astype(jnp.int32), axis=2)
    edges = LANES * jnp.arange(blocks, dtype=jnp.int32)
    strip_starts = count(row_maps[1:], edges[:strip_blocks])[0]
    mask_rows = jnp.zeros((8, pivot_rows), jnp.float32)
    mask_rows = mask_rows.at[0, : tile_mask.shape[0]].set(tile_mask.astype(jnp.float32)[:, 0])
    prefix = own[:, :pivot_rows]

    first_row = (side * half_rows).astype(jnp.int32)
    own_map = lax.dynamic_index_in_dim(row_maps, side, 0, keepdims=False)
    other_map = lax.dynamic_index_in_dim(row_maps, 1 - side, 0, keepdims=False)
    starts = count(jnp.stack([own_map, other_map]), first_row + edges)
    places = search(
        maps,
        [side.astype(jnp.int32), (1 - side).astype(jnp.int32), zero + 1],
        [first_row, first_row, zero],
        [starts[0], starts[1], strip_starts],
    )
    lower = jnp.sum((row_maps < half_rows).astype(jnp.int32), axis=1)
    spill = (child_rows - lower[0] > window) | (lower[1] > window)
    window_at = jnp.where(side == 0, 0, rest // LANES).astype(jnp.int32)
    rest_at = jnp.where(side == 0, window // LANES, 0).astype(jnp.int32)
    add = functools.partial(extend_add, places=places, map_blocks=map_blocks, groups=grid_rows, width=row_count)
    add_other = functools.partial(add, first_place=blocks, starts=starts[1])
    base_sum = add(front, own, first_place=0, starts=starts[0], offset=zero)

    def add_rest(base_sum):
        more = exchange(jnp.where(side == 0, own[:, :rest], own[:, window:]))
        return add_other(base_sum, more, offset=rest_at)

    base = base_sum[0, :, :pivot_rows]
    strip_sent = jnp.concatenate([jnp.where(side == 0, base, prefix), mask_rows])
    strip_sent, received[0], last_sent = lax.optimization_barrier((strip_sent, received[0], last_sent))
    got = exchange(strip_sent)
    received.append(exchange(last_sent))
    base_sum = lax.cond(spill, add_rest, lambda x: x, base_sum)

    strip = extend_add(
        jnp.where(side == 0, base, got[:thin]), jnp.where(side == 0, got[:thin], prefix),
        places, 2 * blocks, strip_starts, zero, map_blocks, 1, pivot_rows,
    )[0]
    first_masks = jnp.where(side == 0, mask_rows, got[thin:])

    corner = jnp.where(place == 0, strip[:, PANEL:], strip[:, :PANEL])
    tail = jnp.concatenate([corner, jnp.broadcast_to(mask_rows[:1, :PANEL], (thin, PANEL))], axis=1)
    wholes, pieces = [], {}

    def assemble(index):
        a, b = parts[index]
        size = b - a
        whole, *chunk_list = add_other(
            base_sum, received[index], offset=window_at, columns=size, part=a // size, tail=tail
        )
        wholes.append(whole)
        pieces.update({a // 8 + i: chunk for i, chunk in enumerate(chunk_list)})

    assemble(0)
    to_gather = jnp.concatenate([strip, first_masks])
    to_gather, inverse, received[1], wholes[0] = lax.optimization_barrier(
        (to_gather, inverse, received[1], wholes[0])
    )
    gathered = lax.all_gather(to_gather, "row", axis=0)
    kept = gathered[0, thin, 1] > 0.5

    assemble(1)

    across = lambda x: lax.all_to_all(x, "row", split_axis=0, concat_axis=0, tiled=True)
    order = [0, 1] + list(range(chunks // 2, chunks)) + list(range(2, chunks // 2))
    whole = jnp.concatenate(wholes[::-1], axis=1)
    pieces[order[1]], whole = lax.optimization_barrier((pieces[order[1]], whole))
    mine = jnp.where(place // PANELS == 0, pieces[order[0]], 0.0)
    for chip in range(1, chunks):
        pairs = [(k, PANELS * chip + k) for k in range(PANELS)]
        mine = mine + lax.ppermute(pieces[order[chip]], "col", pairs)
    tails = mine[:, :, row_count:]
    core0 = place % PANELS == 0
    masks_there = lax.ppermute(tails[PANEL // LANES], "col", [(c, c ^ 1) for c in range(lax.axis_size("col"))])
    cross_mask = jnp.where(core0, masks_there, tails[PANEL // LANES])[0, : tile_mask.shape[0]] > 0.5
    corner = tails[: PANEL // LANES].transpose(1, 0, 2).reshape(1, 8, PANEL)
    mine = jnp.concatenate([mine[:, :, :row_count], jnp.broadcast_to(corner, (grid_rows, 8, PANEL))], axis=2)
    mine = across(mine)
    panels = lax.all_gather(mine.reshape(thin, -1), "col", axis=0, tiled=True)
    panels = panels.reshape(chunks, PANELS, thin, -1)
    whole, mine = lax.optimization_barrier((whole, mine))
    block = across(whole).reshape(PANEL, row_count)

    first, second, fixed = factor(
        order, jnp.stack([place, kept.astype(place.dtype)]).astype(jnp.int32), gathered, inverse, panels
    )

    tiles = row_count // PANEL
    tile_ids = (side * grid_rows + row_place) * tiles + jnp.arange(tiles, dtype=jnp.int32)
    own_mask = tile_mask[:, 0] == 1
    is0, is1 = place == 0, place == 1
    keep = jnp.where(is0, False, jnp.where(is1, tile_ids == 0, True))
    use_first = jnp.where(is0, True, jnp.where(is1, tile_ids >= 1, own_mask & (tile_ids >= 1)))
    use_fixed = jnp.where(is0, False, cross_mask & (tile_ids >= jnp.where(is1, 1, 2)))
    use_second = jnp.where(is0, False, jnp.where(is1, tile_ids >= 1, own_mask & (tile_ids >= 2)))
    flags = jnp.stack([keep, use_first, use_fixed, use_second], axis=1).astype(jnp.int32).reshape(-1)
    lost = update(flags, row_count, panels, first, second, fixed)
    return finish(flags, block, lost)


def solution(mesh):
    return jax.shard_map(
        local,
        mesh=mesh,
        in_specs=(
            P("col", "row", None, "subcube"),
            P("subcube", "col", "row", None, None),
            P(),
            P(None, "row", None),
            P(("subcube", "row"), "col"),
        ),
        out_specs=P(("subcube", "row"), "col"),
        check_vma=False,
    )
```
